128 devices in a mesh: gx: 4 (over y), gy: 32 (over z, x, core).
Axes of the slice: x: 4, y: 4, z: 4, core: 2. Of those that a mesh axis runs over, the one named last changes fastest.
Arguments:
- fine_state: bfloat16 [32768, 256], P(('gx', 'gy')), may hold values from -6 to 6
- coarse_state: bfloat16 [8192, 256], P('gy'), may hold values from -6 to 6
- up_target: int32 [65536], P(('gx', 'gy')), may hold values from 0 to 255
- down_source: int32 [98304], P(('gx', 'gy')), may hold values from 0 to 255
- halo_lists: int32 [64, 128], P('gy'), may hold values from 0 to 255
- same_source: int32 [49152], P('gy'), may hold values from 0 to 511, as said below
- matrices: bfloat16 [3, 6, 256, 256], replicated, may hold values from -0.375 to 0.375
- biases: float32 [3, 4, 256], replicated, may hold values from -3 to 3
- fine_cotangent: bfloat16 [32768, 256], P(('gx', 'gy')), may hold values from -6 to 6
Outputs:
- fine_out: bfloat16 [32768, 256], P(('gx', 'gy'))
- lifted_cotangent: float32 [8192, 256], P('gy')
- grad_matrices: float32 [3, 6, 256, 256], replicated
- grad_biases: float32 [3, 4, 256], replicated
The draws below stay inside these ranges and needn't reach their ends.
Inputs may be any that keep to these rules, and one draw needn't show every extreme that they name: `up_target`: entry n * 2 + k is the in-sector index, among the 256 coarse nodes of fine node n's sector, of the receiver of fine node n's k-th up edge. `down_source`: entry n * 3 + k is the in-sector index, among the 256 coarse nodes of fine node n's sector, of the sender of fine node n's k-th down edge. `halo_lists`: row 2 j lists in-sector indices of coarse nodes of sector j read by sector j - 1, row 2 j + 1 those read by sector j + 1; sectors wrap around; entries may repeat. `same_source`: entry c * 6 + k is a row of the extended block of coarse node c's sector: below 128 a row passed by the previous sector, from 128 to 383 the sector's own node of that index minus 128, above that a row passed by the next sector.
All inputs are finite; a program needn't handle non-finite values.
Results may differ from the reference program's by a relative error of at most 0.025.
Values may be sent and summed in bfloat16 or wider, within the bound.
A program may use at most 128 MiB of HBM per device.

```python
import math
import jax
import jax.numpy as jnp
from jax import lax

D = 256
ND0 = 256
ND1 = 256
CAP = 128
KU = 2
KD = 3
K1 = 6
SECTORS = 32
FINE = 32768
COARSE = 8192
N_GX = 4
N_GY = 32


def draw_same_source(key, part):
    count = COARSE * K1
    pick_key = jax.random.fold_in(key, 11)
    rim_key = jax.random.fold_in(key, 12)
    own_key = jax.random.fold_in(key, 13)
    selector = jax.random.randint(pick_key, (count,), 0, 4)
    rim_index = jax.random.randint(rim_key, (count,), 0, 2 * CAP)
    own_index = jax.random.randint(own_key, (count,), 0, ND1)
    rim_row = jnp.where(rim_index < CAP, rim_index, rim_index + ND1)
    return jnp.where(selector < 3, rim_row, own_index + CAP).astype(jnp.int32)


def plant(values, key, low, top_value):
    place = [jax.random.randint(jax.random.fold_in(key, axis), (), 0, length) for axis, length in enumerate(values.shape)]
    widest = values.shape.index(max(values.shape))
    beside = place[:widest] + [(place[widest] + 1) % values.shape[widest]] + place[widest + 1:]
    return values.at[tuple(place)].set(low).at[tuple(beside)].set(top_value)


def block_levels(key, shape, split, low, high):
    factor_of, own = 1.0, jax.random.fold_in(key, 6)
    for axis_at, shards_of in split:
        steps = jnp.exp(jax.random.uniform(jax.random.fold_in(own, axis_at), (shards_of,), jnp.float32, low / len(split), high / len(split)))
        factor_of = factor_of * jnp.repeat(steps, shape[axis_at] // shards_of).reshape([-1 if axis == axis_at else 1 for axis in range(len(shape))])
    return factor_of


def gaussian(key, shape, deviation, limit, pieces=(), held_as=jnp.bfloat16):
    values = jax.random.normal(key, shape, jnp.float32) * deviation
    if len(pieces) > 0:
        values = block_levels(key, shape, pieces, -0.22, 0.18) * values
    return jnp.clip(values, min=-limit, max=limit).astype(held_as)


def setup_inputs(seed: int = 0) -> dict:
    keys = jax.random.split(jax.random.key(seed), 10)
    return {
        "fine_state": gaussian(keys[0], (FINE, D), 1.0, 6.0, ((0, 128),)),
        "coarse_state": gaussian(keys[1], (COARSE, D), 1.0, 6.0, ((0, 32),)),
        "up_target": plant(jax.random.randint(keys[2], (FINE * KU,), 0, ND1), jax.random.fold_in(keys[2], 1), 0, ND1 - 1).astype(jnp.int32),
        "down_source": plant(jax.random.randint(keys[3], (FINE * KD,), 0, ND1), jax.random.fold_in(keys[3], 1), 0, ND1 - 1).astype(jnp.int32),
        "halo_lists": plant(jax.random.randint(keys[4], (2 * SECTORS, CAP), 0, ND1), jax.random.fold_in(keys[4], 1), 0, ND1 - 1).astype(jnp.int32),
        "same_source": draw_same_source(jax.random.fold_in(keys[9], 71), 0),
        "matrices": gaussian(keys[6], (3, 6, D, D), D ** -0.5, 0.375),
        "biases": gaussian(keys[7], (3, 4, D), 0.5, 3.0, (), jnp.float32),
        "fine_cotangent": gaussian(keys[8], (FINE, D), 1.0, 6.0, ((0, 128),)),
    }


def layer_norm(values):
    centre = lax.optimization_barrier(jnp.mean(values, axis=-1, keepdims=True))
    centred = values - centre
    spread = lax.optimization_barrier(jnp.mean(centred * centred, axis=-1, keepdims=True))
    return centred * lax.rsqrt(spread + 1e-05)

def dot_plain(left_side, right_side):
    return jnp.dot(left_side, right_side, preferred_element_type=jnp.float32)

def dot_rows(left_side, right_side):
    return lax.dot_general(left_side, right_side, (((0,), (0,)), ((), ())), preferred_element_type=jnp.float32)

def dot_cols(left_side, right_side):
    return lax.dot_general(left_side, right_side, (((1,), (1,)), ((), ())), preferred_element_type=jnp.float32)

def silu_back(at_point, cotangent):
    return jax.vjp(jax.nn.silu, at_point)[1](cotangent)[0]

def norm_back(at_point, cotangent):
    return jax.vjp(layer_norm, at_point)[1](cotangent)[0]

def edge_forward(summed, w_second, b_first, b_second):
    shifted = summed + b_first
    active = jax.nn.silu(shifted).astype(jnp.bfloat16)
    inner_sum = dot_plain(active, w_second) + b_second
    return (layer_norm(inner_sum), (shifted, active, inner_sum))

def edge_backward(grad_message, stored, w_second):
    shifted, active, inner_sum = stored
    grad_inner = norm_back(inner_sum, grad_message)
    inner_half = grad_inner.astype(jnp.bfloat16)
    grad_weight = dot_rows(active, inner_half)
    grad_shift = silu_back(shifted, dot_cols(inner_half, w_second))
    return (grad_shift, grad_weight, lax.optimization_barrier(jnp.sum(grad_shift, axis=0)), lax.optimization_barrier(jnp.sum(grad_inner, axis=0)))

def node_forward(state, gathered, w_self, w_agg, w_out, b_third, b_fourth):
    agg_half = gathered.astype(jnp.bfloat16)
    inner_sum = dot_plain(state, w_self) + dot_plain(agg_half, w_agg) + b_third
    active = jax.nn.silu(inner_sum).astype(jnp.bfloat16)
    outer_sum = dot_plain(active, w_out) + b_fourth
    result = (state.astype(jnp.float32) + layer_norm(outer_sum)).astype(jnp.bfloat16)
    return (result, (agg_half, inner_sum, active, outer_sum))

def node_backward(grad_result, state, stored, w_self, w_agg, w_out, want_state):
    agg_half, inner_sum, active, outer_sum = stored
    grad_outer = norm_back(outer_sum, grad_result)
    outer_half = grad_outer.astype(jnp.bfloat16)
    grad_wout = dot_rows(active, outer_half)
    grad_inner = silu_back(inner_sum, dot_cols(outer_half, w_out))
    inner_half = grad_inner.astype(jnp.bfloat16)
    grad_wself = dot_rows(state, inner_half)
    grad_wagg = dot_rows(agg_half, inner_half)
    grad_agg = dot_cols(inner_half, w_agg)
    grad_state = None
    if want_state:
        grad_state = grad_result + dot_cols(inner_half, w_self)
    return (grad_state, grad_agg, (grad_wself, grad_wagg, grad_wout), (lax.optimization_barrier(jnp.sum(grad_inner, axis=0)), lax.optimization_barrier(jnp.sum(grad_outer, axis=0))))

def same_edges(extended, own_rows, sources, w_send, w_recv, w_second, b_first, b_second):
    feature_width = own_rows.shape[1]
    node_count = own_rows.shape[0]
    sent_rows = dot_plain(extended, w_send)
    taken_rows = dot_plain(own_rows, w_recv)
    summed = (sent_rows[sources].reshape(node_count, -1, feature_width) + taken_rows[:, None, :]).reshape(-1, feature_width)
    message, stored = edge_forward(summed, w_second, b_first, b_second)
    return (message.reshape(node_count, -1, feature_width).sum(1), stored)

def pick_rows(row_table, row_picks):
    return row_table[row_picks]

def add_rows(row_table, row_picks, row_values):
    return row_table.at[row_picks].add(row_values)

def sum_leading(stacked):
    return lax.optimization_barrier(jnp.sum(stacked, axis=0))

def reference(fine_state, coarse_state, up_target, down_source, halo_lists, same_source, matrices, biases, fine_cotangent):
    device_count = N_GX * N_GY
    feature_width = fine_state.shape[1]
    fine_blocks = fine_state.reshape(device_count, ND0, feature_width)
    cot_blocks = fine_cotangent.reshape(device_count, ND0, feature_width)
    up_blocks = up_target.reshape(device_count, ND0 * KU)
    down_blocks = down_source.reshape(device_count, ND0 * KD)
    device_ids = jnp.arange(device_count)
    sector_of = device_ids % N_GY
    sector_ids = jnp.arange(SECTORS)
    coarse_sectors = coarse_state.reshape(SECTORS, ND1, feature_width)
    layer_zero, bias_zero = (matrices[0], biases[0])
    layer_one, bias_one = (matrices[1], biases[1])
    layer_two, bias_two = (matrices[2], biases[2])

    def up_forward(device_index):
        fine_block = fine_blocks[device_index]
        targets = up_blocks[device_index]
        target_rows = coarse_sectors[sector_of[device_index]]
        sent_rows = dot_plain(fine_block, layer_zero[0])
        taken_rows = dot_plain(target_rows, layer_zero[1])
        summed = (sent_rows[:, None, :] + taken_rows[targets].reshape(ND0, KU, feature_width)).reshape(-1, feature_width)
        return edge_forward(summed, layer_zero[2], bias_zero[0], bias_zero[1])

    def up_partial(device_index):
        message = up_forward(device_index)[0]
        return jax.ops.segment_sum(message, up_blocks[device_index], num_segments=ND1)
    up_total = lax.map(up_partial, device_ids).reshape(N_GX, SECTORS, ND1, feature_width).sum(0).reshape(COARSE, feature_width)
    coarse_lifted, node_zero = node_forward(coarse_state, up_total, layer_zero[3], layer_zero[4], layer_zero[5], bias_zero[2], bias_zero[3])
    lifted_sectors = coarse_lifted.reshape(SECTORS, ND1, feature_width)
    list_sectors = halo_lists.reshape(SECTORS, 2, CAP)
    payload = jax.vmap(pick_rows)(lifted_sectors, list_sectors)
    from_left = jnp.roll(payload[:, 1], 1, axis=0)
    from_right = jnp.roll(payload[:, 0], -1, axis=0)
    extended = jnp.concatenate([from_left, lifted_sectors, from_right], axis=1)
    source_sectors = same_source.reshape(SECTORS, ND1 * K1)

    def same_forward(sector_index):
        return same_edges(extended[sector_index], lifted_sectors[sector_index], source_sectors[sector_index], layer_one[0], layer_one[1], layer_one[2], bias_one[0], bias_one[1])

    def same_total(sector_index):
        return same_forward(sector_index)[0]
    gathered_one = lax.map(same_total, sector_ids).reshape(COARSE, feature_width)
    coarse_mixed, node_one = node_forward(coarse_lifted, gathered_one, layer_one[3], layer_one[4], layer_one[5], bias_one[2], bias_one[3])
    mixed_sectors = coarse_mixed.reshape(SECTORS, ND1, feature_width)
    loss_scale = 1.0 / math.sqrt(FINE)

    def down_part(device_index):
        fine_block = fine_blocks[device_index]
        sources = down_blocks[device_index]
        sent_rows = dot_plain(mixed_sectors[sector_of[device_index]], layer_two[0])
        taken_rows = dot_plain(fine_block, layer_two[1])
        summed = (sent_rows[sources].reshape(ND0, KD, feature_width) + taken_rows[:, None, :]).reshape(-1, feature_width)
        message, stored = edge_forward(summed, layer_two[2], bias_two[0], bias_two[1])
        gathered = message.reshape(ND0, KD, feature_width).sum(1)
        result, node_stored = node_forward(fine_block, gathered, layer_two[3], layer_two[4], layer_two[5], bias_two[2], bias_two[3])
        grad_result = cot_blocks[device_index].astype(jnp.float32) * loss_scale
        unused, grad_agg, node_weights, node_biases = node_backward(grad_result, fine_block, node_stored, layer_two[3], layer_two[4], layer_two[5], False)
        grad_message = jnp.broadcast_to(grad_agg[:, None, :], (ND0, KD, feature_width)).reshape(-1, feature_width)
        edge_grad, grad_second, grad_bfirst, grad_bsecond = edge_backward(grad_message, stored, layer_two[2])
        grad_taken = edge_grad.reshape(ND0, KD, feature_width).sum(1)
        grad_recv = dot_rows(fine_block, grad_taken.astype(jnp.bfloat16))
        grad_sent = jax.ops.segment_sum(edge_grad, sources, num_segments=ND1)
        return (result, grad_sent, (grad_recv, grad_second) + node_weights, (grad_bfirst, grad_bsecond) + node_biases)
    down_out = lax.map(down_part, device_ids)
    fine_out = down_out[0].reshape(FINE, feature_width)
    sent_total = down_out[1].reshape(N_GX, SECTORS, ND1, feature_width).sum(0).reshape(COARSE, feature_width)
    two_weights = jax.tree.map(sum_leading, down_out[2])
    two_biases = jax.tree.map(sum_leading, down_out[3])
    sent_half = sent_total.astype(jnp.bfloat16)
    grad_send_two = dot_rows(coarse_mixed, sent_half)
    grad_mixed = dot_cols(sent_half, layer_two[0])
    grad_lifted, grad_one_agg, node_one_w, node_one_b = node_backward(grad_mixed, coarse_lifted, node_one, layer_one[3], layer_one[4], layer_one[5], True)
    agg_sectors = grad_one_agg.reshape(SECTORS, ND1, feature_width)

    def same_back(sector_index):
        stored = same_forward(sector_index)[1]
        grad_message = jnp.broadcast_to(agg_sectors[sector_index][:, None, :], (ND1, K1, feature_width)).reshape(-1, feature_width)
        edge_grad, grad_second, grad_bfirst, grad_bsecond = edge_backward(grad_message, stored, layer_one[2])
        grad_taken = edge_grad.reshape(ND1, K1, feature_width).sum(1)
        grad_extended = jax.ops.segment_sum(edge_grad, source_sectors[sector_index], num_segments=ND1 + 2 * CAP)
        return (grad_taken, grad_extended, grad_second, grad_bfirst, grad_bsecond)
    same_out = lax.map(same_back, sector_ids)
    grad_extended = same_out[1]
    own_part = grad_extended[:, CAP:CAP + ND1]
    left_part = grad_extended[:, :CAP]
    right_part = grad_extended[:, CAP + ND1:]
    grad_sent_one = jax.vmap(add_rows)(own_part, list_sectors[:, 0], jnp.roll(right_part, 1, axis=0))
    grad_sent_one = jax.vmap(add_rows)(grad_sent_one, list_sectors[:, 1], jnp.roll(left_part, -1, axis=0))
    sent_one_half = grad_sent_one.reshape(COARSE, feature_width).astype(jnp.bfloat16)
    taken_one_half = same_out[0].reshape(COARSE, feature_width).astype(jnp.bfloat16)
    grad_recv_one = dot_rows(coarse_lifted, taken_one_half)
    grad_send_one = dot_rows(coarse_lifted, sent_one_half)
    same_second = lax.optimization_barrier(jnp.sum(same_out[2], axis=0))
    same_bfirst = lax.optimization_barrier(jnp.sum(same_out[3], axis=0))
    same_bsecond = lax.optimization_barrier(jnp.sum(same_out[4], axis=0))
    grad_lifted = grad_lifted + dot_cols(taken_one_half, layer_one[1]) + dot_cols(sent_one_half, layer_one[0])
    lifted_cotangent = grad_lifted * math.sqrt(FINE)
    unused, grad_zero_agg, node_zero_w, node_zero_b = node_backward(grad_lifted, coarse_state, node_zero, layer_zero[3], layer_zero[4], layer_zero[5], False)
    zero_sectors = grad_zero_agg.reshape(SECTORS, ND1, feature_width)

    def up_back(device_index):
        fine_block = fine_blocks[device_index]
        targets = up_blocks[device_index]
        target_rows = coarse_sectors[sector_of[device_index]]
        stored = up_forward(device_index)[1]
        grad_message = zero_sectors[sector_of[device_index]][targets]
        edge_grad, grad_second, grad_bfirst, grad_bsecond = edge_backward(grad_message, stored, layer_zero[2])
        grad_send = dot_rows(fine_block, edge_grad.reshape(ND0, KU, feature_width).sum(1).astype(jnp.bfloat16))
        grad_recv = dot_rows(target_rows[targets], edge_grad.astype(jnp.bfloat16))
        return (grad_send, grad_recv, grad_second, grad_bfirst, grad_bsecond)
    up_out = jax.tree.map(sum_leading, lax.map(up_back, device_ids))
    grad_matrices = jnp.stack([jnp.stack([up_out[0], up_out[1], up_out[2], node_zero_w[0], node_zero_w[1], node_zero_w[2]]), jnp.stack([grad_send_one, grad_recv_one, same_second, node_one_w[0], node_one_w[1], node_one_w[2]]), jnp.stack([grad_send_two, two_weights[0], two_weights[1], two_weights[2], two_weights[3], two_weights[4]])])
    grad_biases = jnp.stack([jnp.stack([up_out[3], up_out[4], node_zero_b[0], node_zero_b[1]]), jnp.stack([same_bfirst, same_bsecond, node_one_b[0], node_one_b[1]]), jnp.stack([two_biases[0], two_biases[1], two_biases[2], two_biases[3]])])
    return (fine_out, lifted_cotangent, grad_matrices, grad_biases)
```

```python
import math

import jax
import jax.numpy as jnp
from jax import lax
from jax.experimental import pallas as pl
from jax.experimental.pallas import tpu as pltpu
from jax.sharding import PartitionSpec as P

MESH = pl.DeviceIdType.MESH
F32 = jnp.float32
BF16 = jnp.bfloat16
B = 256
H = 128
UP, DOWN, SAME = (0, 2), (2, 5), (5, 11)
COPIES = 104


def dot_plain(a, b):
    return jnp.dot(a, b, preferred_element_type=F32)


def dot_rows(a, b):
    return lax.dot_general(a, b, (((0,), (0,)), ((), ())), preferred_element_type=F32)


def dot_cols(a, b):
    return lax.dot_general(a, b, (((1,), (1,)), ((), ())), preferred_element_type=F32)


def silu_parts(x):
    gate = 0.5 * jnp.tanh(0.5 * x) + 0.5
    active = x * gate
    return active, gate + active * (1.0 - gate)


def row_mean(x):
    return jnp.mean(x, axis=-1, keepdims=True)


def normed(y):
    centred = y - row_mean(y)
    scale = lax.rsqrt(row_mean(centred * centred) + 1e-05)
    return centred * scale, scale


def norm_back(g, unit, scale):
    return scale * (g - row_mean(g) - unit * row_mean(g * unit))


def col_sum(x):
    return jnp.sum(x, axis=0, keepdims=True)


class Group:
    def __init__(self, post, place, axes, rows, refs, out):
        self.post, self.place, self.axes, self.rows, self.out = post, place, axes, rows, out
        self.g, self.rc, self.s1, self.r1, self.s2, self.r2, self.s3, self.r3, self.s4 = refs
        self.count = rows.stop - rows.start
        self.step = 0
        core = place.core
        self.copies = []
        self.lanes = pl.ds(pl.multiple_of(core * H, H), H)

    def put(self, i, value):
        half = value.astype(BF16)
        self.g[0, i] = half[:, :H]
        self.g[1, i] = half[:, H:]

    def landed(self):
        for copy in self.copies:
            copy.wait_recv()
        self.copies = []

    def advance(self):
        getattr(self, "step%d" % self.step)()
        self.step += 1

    def step0(self):
        other = 1 - self.place.core
        self.copies = [self.post(self.g.at[other], self.rc, self.place.partner())]

    def step1(self):
        self.landed()
        core = self.place.core
        for i in range(self.count):
            self.s1[i] = (self.g[core, i].astype(F32) + self.rc[i].astype(F32)).astype(BF16)
        self.scatter(self.axes[0], 64, self.s1, self.r1)

    def scatter(self, axis, size, src, landing):
        at = self.place.at(axis)
        for d in (1, 2, 3):
            to = lax.rem(at + d, 4)
            rows = pl.ds(pl.multiple_of(to * size, size), size)
            self.copies.append(self.post(src.at[:, rows, :], landing.at[d - 1], self.place.peer(axis, d)))

    def gather_sum(self, axis, size, src, landing, out):
        at = self.place.at(axis)
        rows = pl.ds(pl.multiple_of(at * size, size), size)
        for i in range(self.count):
            total = src[i, rows, :].astype(F32)
            for d in range(3):
                total += landing[d, i].astype(F32)
            out[i] = total.astype(BF16)

    def step2(self):
        self.landed()
        self.gather_sum(self.axes[0], 64, self.s1, self.r1, self.s2)
        self.scatter(self.axes[1], 16, self.s2, self.r2)

    def step3(self):
        self.landed()
        if len(self.axes) == 2:
            self.gather_sum(self.axes[1], 16, self.s2, self.r2, self.s4)
            return
        self.gather_sum(self.axes[1], 16, self.s2, self.r2, self.s3)
        at = self.place.at(self.axes[2])
        for d in (1, 2, 3):
            self.copies.append(self.post(self.s3, self.r3.at[at], self.place.peer(self.axes[2], d)))
        self.r3[at] = self.s3[...]

    def step4(self):
        self.landed()
        if len(self.axes) == 3:
            for i in range(self.count):
                total = self.r3[0, i].astype(F32)
                for j in (1, 2, 3):
                    total += self.r3[j, i].astype(F32)
                self.s4[i] = total.astype(BF16)
        start = self.place.at(self.axes[0]) * 64 + self.place.at(self.axes[1]) * 16
        rows = pl.ds(pl.multiple_of(start, 16), 16)
        spot = self.out.at[self.rows, rows, self.lanes]
        for d in (1, 2, 3):
            self.copies.append(self.post(self.s4, spot, self.place.peer(self.axes[1], d)))
        for i in range(self.count):
            self.out[self.rows.start + i, rows, self.lanes] = self.s4[i]

    def step5(self):
        self.landed()
        rows = pl.ds(pl.multiple_of(self.place.at(self.axes[0]) * 64, 64), 64)
        spot = self.out.at[self.rows, rows, self.lanes]
        for d in (1, 2, 3):
            self.copies.append(self.post(spot, spot, self.place.peer(self.axes[0], d)))

    def step6(self):
        self.landed()
        spot = self.out.at[self.rows, :, self.lanes]
        self.copies = [self.post(spot, spot, self.place.partner())]

    def step7(self):
        self.landed()


class Place:
    def __init__(self):
        self.gx = lax.axis_index("gx")
        self.gy = lax.axis_index("gy")
        self.core = lax.rem(self.gy, 2)
        self.x = lax.rem(self.gy // 2, 4)
        self.z = self.gy // 8

    def at(self, axis):
        return {"x": self.x, "y": self.gx, "z": self.z}[axis]

    def partner(self):
        return (self.gx, self.gy + 1 - 2 * self.core)

    def peer(self, axis, d):
        if axis == "y":
            return (lax.rem(self.gx + d, 4), self.gy)
        if axis == "x":
            return (self.gx, self.z * 8 + lax.rem(self.x + d, 4) * 2 + self.core)
        return (self.gx, lax.rem(self.z + d, 4) * 8 + self.x * 2 + self.core)

    def beside(self, d):
        return (self.gx, lax.rem(self.gy + d + 32, 32))


def deal(source, raw, index, first, end):
    ways = end - first
    raw[:2 * ways, :] = source[...]
    rows = raw[...]
    lane = lax.broadcasted_iota(jnp.int32, rows.shape, 1)
    for k in range(ways):
        place = lane * ways + k
        picked = jnp.take_along_axis(rows, lax.rem(place, H), axis=1, mode="promise_in_bounds")
        line = place[0:1] // H
        for half in (0, 1):
            row = picked[ways * half:ways * half + 1]
            for i in range(1, ways):
                row = jnp.where(line == i, picked[ways * half + i:ways * half + i + 1], row)
            index[first + k:first + k + 1, half * H:half * H + H] = row


def kernel(total_fine, *refs):
    (fine, coarse, cot, up_raw, down_raw, halo_raw, same_raw, mats, bias, fine_out, lifted_cot, grads, gbias) = refs[:13]
    (send_sems, recv_sems, onehot, samehot, act, slope, unit, scale, dys, nact, nslope, nunit, nscale,
     table, ext, gtab, pres, csend, crecv, hsend, hback, node_in, bias_acc, bias_core, bias_slots, raw, index) = refs[13:40]
    group_refs = refs[40:]
    place = Place()
    posted = []

    def post(src, dst, device):
        i = len(posted)
        copy = pltpu.make_async_remote_copy(
            src_ref=src, dst_ref=dst, send_sem=send_sems.at[i], recv_sem=recv_sems.at[i],
            device_id=device, device_id_type=MESH,
        )
        copy.start()
        posted.append(copy)
        return copy

    barrier = pltpu.get_barrier_semaphore()
    near = [place.peer(a, d) for a in ("x", "y", "z") for d in (1, 2, 3)]
    near += [place.partner(), place.beside(1), place.beside(-1)]
    for device in near:
        pl.semaphore_signal(barrier, inc=1, device_id=device, device_id_type=MESH)

    def groups_of(at, axes, rows):
        return Group(post, place, axes, rows, group_refs[9 * at:9 * at + 9], grads)

    edge0 = groups_of(0, ("y", "z", "x"), slice(0, 3))
    node0 = groups_of(1, ("x", "z"), slice(3, 6))
    layer1 = groups_of(2, ("z", "x"), slice(6, 12))
    layer2 = groups_of(3, ("x", "z", "y"), slice(12, 18))

    bias_acc[...] = jnp.zeros_like(bias_acc)
    deal(up_raw, raw, index, *UP)

    def add_bias(row, value):
        bias_acc[row:row + 1, :] += value

    def w(layer, i):
        return mats[layer, i]

    def b(layer, i):
        return bias[layer, i:i + 1, :]

    def hot_rows(block, size):
        nodes = lax.broadcasted_iota(jnp.int32, (size, B), 0)
        return jnp.where(nodes == index[block:block + 1, :], 1.0, 0.0).astype(BF16)

    def edge_forward(block, pre, layer):
        active, slope_now = silu_parts(pre)
        half = active.astype(BF16)
        act[block] = half
        slope[block] = slope_now.astype(BF16)
        message, scale_now = normed(dot_plain(half, w(layer, 2)) + b(layer, 1))
        unit[block] = message.astype(BF16)
        scale[block] = scale_now
        return message

    def edge_backward(block, g, layer):
        dy = norm_back(g, unit[block].astype(F32), scale[block])
        half = dy.astype(BF16)
        dys[block] = half
        dp = slope[block].astype(F32) * dot_cols(half, w(layer, 2))
        return dp, col_sum(dy), col_sum(dp)

    def node_forward(layer, state, agg, pre):
        node_in[layer] = agg
        active, slope_now = silu_parts(pre + dot_plain(agg, w(layer, 4)))
        half = active.astype(BF16)
        nact[layer] = half
        nslope[layer] = slope_now.astype(BF16)
        unit_now, scale_now = normed(dot_plain(half, w(layer, 5)) + b(layer, 3))
        nunit[layer] = unit_now.astype(BF16)
        nscale[layer] = scale_now
        return (state.astype(F32) + unit_now).astype(BF16)

    def node_backward(layer, g, share):
        dz = norm_back(g, nunit[layer].astype(F32), nscale[layer])
        dz16 = dz.astype(BF16)
        dq = nslope[layer].astype(F32) * dot_cols(dz16, w(layer, 5))
        dq16 = dq.astype(BF16)
        add_bias(4 * layer + 3, share * col_sum(dz))
        add_bias(4 * layer + 2, share * col_sum(dq))
        return dz16, dq16

    def sum_start(first, value):
        half = value.astype(BF16)
        csend[first, 0] = half[:H]
        csend[first, 1] = half[H:]
        odd = lax.rem(place.gx, 2)
        one = (place.gx + 1 - 2 * odd, place.gy)
        two = (lax.rem(place.gx + 2 * odd + 3, 4), place.gy)
        waits = [
            post(csend.at[first, 0], crecv.at[first, 0], one),
            post(csend.at[first, 1], crecv.at[first, 1], two),
        ]
        return waits, one, two

    def sum_middle(first, state):
        waits, one, two = state
        for i in (0, 1):
            waits[i].wait_recv()
            both = csend[first, i].astype(F32) + crecv[first, i].astype(F32)
            csend[first + 1, i] = both.astype(BF16)
        return [
            post(csend.at[first + 1, 0], crecv.at[first + 1, 0], two),
            post(csend.at[first + 1, 1], crecv.at[first + 1, 1], one),
        ]

    def sum_end(first, waits):
        parts = []
        for i in (0, 1):
            waits[i].wait_recv()
            both = csend[first + 1, i].astype(F32) + crecv[first + 1, i].astype(F32)
            parts.append(both.astype(BF16))
        return jnp.concatenate(parts, axis=0)

    for block in range(*UP):
        onehot[block] = hot_rows(block, B)
    sent = dot_plain(fine[...], w(0, 0)) + b(0, 0)
    table[...] = dot_plain(coarse[...], w(0, 1)).astype(BF16)
    up_sum = None
    for block in range(*UP):
        message = edge_forward(block, sent + dot_rows(onehot[block], table[...]), 0)
        part = dot_plain(onehot[block], message.astype(BF16))
        up_sum = part if up_sum is None else up_sum + part

    pl.semaphore_wait(barrier, len(near))
    state = sum_start(0, up_sum)
    pres[0] = dot_plain(coarse[...], w(0, 3)) + b(0, 2)
    deal(down_raw, raw, index, *DOWN)
    deal(same_raw, raw, index, *SAME)
    index[11:12, :H] = halo_raw[0:1, :]
    index[11:12, H:] = halo_raw[1:2, :]
    for block in range(*DOWN):
        onehot[block] = hot_rows(block, B)
    onehot[5] = hot_rows(11, B)
    state = sum_middle(0, state)
    for block in range(*SAME):
        samehot[block - 5] = hot_rows(block, 2 * B)
    pres[1] = dot_plain(fine[...], w(2, 3)) + b(2, 2)
    pres[2] = dot_plain(fine[...], w(2, 1)) + b(2, 0)
    agg = sum_end(0, state)
    lifted = node_forward(0, coarse[...], agg, pres[0])
    ext[H:H + B] = lifted
    payload = dot_rows(onehot[5], lifted).astype(BF16)
    hsend[0] = payload[:H]
    hsend[1] = payload[H:]
    halo = [
        post(hsend.at[0], ext.at[H + B:], place.beside(-1)),
        post(hsend.at[1], ext.at[:H], place.beside(1)),
    ]

    pres[3] = dot_plain(lifted, w(1, 1)) + b(1, 0)
    pres[4] = dot_plain(lifted, w(1, 3)) + b(1, 2)
    for copy in halo:
        copy.wait_recv()
    gtab[...] = dot_plain(ext[...], w(1, 0)).astype(BF16)
    same_sum = None
    for block in range(*SAME):
        message = edge_forward(block, pres[3] + dot_rows(samehot[block - 5], gtab[...]), 1)
        same_sum = message if same_sum is None else same_sum + message
    mixed = node_forward(1, ext[H:H + B], same_sum.astype(BF16), pres[4])
    nact[3] = mixed

    table[...] = dot_plain(mixed, w(2, 0)).astype(BF16)
    down_sum = None
    for block in range(*DOWN):
        message = edge_forward(block, pres[2] + dot_rows(onehot[block], table[...]), 2)
        down_sum = message if down_sum is None else down_sum + message
    fine_out[...] = node_forward(2, fine[...], down_sum.astype(BF16), pres[1])
    dz2, dq2 = node_backward(2, cot[...].astype(F32) * (1.0 / math.sqrt(total_fine)), 1.0)
    g = dot_cols(dq2, w(2, 4))
    taken = back = None
    for block in range(*DOWN):
        dp, db2, db1 = edge_backward(block, g, 2)
        add_bias(8, db1)
        add_bias(9, db2)
        part = dot_plain(onehot[block], dp.astype(BF16))
        taken = dp if taken is None else taken + dp
        back = part if back is None else back + part
    state = sum_start(2, back)
    layer2.put(1, dot_rows(fine[...], taken.astype(BF16)))
    layer2.put(2, dot_rows(act[2:5].reshape(3 * B, B), dys[2:5].reshape(3 * B, B)))
    state = sum_middle(2, state)
    layer2.put(3, dot_rows(fine[...], dq2))
    layer2.put(4, dot_rows(node_in[2], dq2))
    layer2.put(5, dot_rows(nact[2], dz2))
    sent_half = sum_end(2, state)
    grad_mixed = dot_cols(sent_half, w(2, 0))
    layer2.put(0, 0.25 * dot_rows(nact[3], sent_half))
    layer2.advance()

    dz1, dq1 = node_backward(1, grad_mixed, 0.25)
    pres[0] = grad_mixed + dot_cols(dq1, w(1, 3))
    g = dot_cols(dq1, w(1, 4))
    taken = back = None
    for block in range(*SAME):
        dp, db2, db1 = edge_backward(block, g, 1)
        add_bias(4, 0.25 * db1)
        add_bias(5, 0.25 * db2)
        part = dot_plain(samehot[block - 5], dp.astype(BF16))
        taken = dp if taken is None else taken + dp
        back = part if back is None else back + part
    hsend[2] = back[:H].astype(BF16)
    hsend[3] = back[H + B:].astype(BF16)
    returns = [
        post(hsend.at[2], hback.at[1], place.beside(-1)),
        post(hsend.at[3], hback.at[0], place.beside(1)),
    ]
    own = back[H:H + B]
    layer2.advance()
    lifted = ext[H:H + B]
    taken_half = taken.astype(BF16)
    layer1.put(1, 1.0 * dot_rows(lifted, taken_half))
    layer1.put(2, dot_rows(act[5:11].reshape(6 * B, B), dys[5:11].reshape(6 * B, B)))
    layer1.put(3, dot_rows(lifted, dq1))
    layer1.put(4, dot_rows(node_in[1], dq1))
    layer1.put(5, dot_rows(nact[1], dz1))
    grad_lifted = pres[0] + dot_cols(taken_half, w(1, 1))
    for copy in returns:
        copy.wait_recv()
    own += dot_plain(onehot[5], hback[...].reshape(B, B))
    own_half = own.astype(BF16)
    grad_lifted += dot_cols(own_half, w(1, 0))
    lifted_cot[...] = grad_lifted * math.sqrt(total_fine)
    layer1.put(0, dot_rows(lifted, own_half))
    layer1.advance()
    layer2.advance()

    dz0, dq0 = node_backward(0, grad_lifted, 0.25)
    table[...] = dot_cols(dq0, w(0, 4)).astype(BF16)
    taken = back = None
    for block in range(*UP):
        dp, db2, db1 = edge_backward(block, dot_rows(onehot[block], table[...]), 0)
        add_bias(0, db1)
        add_bias(1, db2)
        part = dot_plain(onehot[block], dp.astype(BF16))
        taken = dp if taken is None else taken + dp
        back = part if back is None else back + part
    edge0.put(0, dot_rows(fine[...], taken.astype(BF16)))
    edge0.put(1, dot_rows(coarse[...], back.astype(BF16)))
    edge0.put(2, dot_rows(act[0:2].reshape(2 * B, B), dys[0:2].reshape(2 * B, B)))
    edge0.advance()
    bias_waits = [post(bias_acc, bias_core, place.partner())]
    node0.put(0, dot_rows(coarse[...], dq0))
    node0.put(1, dot_rows(node_in[0], dq0))
    node0.put(2, dot_rows(nact[0], dz0))
    node0.advance()

    def bias_step(step):
        for copy in bias_waits:
            copy.wait_recv()
        bias_waits.clear()
        if step == 0:
            total = bias_acc[...] + bias_core[...]
        else:
            total = bias_slots[step - 1, 0] + bias_slots[step - 1, 1]
            total = total + bias_slots[step - 1, 2] + bias_slots[step - 1, 3]
        if step == 3:
            gbias[...] = total
            return
        axis = "yxz"[step]
        at = place.at(axis)
        bias_slots[step, at] = total
        for d in (1, 2, 3):
            spot = bias_slots.at[step, at]
            bias_waits.append(post(spot, spot, place.peer(axis, d)))

    layer2.advance()
    layer1.advance()
    for step in range(7):
        edge0.advance()
        node0.advance()
        if layer2.step < 8:
            layer2.advance()
        if layer1.step < 8:
            layer1.advance()
        if step < 4:
            bias_step(step)
    assert all(group.step == 8 for group in (edge0, node0, layer1, layer2))
    for copy in posted:
        copy.wait_send()


def finish(fine_in, lifted_in, grads, gbias, fine_out, lifted_out, matrices_out, biases_out, wide, sems):
    copies = [
        pltpu.make_async_copy(fine_in, fine_out, sems.at[18]),
        pltpu.make_async_copy(lifted_in, lifted_out, sems.at[19]),
    ]
    for copy in copies:
        copy.start()
    for i in range(18):
        wide[i] = grads[i].astype(F32)
        copies.append(pltpu.make_async_copy(wide.at[i], matrices_out.at[i // 6, i % 6], sems.at[i]))
        copies[-1].start()
    for layer in range(3):
        biases_out[layer] = gbias[4 * layer:4 * layer + 4, :]
    for copy in copies:
        copy.wait()


def group_scratch(count):
    return [
        pltpu.VMEM((2, count, B, H), BF16),
        pltpu.VMEM((count, B, H), BF16),
        pltpu.VMEM((count, B, H), BF16),
        pltpu.VMEM((3, count, 64, H), BF16),
        pltpu.VMEM((count, 64, H), BF16),
        pltpu.VMEM((3, count, 16, H), BF16),
        pltpu.VMEM((count, 16, H), BF16),
        pltpu.VMEM((4, count, 16, H), BF16),
        pltpu.VMEM((count, 16, H), BF16),
    ]


def local(fine_state, coarse_state, up_target, down_source, halo_lists, same_source, matrices, biases, fine_cotangent):
    total_fine = fine_state.shape[0] * lax.axis_size("gx") * lax.axis_size("gy")
    scratch = [
        pltpu.SemaphoreType.DMA((COPIES,)),
        pltpu.SemaphoreType.DMA((COPIES,)),
        pltpu.VMEM((6, B, B), BF16),
        pltpu.VMEM((6, 2 * B, B), BF16),
        pltpu.VMEM((11, B, B), BF16),
        pltpu.VMEM((11, B, B), BF16),
        pltpu.VMEM((11, B, B), BF16),
        pltpu.VMEM((11, B, 1), F32),
        pltpu.VMEM((11, B, B), BF16),
        pltpu.VMEM((4, B, B), BF16),
        pltpu.VMEM((3, B, B), BF16),
        pltpu.VMEM((3, B, B), BF16),
        pltpu.VMEM((3, B, 1), F32),
        pltpu.VMEM((B, B), BF16),
        pltpu.VMEM((2 * B, B), BF16),
        pltpu.VMEM((2 * B, B), BF16),
        pltpu.VMEM((5, B, B), F32),
        pltpu.VMEM((4, 2, H, B), BF16),
        pltpu.VMEM((4, 2, H, B), BF16),
        pltpu.VMEM((4, H, B), BF16),
        pltpu.VMEM((2, H, B), BF16),
        pltpu.VMEM((3, B, B), BF16),
        pltpu.VMEM((16, B), F32),
        pltpu.VMEM((16, B), F32),
        pltpu.VMEM((3, 4, 16, B), F32),
        pltpu.VMEM((16, H), jnp.int32),
        pltpu.VMEM((16, B), jnp.int32),
    ]
    for count in (3, 3, 6, 6):
        scratch += group_scratch(count)
    vmem = pl.BlockSpec(memory_space=pltpu.VMEM)

    def body(*refs):
        kernel(total_fine, *refs)

    fine_out, lifted, grads, gbias = pl.pallas_call(
        body,
        out_shape=(
            jax.ShapeDtypeStruct((B, B), BF16),
            jax.ShapeDtypeStruct((B, B), F32),
            jax.ShapeDtypeStruct((18, B, B), BF16),
            jax.ShapeDtypeStruct((16, B), F32),
        ),
        in_specs=[vmem] * 9,
        out_specs=(vmem,) * 4,
        scratch_shapes=scratch,
        compiler_params=pltpu.CompilerParams(
            collective_id=0, has_side_effects=True, vmem_limit_bytes=32 << 20
        ),
        name="sweep",
    )(
        fine_state, coarse_state, fine_cotangent, up_target.reshape(4, H), down_source.reshape(6, H), halo_lists,
        same_source.reshape(12, H), matrices, biases,
    )
    hbm = pl.BlockSpec(memory_space=pl.ANY)
    return pl.pallas_call(
        finish,
        out_shape=(
            jax.ShapeDtypeStruct((B, B), BF16),
            jax.ShapeDtypeStruct((B, B), F32),
            jax.ShapeDtypeStruct((3, 6, B, B), F32),
            jax.ShapeDtypeStruct((3, 4, B), F32),
        ),
        in_specs=[vmem] * 4,
        out_specs=(hbm, hbm, hbm, vmem),
        scratch_shapes=[pltpu.VMEM((18, B, B), F32), pltpu.SemaphoreType.DMA((20,))],
        compiler_params=pltpu.CompilerParams(vmem_limit_bytes=16 << 20),
        name="finish",
    )(fine_out, lifted, grads, gbias)


def solution(mesh):
    in_specs = (
        P(("gx", "gy"), None),
        P("gy", None),
        P(("gx", "gy")),
        P(("gx", "gy")),
        P("gy", None),
        P("gy"),
        P(),
        P(),
        P(("gx", "gy"), None),
    )
    out_specs = (P(("gx", "gy"), None), P("gy", None), P(), P())
    return jax.shard_map(local, mesh=mesh, in_specs=in_specs, out_specs=out_specs, check_vma=False)
```

```python
import math

import jax
import jax.numpy as jnp
from jax import lax
from jax.experimental import pallas as pl
from jax.experimental.pallas import tpu as pltpu
from jax.sharding import PartitionSpec as P

MESH = pl.DeviceIdType.MESH
F32 = jnp.float32
BF16 = jnp.bfloat16
B = 256
H = 128
UP, DOWN, SAME = (0, 2), (2, 5), (5, 11)
COPIES = 104


def dot_plain(a, b):
    return jnp.dot(a, b, preferred_element_type=F32)


def dot_rows(a, b):
    return lax.dot_general(a, b, (((0,), (0,)), ((), ())), preferred_element_type=F32)


def dot_cols(a, b):
    return lax.dot_general(a, b, (((1,), (1,)), ((), ())), preferred_element_type=F32)


def silu_parts(x):
    gate = 0.5 * jnp.tanh(0.5 * x) + 0.5
    active = x * gate
    return active, gate + active * (1.0 - gate)


def row_mean(x):
    return jnp.mean(x, axis=-1, keepdims=True)


def normed(y):
    centred = y - row_mean(y)
    scale = lax.rsqrt(row_mean(centred * centred) + 1e-05)
    return centred * scale, scale


def norm_back(g, unit, scale):
    return scale * (g - row_mean(g) - unit * row_mean(g * unit))


def col_sum(x):
    return jnp.sum(x, axis=0, keepdims=True)


class Group:
    def __init__(self, post, place, axes, rows, refs, out):
        self.post, self.place, self.axes, self.rows, self.out = post, place, axes, rows, out
        self.g, self.rc, self.s1, self.r1, self.s2, self.r2, self.s3, self.r3, self.s4 = refs
        self.count = rows.stop - rows.start
        self.step = 0
        core = place.core
        self.copies = []
        self.lanes = pl.ds(pl.multiple_of(core * H, H), H)

    def put(self, i, value):
        half = value.astype(BF16)
        self.g[0, i] = half[:, :H]
        self.g[1, i] = half[:, H:]

    def landed(self):
        for copy in self.copies:
            copy.wait_recv()
        self.copies = []

    def advance(self):
        getattr(self, "step%d" % self.step)()
        self.step += 1

    def step0(self):
        other = 1 - self.place.core
        self.copies = [self.post(self.g.at[other], self.rc, self.place.partner())]

    def step1(self):
        self.landed()
        core = self.place.core
        for i in range(self.count):
            self.s1[i] = (self.g[core, i].astype(F32) + self.rc[i].astype(F32)).astype(BF16)
        self.scatter(self.axes[0], 64, self.s1, self.r1)

    def scatter(self, axis, size, src, landing):
        at = self.place.at(axis)
        for d in (1, 2, 3):
            to = lax.rem(at + d, 4)
            rows = pl.ds(pl.multiple_of(to * size, size), size)
            self.copies.append(self.post(src.at[:, rows, :], landing.at[d - 1], self.place.peer(axis, d)))

    def gather_sum(self, axis, size, src, landing, out):
        at = self.place.at(axis)
        rows = pl.ds(pl.multiple_of(at * size, size), size)
        for i in range(self.count):
            total = src[i, rows, :].astype(F32)
            for d in range(3):
                total += landing[d, i].astype(F32)
            out[i] = total.astype(BF16)

    def step2(self):
        self.landed()
        self.gather_sum(self.axes[0], 64, self.s1, self.r1, self.s2)
        self.scatter(self.axes[1], 16, self.s2, self.r2)

    def step3(self):
        self.landed()
        if len(self.axes) == 2:
            self.gather_sum(self.axes[1], 16, self.s2, self.r2, self.s4)
            return
        self.gather_sum(self.axes[1], 16, self.s2, self.r2, self.s3)
        at = self.place.at(self.axes[2])
        for d in (1, 2, 3):
            self.copies.append(self.post(self.s3, self.r3.at[at], self.place.peer(self.axes[2], d)))
        self.r3[at] = self.s3[...]

    def step4(self):
        self.landed()
        if len(self.axes) == 3:
            for i in range(self.count):
                total = self.r3[0, i].astype(F32)
                for j in (1, 2, 3):
                    total += self.r3[j, i].astype(F32)
                self.s4[i] = total.astype(BF16)
        start = self.place.at(self.axes[0]) * 64 + self.place.at(self.axes[1]) * 16
        rows = pl.ds(pl.multiple_of(start, 16), 16)
        spot = self.out.at[self.rows, rows, self.lanes]
        for d in (1, 2, 3):
            self.copies.append(self.post(self.s4, spot, self.place.peer(self.axes[1], d)))
        for i in range(self.count):
            self.out[self.rows.start + i, rows, self.lanes] = self.s4[i]

    def step5(self):
        self.landed()
        rows = pl.ds(pl.multiple_of(self.place.at(self.axes[0]) * 64, 64), 64)
        spot = self.out.at[self.rows, rows, self.lanes]
        for d in (1, 2, 3):
            self.copies.append(self.post(spot, spot, self.place.peer(self.axes[0], d)))

    def step6(self):
        self.landed()
        spot = self.out.at[self.rows, :, self.lanes]
        self.copies = [self.post(spot, spot, self.place.partner())]

    def step7(self):
        self.landed()


class Place:
    def __init__(self):
        self.gx = lax.axis_index("gx")
        self.gy = lax.axis_index("gy")
        self.core = lax.rem(self.gy, 2)
        self.x = lax.rem(self.gy // 2, 4)
        self.z = self.gy // 8

    def at(self, axis):
        return {"x": self.x, "y": self.gx, "z": self.z}[axis]

    def partner(self):
        return (self.gx, self.gy + 1 - 2 * self.core)

    def peer(self, axis, d):
        if axis == "y":
            return (lax.rem(self.gx + d, 4), self.gy)
        if axis == "x":
            return (self.gx, self.z * 8 + lax.rem(self.x + d, 4) * 2 + self.core)
        return (self.gx, lax.rem(self.z + d, 4) * 8 + self.x * 2 + self.core)

    def beside(self, d):
        return (self.gx, lax.rem(self.gy + d + 32, 32))


def deal(source, raw, index, first, end):
    ways = end - first
    raw[:2 * ways, :] = source[...]
    rows = raw[...]
    lane = lax.broadcasted_iota(jnp.int32, rows.shape, 1)
    for k in range(ways):
        place = lane * ways + k
        picked = jnp.take_along_axis(rows, lax.rem(place, H), axis=1, mode="promise_in_bounds")
        line = place[0:1] // H
        for half in (0, 1):
            row = picked[ways * half:ways * half + 1]
            for i in range(1, ways):
                row = jnp.where(line == i, picked[ways * half + i:ways * half + i + 1], row)
            index[first + k:first + k + 1, half * H:half * H + H] = row


def kernel(total_fine, *refs):
    inputs, (fine_out, lifted_cot, grads, gbias) = refs[:9], refs[9:13]
    (send_sems, recv_sems, onehot, samehot, act, slope, unit, scale, dys, nact, nslope, nunit, nscale,
     table, ext, gtab, pres, csend, crecv, hsend, hback, node_in, bias_acc, bias_core, bias_slots, raw, index, load_sems,
     fine, coarse, cot, up_raw, down_raw, halo_raw, same_raw, mats, bias) = refs[13:50]
    group_refs = refs[50:]
    place = Place()
    posted = []

    def post(src, dst, device):
        i = len(posted)
        copy = pltpu.make_async_remote_copy(
            src_ref=src, dst_ref=dst, send_sem=send_sems.at[i], recv_sem=recv_sems.at[i],
            device_id=device, device_id_type=MESH,
        )
        copy.start()
        posted.append(copy)
        return copy

    barrier = pltpu.get_barrier_semaphore()
    near = [place.peer(a, d) for a in ("x", "y", "z") for d in (1, 2, 3)]
    near += [place.partner(), place.beside(1), place.beside(-1)]
    for device in near:
        pl.semaphore_signal(barrier, inc=1, device_id=device, device_id_type=MESH)

    loads = []
    for i, (src, dst) in enumerate([
        (inputs[3], up_raw), (inputs[0], fine), (inputs[1], coarse), (inputs[8], bias),
        (inputs[7].at[0, 0:3], mats.at[0, 0:3]), (inputs[4], down_raw), (inputs[6], same_raw), (inputs[5], halo_raw),
        (inputs[7].at[0, 3:6], mats.at[0, 3:6]), (inputs[7].at[2], mats.at[2]), (inputs[7].at[1], mats.at[1]),
        (inputs[2], cot),
    ]):
        loads.append(pltpu.make_async_copy(src, dst, load_sems.at[i]))
        loads[-1].start()

    def groups_of(at, axes, rows):
        return Group(post, place, axes, rows, group_refs[9 * at:9 * at + 9], grads)

    edge0 = groups_of(0, ("y", "z", "x"), slice(0, 3))
    node0 = groups_of(1, ("x", "z"), slice(3, 6))
    layer1 = groups_of(2, ("z", "x"), slice(6, 12))
    layer2 = groups_of(3, ("x", "z", "y"), slice(12, 18))

    bias_acc[...] = jnp.zeros_like(bias_acc)
    for load in loads[:5]:
        load.wait()
    deal(up_raw, raw, index, *UP)

    def add_bias(row, value):
        bias_acc[row:row + 1, :] += value

    def w(layer, i):
        return mats[layer, i]

    def b(layer, i):
        return bias[layer, i:i + 1, :]

    def hot_rows(block, size):
        nodes = lax.broadcasted_iota(jnp.int32, (size, B), 0)
        return jnp.where(nodes == index[block:block + 1, :], 1.0, 0.0).astype(BF16)

    def edge_forward(block, pre, layer):
        active, slope_now = silu_parts(pre)
        half = active.astype(BF16)
        act[block] = half
        slope[block] = slope_now.astype(BF16)
        message, scale_now = normed(dot_plain(half, w(layer, 2)) + b(layer, 1))
        unit[block] = message.astype(BF16)
        scale[block] = scale_now
        return message

    def edge_backward(block, g, layer):
        dy = norm_back(g, unit[block].astype(F32), scale[block])
        half = dy.astype(BF16)
        dys[block] = half
        dp = slope[block].astype(F32) * dot_cols(half, w(layer, 2))
        return dp, col_sum(dy), col_sum(dp)

    def node_forward(layer, state, agg, pre):
        node_in[layer] = agg
        active, slope_now = silu_parts(pre + dot_plain(agg, w(layer, 4)))
        half = active.astype(BF16)
        nact[layer] = half
        nslope[layer] = slope_now.astype(BF16)
        unit_now, scale_now = normed(dot_plain(half, w(layer, 5)) + b(layer, 3))
        nunit[layer] = unit_now.astype(BF16)
        nscale[layer] = scale_now
        return (state.astype(F32) + unit_now).astype(BF16)

    def node_backward(layer, g, share):
        dz = norm_back(g, nunit[layer].astype(F32), nscale[layer])
        dz16 = dz.astype(BF16)
        dq = nslope[layer].astype(F32) * dot_cols(dz16, w(layer, 5))
        dq16 = dq.astype(BF16)
        add_bias(4 * layer + 3, share * col_sum(dz))
        add_bias(4 * layer + 2, share * col_sum(dq))
        return dz16, dq16

    def sum_start(first, value):
        half = value.astype(BF16)
        csend[first, 0] = half[:H]
        csend[first, 1] = half[H:]
        odd = lax.rem(place.gx, 2)
        one = (place.gx + 1 - 2 * odd, place.gy)
        two = (lax.rem(place.gx + 2 * odd + 3, 4), place.gy)
        waits = [
            post(csend.at[first, 0], crecv.at[first, 0], one),
            post(csend.at[first, 1], crecv.at[first, 1], two),
        ]
        return waits, one, two

    def sum_middle(first, state):
        waits, one, two = state
        for i in (0, 1):
            waits[i].wait_recv()
            both = csend[first, i].astype(F32) + crecv[first, i].astype(F32)
            csend[first + 1, i] = both.astype(BF16)
        return [
            post(csend.at[first + 1, 0], crecv.at[first + 1, 0], two),
            post(csend.at[first + 1, 1], crecv.at[first + 1, 1], one),
        ]

    def sum_end(first, waits):
        parts = []
        for i in (0, 1):
            waits[i].wait_recv()
            both = csend[first + 1, i].astype(F32) + crecv[first + 1, i].astype(F32)
            parts.append(both.astype(BF16))
        return jnp.concatenate(parts, axis=0)

    for block in range(*UP):
        onehot[block] = hot_rows(block, B)
    sent = dot_plain(fine[...], w(0, 0)) + b(0, 0)
    table[...] = dot_plain(coarse[...], w(0, 1)).astype(BF16)
    up_sum = None
    for block in range(*UP):
        message = edge_forward(block, sent + dot_rows(onehot[block], table[...]), 0)
        part = dot_plain(onehot[block], message.astype(BF16))
        up_sum = part if up_sum is None else up_sum + part

    pl.semaphore_wait(barrier, len(near))
    state = sum_start(0, up_sum)
    for load in loads[5:]:
        load.wait()
    pres[0] = dot_plain(coarse[...], w(0, 3)) + b(0, 2)
    deal(down_raw, raw, index, *DOWN)
    deal(same_raw, raw, index, *SAME)
    index[11:12, :H] = halo_raw[0:1, :]
    index[11:12, H:] = halo_raw[1:2, :]
    for block in range(*DOWN):
        onehot[block] = hot_rows(block, B)
    onehot[5] = hot_rows(11, B)
    state = sum_middle(0, state)
    for block in range(*SAME):
        samehot[block - 5] = hot_rows(block, 2 * B)
    pres[1] = dot_plain(fine[...], w(2, 3)) + b(2, 2)
    pres[2] = dot_plain(fine[...], w(2, 1)) + b(2, 0)
    agg = sum_end(0, state)
    lifted = node_forward(0, coarse[...], agg, pres[0])
    ext[H:H + B] = lifted
    payload = dot_rows(onehot[5], lifted).astype(BF16)
    hsend[0] = payload[:H]
    hsend[1] = payload[H:]
    halo = [
        post(hsend.at[0], ext.at[H + B:], place.beside(-1)),
        post(hsend.at[1], ext.at[:H], place.beside(1)),
    ]

    pres[3] = dot_plain(lifted, w(1, 1)) + b(1, 0)
    pres[4] = dot_plain(lifted, w(1, 3)) + b(1, 2)
    for copy in halo:
        copy.wait_recv()
    gtab[...] = dot_plain(ext[...], w(1, 0)).astype(BF16)
    same_sum = None
    for block in range(*SAME):
        message = edge_forward(block, pres[3] + dot_rows(samehot[block - 5], gtab[...]), 1)
        same_sum = message if same_sum is None else same_sum + message
    mixed = node_forward(1, ext[H:H + B], same_sum.astype(BF16), pres[4])
    nact[3] = mixed

    table[...] = dot_plain(mixed, w(2, 0)).astype(BF16)
    down_sum = None
    for block in range(*DOWN):
        message = edge_forward(block, pres[2] + dot_rows(onehot[block], table[...]), 2)
        down_sum = message if down_sum is None else down_sum + message
    fine_out[...] = node_forward(2, fine[...], down_sum.astype(BF16), pres[1])
    dz2, dq2 = node_backward(2, cot[...].astype(F32) * (1.0 / math.sqrt(total_fine)), 1.0)
    g = dot_cols(dq2, w(2, 4))
    taken = back = None
    for block in range(*DOWN):
        dp, db2, db1 = edge_backward(block, g, 2)
        add_bias(8, db1)
        add_bias(9, db2)
        part = dot_plain(onehot[block], dp.astype(BF16))
        taken = dp if taken is None else taken + dp
        back = part if back is None else back + part
    state = sum_start(2, back)
    layer2.put(1, dot_rows(fine[...], taken.astype(BF16)))
    layer2.put(2, dot_rows(act[2:5].reshape(3 * B, B), dys[2:5].reshape(3 * B, B)))
    state = sum_middle(2, state)
    layer2.put(3, dot_rows(fine[...], dq2))
    layer2.put(4, dot_rows(node_in[2], dq2))
    layer2.put(5, dot_rows(nact[2], dz2))
    sent_half = sum_end(2, state)
    grad_mixed = dot_cols(sent_half, w(2, 0))
    layer2.put(0, 0.25 * dot_rows(nact[3], sent_half))
    layer2.advance()

    dz1, dq1 = node_backward(1, grad_mixed, 0.25)
    pres[0] = grad_mixed + dot_cols(dq1, w(1, 3))
    g = dot_cols(dq1, w(1, 4))
    taken = back = None
    for block in range(*SAME):
        dp, db2, db1 = edge_backward(block, g, 1)
        add_bias(4, 0.25 * db1)
        add_bias(5, 0.25 * db2)
        part = dot_plain(samehot[block - 5], dp.astype(BF16))
        taken = dp if taken is None else taken + dp
        back = part if back is None else back + part
    hsend[2] = back[:H].astype(BF16)
    hsend[3] = back[H + B:].astype(BF16)
    returns = [
        post(hsend.at[2], hback.at[1], place.beside(-1)),
        post(hsend.at[3], hback.at[0], place.beside(1)),
    ]
    own = back[H:H + B]
    layer2.advance()
    lifted = ext[H:H + B]
    taken_half = taken.astype(BF16)
    layer1.put(1, 1.0 * dot_rows(lifted, taken_half))
    layer1.put(2, dot_rows(act[5:11].reshape(6 * B, B), dys[5:11].reshape(6 * B, B)))
    layer1.put(3, dot_rows(lifted, dq1))
    layer1.put(4, dot_rows(node_in[1], dq1))
    layer1.put(5, dot_rows(nact[1], dz1))
    grad_lifted = pres[0] + dot_cols(taken_half, w(1, 1))
    for copy in returns:
        copy.wait_recv()
    own += dot_plain(onehot[5], hback[...].reshape(B, B))
    own_half = own.astype(BF16)
    grad_lifted += dot_cols(own_half, w(1, 0))
    lifted_cot[...] = grad_lifted * math.sqrt(total_fine)
    layer1.put(0, dot_rows(lifted, own_half))
    layer1.advance()
    layer2.advance()

    dz0, dq0 = node_backward(0, grad_lifted, 0.25)
    table[...] = dot_cols(dq0, w(0, 4)).astype(BF16)
    taken = back = None
    for block in range(*UP):
        dp, db2, db1 = edge_backward(block, dot_rows(onehot[block], table[...]), 0)
        add_bias(0, db1)
        add_bias(1, db2)
        part = dot_plain(onehot[block], dp.astype(BF16))
        taken = dp if taken is None else taken + dp
        back = part if back is None else back + part
    edge0.put(0, dot_rows(fine[...], taken.astype(BF16)))
    edge0.put(1, dot_rows(coarse[...], back.astype(BF16)))
    edge0.put(2, dot_rows(act[0:2].reshape(2 * B, B), dys[0:2].reshape(2 * B, B)))
    edge0.advance()
    bias_waits = [post(bias_acc, bias_core, place.partner())]
    node0.put(0, dot_rows(coarse[...], dq0))
    node0.put(1, dot_rows(node_in[0], dq0))
    node0.put(2, dot_rows(nact[0], dz0))
    node0.advance()

    def bias_step(step):
        for copy in bias_waits:
            copy.wait_recv()
        bias_waits.clear()
        if step == 0:
            total = bias_acc[...] + bias_core[...]
        else:
            total = bias_slots[step - 1, 0] + bias_slots[step - 1, 1]
            total = total + bias_slots[step - 1, 2] + bias_slots[step - 1, 3]
        if step == 3:
            gbias[...] = total
            return
        axis = "yxz"[step]
        at = place.at(axis)
        bias_slots[step, at] = total
        for d in (1, 2, 3):
            spot = bias_slots.at[step, at]
            bias_waits.append(post(spot, spot, place.peer(axis, d)))

    layer2.advance()
    layer1.advance()
    for step in range(7):
        edge0.advance()
        node0.advance()
        if layer2.step < 8:
            layer2.advance()
        if layer1.step < 8:
            layer1.advance()
        if step < 4:
            bias_step(step)
    assert all(group.step == 8 for group in (edge0, node0, layer1, layer2))
    for copy in posted:
        copy.wait_send()


def finish(fine_in, lifted_in, grads, gbias, fine_out, lifted_out, matrices_out, biases_out, wide, sems):
    copies = [
        pltpu.make_async_copy(fine_in, fine_out, sems.at[18]),
        pltpu.make_async_copy(lifted_in, lifted_out, sems.at[19]),
    ]
    for copy in copies:
        copy.start()
    for i in range(18):
        wide[i] = grads[i].astype(F32)
        copies.append(pltpu.make_async_copy(wide.at[i], matrices_out.at[i // 6, i % 6], sems.at[i]))
        copies[-1].start()
    for layer in range(3):
        biases_out[layer] = gbias[4 * layer:4 * layer + 4, :]
    for copy in copies:
        copy.wait()


def group_scratch(count):
    return [
        pltpu.VMEM((2, count, B, H), BF16),
        pltpu.VMEM((count, B, H), BF16),
        pltpu.VMEM((count, B, H), BF16),
        pltpu.VMEM((3, count, 64, H), BF16),
        pltpu.VMEM((count, 64, H), BF16),
        pltpu.VMEM((3, count, 16, H), BF16),
        pltpu.VMEM((count, 16, H), BF16),
        pltpu.VMEM((4, count, 16, H), BF16),
        pltpu.VMEM((count, 16, H), BF16),
    ]


def local(fine_state, coarse_state, up_target, down_source, halo_lists, same_source, matrices, biases, fine_cotangent):
    total_fine = fine_state.shape[0] * lax.axis_size("gx") * lax.axis_size("gy")
    scratch = [
        pltpu.SemaphoreType.DMA((COPIES,)),
        pltpu.SemaphoreType.DMA((COPIES,)),
        pltpu.VMEM((6, B, B), BF16),
        pltpu.VMEM((6, 2 * B, B), BF16),
        pltpu.VMEM((11, B, B), BF16),
        pltpu.VMEM((11, B, B), BF16),
        pltpu.VMEM((11, B, B), BF16),
        pltpu.VMEM((11, B, 1), F32),
        pltpu.VMEM((11, B, B), BF16),
        pltpu.VMEM((4, B, B), BF16),
        pltpu.VMEM((3, B, B), BF16),
        pltpu.VMEM((3, B, B), BF16),
        pltpu.VMEM((3, B, 1), F32),
        pltpu.VMEM((B, B), BF16),
        pltpu.VMEM((2 * B, B), BF16),
        pltpu.VMEM((2 * B, B), BF16),
        pltpu.VMEM((5, B, B), F32),
        pltpu.VMEM((4, 2, H, B), BF16),
        pltpu.VMEM((4, 2, H, B), BF16),
        pltpu.VMEM((4, H, B), BF16),
        pltpu.VMEM((2, H, B), BF16),
        pltpu.VMEM((3, B, B), BF16),
        pltpu.VMEM((16, B), F32),
        pltpu.VMEM((16, B), F32),
        pltpu.VMEM((3, 4, 16, B), F32),
        pltpu.VMEM((16, H), jnp.int32),
        pltpu.VMEM((16, B), jnp.int32),
        pltpu.SemaphoreType.DMA((12,)),
        pltpu.VMEM((B, B), BF16),
        pltpu.VMEM((B, B), BF16),
        pltpu.VMEM((B, B), BF16),
        pltpu.VMEM((4, H), jnp.int32),
        pltpu.VMEM((6, H), jnp.int32),
        pltpu.VMEM((2, H), jnp.int32),
        pltpu.VMEM((12, H), jnp.int32),
        pltpu.VMEM((3, 6, B, B), BF16),
        pltpu.VMEM((3, 4, B), F32),
    ]
    for count in (3, 3, 6, 6):
        scratch += group_scratch(count)
    vmem = pl.BlockSpec(memory_space=pltpu.VMEM)

    def body(*refs):
        kernel(total_fine, *refs)

    fine_out, lifted, grads, gbias = pl.pallas_call(
        body,
        out_shape=(
            jax.ShapeDtypeStruct((B, B), BF16),
            jax.ShapeDtypeStruct((B, B), F32),
            jax.ShapeDtypeStruct((18, B, B), BF16),
            jax.ShapeDtypeStruct((16, B), F32),
        ),
        in_specs=[pl.BlockSpec(memory_space=pltpu.HBM)] * 9,
        out_specs=(vmem,) * 4,
        scratch_shapes=scratch,
        compiler_params=pltpu.CompilerParams(
            collective_id=0, has_side_effects=True, vmem_limit_bytes=32 << 20
        ),
        name="sweep",
    )(*[
        pltpu.with_memory_space_constraint(value, pltpu.HBM)
        for value in (
            fine_state, coarse_state, fine_cotangent, up_target.reshape(4, H), down_source.reshape(6, H), halo_lists,
            same_source.reshape(12, H), matrices, biases,
        )
    ])
    hbm = pl.BlockSpec(memory_space=pl.ANY)
    return pl.pallas_call(
        finish,
        out_shape=(
            jax.ShapeDtypeStruct((B, B), BF16),
            jax.ShapeDtypeStruct((B, B), F32),
            jax.ShapeDtypeStruct((3, 6, B, B), F32),
            jax.ShapeDtypeStruct((3, 4, B), F32),
        ),
        in_specs=[vmem] * 4,
        out_specs=(hbm, hbm, hbm, vmem),
        scratch_shapes=[pltpu.VMEM((18, B, B), F32), pltpu.SemaphoreType.DMA((20,))],
        compiler_params=pltpu.CompilerParams(vmem_limit_bytes=16 << 20),
        name="finish",
    )(fine_out, lifted, grads, gbias)


def solution(mesh):
    in_specs = (
        P(("gx", "gy"), None),
        P("gy", None),
        P(("gx", "gy")),
        P(("gx", "gy")),
        P("gy", None),
        P("gy"),
        P(),
        P(),
        P(("gx", "gy"), None),
    )
    out_specs = (P(("gx", "gy"), None), P("gy", None), P(), P())
    return jax.shard_map(local, mesh=mesh, in_specs=in_specs, out_specs=out_specs, check_vma=False)
```

```python
import math

import jax
import jax.numpy as jnp
from jax import lax
from jax.experimental import pallas as pl
from jax.experimental.pallas import tpu as pltpu
from jax.sharding import PartitionSpec as P

MESH = pl.DeviceIdType.MESH
F32 = jnp.float32
BF16 = jnp.bfloat16
B = 256
H = 128
UP, DOWN, SAME = (0, 2), (2, 5), (5, 11)
COPIES = 120
GROUPS = (
    (("x", "z", "y"), 0, 2, False),
    (("z", "x", "y"), 2, 3, False),
    (("y", "x", "z"), 3, 6, True),
    (("y", "z", "x"), 6, 12, True),
    (("x", "z", "y"), 12, 15, False),
    (("z", "x", "y"), 15, 18, False),
)


def dot_plain(a, b):
    return jnp.dot(a, b, preferred_element_type=F32)


def dot_rows(a, b):
    return lax.dot_general(a, b, (((0,), (0,)), ((), ())), preferred_element_type=F32)


def dot_cols(a, b):
    return lax.dot_general(a, b, (((1,), (1,)), ((), ())), preferred_element_type=F32)


def silu_parts(x):
    gate = 0.5 * jnp.tanh(0.5 * x) + 0.5
    active = x * gate
    return active, gate + active * (1.0 - gate)


def row_mean(x):
    return jnp.mean(x, axis=-1, keepdims=True)


def normed(y):
    centred = y - row_mean(y)
    scale = lax.rsqrt(row_mean(centred * centred) + 1e-05)
    return centred * scale, scale


def norm_back(g, unit, scale):
    return scale * (g - row_mean(g) - unit * row_mean(g * unit))


def col_sum(x):
    return jnp.sum(x, axis=0, keepdims=True)


class Group:
    def __init__(self, post, place, axes, rows, shared, refs, out):
        self.shared = shared
        self.post, self.place, self.axes, self.rows, self.out = post, place, axes, rows, out
        self.g, self.rc, self.s1, self.r1, self.s2, self.r2, self.s3, self.r3, self.s4 = refs
        self.count = rows.stop - rows.start
        self.step = 0
        core = place.core
        self.copies = []
        self.lanes = pl.ds(pl.multiple_of(core * H, H), H)

    def put(self, i, value):
        half = value.astype(BF16)
        self.g[0, i] = half[:, :H]
        self.g[1, i] = half[:, H:]

    def landed(self):
        for copy in self.copies:
            copy.wait_recv()
        self.copies = []

    def advance(self):
        getattr(self, "step%d" % self.step)()
        self.step += 1

    def quarter(self):
        return pl.ds(pl.multiple_of(self.place.at(self.axes[0]) * 64, 64), 64)

    def step0(self):
        other = 1 - self.place.core
        src = self.g.at[other, :, self.quarter(), :] if self.shared else self.g.at[other]
        self.copies = [self.post(src, self.rc, self.place.partner())]

    def step1(self):
        self.landed()
        core = self.place.core
        if self.shared:
            for i in range(self.count):
                own = self.g[core, i, self.quarter(), :].astype(F32)
                self.s2[i] = (own + self.rc[i].astype(F32)).astype(BF16)
            self.scatter(self.axes[1], 16, self.s2, self.r2)
            self.step = 2
            return
        for i in range(self.count):
            self.s1[i] = (self.g[core, i].astype(F32) + self.rc[i].astype(F32)).astype(BF16)
        self.scatter(self.axes[0], 64, self.s1, self.r1)

    def scatter(self, axis, size, src, landing):
        at = self.place.at(axis)
        for d in (1, 2, 3):
            to = lax.rem(at + d, 4)
            rows = pl.ds(pl.multiple_of(to * size, size), size)
            self.copies.append(self.post(src.at[:, rows, :], landing.at[d - 1], self.place.peer(axis, d)))

    def gather_sum(self, axis, size, src, landing, out):
        at = self.place.at(axis)
        rows = pl.ds(pl.multiple_of(at * size, size), size)
        for i in range(self.count):
            total = src[i, rows, :].astype(F32)
            for d in range(3):
                total += landing[d, i].astype(F32)
            out[i] = total.astype(BF16)

    def step2(self):
        self.landed()
        self.gather_sum(self.axes[0], 64, self.s1, self.r1, self.s2)
        self.scatter(self.axes[1], 16, self.s2, self.r2)

    def step3(self):
        self.landed()
        self.gather_sum(self.axes[1], 16, self.s2, self.r2, self.s3)
        at = self.place.at(self.axes[2])
        for d in (1, 2, 3):
            self.copies.append(self.post(self.s3, self.r3.at[at], self.place.peer(self.axes[2], d)))
        self.r3[at] = self.s3[...]

    def step4(self):
        self.landed()
        for i in range(self.count):
            total = self.r3[0, i].astype(F32)
            for j in (1, 2, 3):
                total += self.r3[j, i].astype(F32)
            self.s4[i] = total.astype(BF16)
        start = self.place.at(self.axes[0]) * 64 + self.place.at(self.axes[1]) * 16
        rows = pl.ds(pl.multiple_of(start, 16), 16)
        spot = self.out.at[self.rows, rows, self.lanes]
        for d in (1, 2, 3):
            self.copies.append(self.post(self.s4, spot, self.place.peer(self.axes[1], d)))
        for i in range(self.count):
            self.out[self.rows.start + i, rows, self.lanes] = self.s4[i]

    def step5(self):
        self.landed()
        spot = self.out.at[self.rows, self.quarter(), self.lanes]
        for d in (1, 2, 3):
            self.copies.append(self.post(spot, spot, self.place.peer(self.axes[0], d)))

    def step6(self):
        self.landed()
        spot = self.out.at[self.rows, :, self.lanes]
        self.copies = [self.post(spot, spot, self.place.partner())]

    def step7(self):
        self.landed()


class Place:
    def __init__(self):
        self.gx = lax.axis_index("gx")
        self.gy = lax.axis_index("gy")
        self.core = lax.rem(self.gy, 2)
        self.x = lax.rem(self.gy // 2, 4)
        self.z = self.gy // 8

    def at(self, axis):
        return {"x": self.x, "y": self.gx, "z": self.z}[axis]

    def partner(self):
        return (self.gx, self.gy + 1 - 2 * self.core)

    def peer(self, axis, d):
        if axis == "y":
            return (lax.rem(self.gx + d, 4), self.gy)
        if axis == "x":
            return (self.gx, self.z * 8 + lax.rem(self.x + d, 4) * 2 + self.core)
        return (self.gx, lax.rem(self.z + d, 4) * 8 + self.x * 2 + self.core)

    def beside(self, d):
        return (self.gx, lax.rem(self.gy + d + 32, 32))


def deal(source, raw, index, first, end):
    ways = end - first
    raw[:2 * ways, :] = source[...]
    rows = raw[...]
    lane = lax.broadcasted_iota(jnp.int32, rows.shape, 1)
    for k in range(ways):
        place = lane * ways + k
        picked = jnp.take_along_axis(rows, lax.rem(place, H), axis=1, mode="promise_in_bounds")
        line = place[0:1] // H
        for half in (0, 1):
            row = picked[ways * half:ways * half + 1]
            for i in range(1, ways):
                row = jnp.where(line == i, picked[ways * half + i:ways * half + i + 1], row)
            index[first + k:first + k + 1, half * H:half * H + H] = row


def kernel(total_fine, *refs):
    inputs, (fine_out, lifted_cot, grads, gbias) = refs[:9], refs[9:13]
    (send_sems, recv_sems, onehot, samehot, act, slope, unit, scale, dys, nact, nslope, nunit, nscale,
     table, ext, gtab, pres, csend, crecv, hsend, hback, node_in, bias_acc, bias_core, bias_slots, raw, index, load_sems,
     fine, coarse, cot, up_raw, down_raw, halo_raw, same_raw, mats, bias) = refs[13:50]
    group_refs = refs[50:]
    place = Place()
    posted = []

    def post(src, dst, device):
        i = len(posted)
        copy = pltpu.make_async_remote_copy(
            src_ref=src, dst_ref=dst, send_sem=send_sems.at[i], recv_sem=recv_sems.at[i],
            device_id=device, device_id_type=MESH,
        )
        copy.start()
        posted.append(copy)
        return copy

    barrier = pltpu.get_barrier_semaphore()
    near = [place.peer(a, d) for a in ("x", "y", "z") for d in (1, 2, 3)]
    near += [place.partner(), place.beside(1), place.beside(-1)]
    for device in near:
        pl.semaphore_signal(barrier, inc=1, device_id=device, device_id_type=MESH)

    loads = []
    for i, (src, dst) in enumerate([
        (inputs[3], up_raw), (inputs[0], fine), (inputs[1], coarse), (inputs[8], bias),
        (inputs[7].at[0, 0:3], mats.at[0, 0:3]), (inputs[4], down_raw), (inputs[6], same_raw), (inputs[5], halo_raw),
        (inputs[7].at[0, 3:6], mats.at[0, 3:6]), (inputs[7].at[2], mats.at[2]), (inputs[7].at[1], mats.at[1]),
        (inputs[2], cot),
    ]):
        loads.append(pltpu.make_async_copy(src, dst, load_sems.at[i]))
        loads[-1].start()

    edge0a, edge0b, node0, layer1, layer2a, layer2b = [
        Group(post, place, axes, slice(first, end), shared, group_refs[9 * at:9 * at + 9], grads)
        for at, (axes, first, end, shared) in enumerate(GROUPS)
    ]

    bias_acc[...] = jnp.zeros_like(bias_acc)
    for load in loads[:5]:
        load.wait()
    deal(up_raw, raw, index, *UP)

    def step_on(*groups):
        for group in groups:
            if group.step < 8:
                group.advance()

    def add_bias(row, value):
        bias_acc[row:row + 1, :] += value

    def w(layer, i):
        return mats[layer, i]

    def b(layer, i):
        return bias[layer, i:i + 1, :]

    def hot_rows(block, size):
        nodes = lax.broadcasted_iota(jnp.int32, (size, B), 0)
        return jnp.where(nodes == index[block:block + 1, :], 1.0, 0.0).astype(BF16)

    def edge_forward(block, pre, layer):
        active, slope_now = silu_parts(pre)
        half = active.astype(BF16)
        act[block] = half
        slope[block] = slope_now.astype(BF16)
        message, scale_now = normed(dot_plain(half, w(layer, 2)) + b(layer, 1))
        unit[block] = message.astype(BF16)
        scale[block] = scale_now
        return message

    def edge_backward(block, g, layer):
        dy = norm_back(g, unit[block].astype(F32), scale[block])
        half = dy.astype(BF16)
        dys[block] = half
        dp = slope[block].astype(F32) * dot_cols(half, w(layer, 2))
        return dp, col_sum(dy), col_sum(dp)

    def node_forward(layer, state, agg, pre):
        node_in[layer] = agg
        active, slope_now = silu_parts(pre + dot_plain(agg, w(layer, 4)))
        half = active.astype(BF16)
        nact[layer] = half
        nslope[layer] = slope_now.astype(BF16)
        unit_now, scale_now = normed(dot_plain(half, w(layer, 5)) + b(layer, 3))
        nunit[layer] = unit_now.astype(BF16)
        nscale[layer] = scale_now
        return (state.astype(F32) + unit_now).astype(BF16)

    def node_backward(layer, g, share):
        dz = norm_back(g, nunit[layer].astype(F32), nscale[layer])
        dz16 = dz.astype(BF16)
        dq = nslope[layer].astype(F32) * dot_cols(dz16, w(layer, 5))
        dq16 = dq.astype(BF16)
        add_bias(4 * layer + 3, share * col_sum(dz))
        add_bias(4 * layer + 2, share * col_sum(dq))
        return dz16, dq16

    def sum_start(first, value):
        half = value.astype(BF16)
        csend[first, 0] = half[:H]
        csend[first, 1] = half[H:]
        odd = lax.rem(place.gx, 2)
        one = (place.gx + 1 - 2 * odd, place.gy)
        two = (lax.rem(place.gx + 2 * odd + 3, 4), place.gy)
        waits = [
            post(csend.at[first, 0], crecv.at[first, 0], one),
            post(csend.at[first, 1], crecv.at[first, 1], two),
        ]
        return waits, one, two

    def sum_middle(first, state):
        waits, one, two = state
        for i in (0, 1):
            waits[i].wait_recv()
            both = csend[first, i].astype(F32) + crecv[first, i].astype(F32)
            csend[first + 1, i] = both.astype(BF16)
        return [
            post(csend.at[first + 1, 0], crecv.at[first + 1, 0], two),
            post(csend.at[first + 1, 1], crecv.at[first + 1, 1], one),
        ]

    def sum_end(first, waits):
        parts = []
        for i in (0, 1):
            waits[i].wait_recv()
            both = csend[first + 1, i].astype(F32) + crecv[first + 1, i].astype(F32)
            parts.append(both.astype(BF16))
        return jnp.concatenate(parts, axis=0)

    for block in range(*UP):
        onehot[block] = hot_rows(block, B)
    sent = dot_plain(fine[...], w(0, 0)) + b(0, 0)
    table[...] = dot_plain(coarse[...], w(0, 1)).astype(BF16)
    up_sum = None
    for block in range(*UP):
        message = edge_forward(block, sent + dot_rows(onehot[block], table[...]), 0)
        part = dot_plain(onehot[block], message.astype(BF16))
        up_sum = part if up_sum is None else up_sum + part

    pl.semaphore_wait(barrier, len(near))
    state = sum_start(0, up_sum)
    for load in loads[5:]:
        load.wait()
    pres[0] = dot_plain(coarse[...], w(0, 3)) + b(0, 2)
    deal(down_raw, raw, index, *DOWN)
    deal(same_raw, raw, index, *SAME)
    index[11:12, :H] = halo_raw[0:1, :]
    index[11:12, H:] = halo_raw[1:2, :]
    for block in range(*DOWN):
        onehot[block] = hot_rows(block, B)
    onehot[5] = hot_rows(11, B)
    state = sum_middle(0, state)
    for block in range(*SAME):
        samehot[block - 5] = hot_rows(block, 2 * B)
    pres[1] = dot_plain(fine[...], w(2, 3)) + b(2, 2)
    pres[2] = dot_plain(fine[...], w(2, 1)) + b(2, 0)
    agg = sum_end(0, state)
    lifted = node_forward(0, coarse[...], agg, pres[0])
    ext[H:H + B] = lifted
    payload = dot_rows(onehot[5], lifted).astype(BF16)
    hsend[0] = payload[:H]
    hsend[1] = payload[H:]
    halo = [
        post(hsend.at[0], ext.at[H + B:], place.beside(-1)),
        post(hsend.at[1], ext.at[:H], place.beside(1)),
    ]

    pres[3] = dot_plain(lifted, w(1, 1)) + b(1, 0)
    pres[4] = dot_plain(lifted, w(1, 3)) + b(1, 2)
    for copy in halo:
        copy.wait_recv()
    gtab[...] = dot_plain(ext[...], w(1, 0)).astype(BF16)
    same_sum = None
    for block in range(*SAME):
        message = edge_forward(block, pres[3] + dot_rows(samehot[block - 5], gtab[...]), 1)
        same_sum = message if same_sum is None else same_sum + message
    mixed = node_forward(1, ext[H:H + B], same_sum.astype(BF16), pres[4])
    nact[3] = mixed

    table[...] = dot_plain(mixed, w(2, 0)).astype(BF16)
    down_sum = None
    for block in range(*DOWN):
        message = edge_forward(block, pres[2] + dot_rows(onehot[block], table[...]), 2)
        down_sum = message if down_sum is None else down_sum + message
    fine_out[...] = node_forward(2, fine[...], down_sum.astype(BF16), pres[1])
    dz2, dq2 = node_backward(2, cot[...].astype(F32) * (1.0 / math.sqrt(total_fine)), 1.0)
    g = dot_cols(dq2, w(2, 4))
    taken = back = None
    for block in range(*DOWN):
        dp, db2, db1 = edge_backward(block, g, 2)
        add_bias(8, db1)
        add_bias(9, db2)
        part = dot_plain(onehot[block], dp.astype(BF16))
        taken = dp if taken is None else taken + dp
        back = part if back is None else back + part
    state = sum_start(2, back)
    layer2a.put(1, dot_rows(fine[...], taken.astype(BF16)))
    layer2a.put(2, dot_rows(act[2:5].reshape(3 * B, B), dys[2:5].reshape(3 * B, B)))
    state = sum_middle(2, state)
    layer2b.put(0, dot_rows(fine[...], dq2))
    layer2b.put(1, dot_rows(node_in[2], dq2))
    layer2b.put(2, dot_rows(nact[2], dz2))
    sent_half = sum_end(2, state)
    grad_mixed = dot_cols(sent_half, w(2, 0))
    layer2a.put(0, 0.25 * dot_rows(nact[3], sent_half))
    step_on(layer2a, layer2b)

    dz1, dq1 = node_backward(1, grad_mixed, 0.25)
    pres[0] = grad_mixed + dot_cols(dq1, w(1, 3))
    g = dot_cols(dq1, w(1, 4))
    taken = back = None
    for block in range(*SAME):
        dp, db2, db1 = edge_backward(block, g, 1)
        add_bias(4, 0.25 * db1)
        add_bias(5, 0.25 * db2)
        part = dot_plain(samehot[block - 5], dp.astype(BF16))
        taken = dp if taken is None else taken + dp
        back = part if back is None else back + part
    hsend[2] = back[:H].astype(BF16)
    hsend[3] = back[H + B:].astype(BF16)
    returns = [
        post(hsend.at[2], hback.at[1], place.beside(-1)),
        post(hsend.at[3], hback.at[0], place.beside(1)),
    ]
    own = back[H:H + B]
    step_on(layer2a, layer2b)
    lifted = ext[H:H + B]
    taken_half = taken.astype(BF16)
    layer1.put(1, 1.0 * dot_rows(lifted, taken_half))
    layer1.put(2, dot_rows(act[5:11].reshape(6 * B, B), dys[5:11].reshape(6 * B, B)))
    layer1.put(3, dot_rows(lifted, dq1))
    layer1.put(4, dot_rows(node_in[1], dq1))
    layer1.put(5, dot_rows(nact[1], dz1))
    grad_lifted = pres[0] + dot_cols(taken_half, w(1, 1))
    step_on(layer2a, layer2b)
    for copy in returns:
        copy.wait_recv()
    own += dot_plain(onehot[5], hback[...].reshape(B, B))
    own_half = own.astype(BF16)
    grad_lifted += dot_cols(own_half, w(1, 0))
    lifted_cot[...] = grad_lifted * math.sqrt(total_fine)
    layer1.put(0, dot_rows(lifted, own_half))
    step_on(layer1)

    dz0, dq0 = node_backward(0, grad_lifted, 0.25)
    table[...] = dot_cols(dq0, w(0, 4)).astype(BF16)
    step_on(layer2a, layer2b, layer1)
    taken = back = None
    for block in range(*UP):
        dp, db2, db1 = edge_backward(block, dot_rows(onehot[block], table[...]), 0)
        add_bias(0, db1)
        add_bias(1, db2)
        part = dot_plain(onehot[block], dp.astype(BF16))
        taken = dp if taken is None else taken + dp
        back = part if back is None else back + part
    edge0a.put(0, dot_rows(fine[...], taken.astype(BF16)))
    edge0a.put(1, dot_rows(coarse[...], back.astype(BF16)))
    edge0b.put(0, dot_rows(act[0:2].reshape(2 * B, B), dys[0:2].reshape(2 * B, B)))
    step_on(edge0a, edge0b)
    bias_waits = [post(bias_acc, bias_core, place.partner())]
    node0.put(0, dot_rows(coarse[...], dq0))
    node0.put(1, dot_rows(node_in[0], dq0))
    node0.put(2, dot_rows(nact[0], dz0))
    step_on(node0)

    def bias_step(step):
        for copy in bias_waits:
            copy.wait_recv()
        bias_waits.clear()
        if step == 0:
            total = bias_acc[...] + bias_core[...]
        else:
            total = bias_slots[step - 1, 0] + bias_slots[step - 1, 1]
            total = total + bias_slots[step - 1, 2] + bias_slots[step - 1, 3]
        if step == 3:
            gbias[...] = total
            return
        axis = "yxz"[step]
        at = place.at(axis)
        bias_slots[step, at] = total
        for d in (1, 2, 3):
            spot = bias_slots.at[step, at]
            bias_waits.append(post(spot, spot, place.peer(axis, d)))

    for step in range(7):
        step_on(edge0a, edge0b, node0, layer2a, layer2b, layer1)
        if step < 4:
            bias_step(step)
    assert all(group.step == 8 for group in (edge0a, edge0b, node0, layer1, layer2a, layer2b))
    for copy in posted:
        copy.wait_send()


def finish(fine_in, lifted_in, grads, gbias, fine_out, lifted_out, matrices_out, biases_out, wide, sems):
    copies = [
        pltpu.make_async_copy(fine_in, fine_out, sems.at[18]),
        pltpu.make_async_copy(lifted_in, lifted_out, sems.at[19]),
    ]
    for copy in copies:
        copy.start()
    for i in range(18):
        wide[i] = grads[i].astype(F32)
        copies.append(pltpu.make_async_copy(wide.at[i], matrices_out.at[i // 6, i % 6], sems.at[i]))
        copies[-1].start()
    for layer in range(3):
        biases_out[layer] = gbias[4 * layer:4 * layer + 4, :]
    for copy in copies:
        copy.wait()


def group_scratch(count, shared):
    whole = 64 if shared else B
    spare = 16 if shared else B
    return [
        pltpu.VMEM((2, count, B, H), BF16),
        pltpu.VMEM((count, whole, H), BF16),
        pltpu.VMEM((count, spare, H), BF16),
        pltpu.VMEM((3, count, spare // 4, H), BF16),
        pltpu.VMEM((count, 64, H), BF16),
        pltpu.VMEM((3, count, 16, H), BF16),
        pltpu.VMEM((count, 16, H), BF16),
        pltpu.VMEM((4, count, 16, H), BF16),
        pltpu.VMEM((count, 16, H), BF16),
    ]


def local(fine_state, coarse_state, up_target, down_source, halo_lists, same_source, matrices, biases, fine_cotangent):
    total_fine = fine_state.shape[0] * lax.axis_size("gx") * lax.axis_size("gy")
    scratch = [
        pltpu.SemaphoreType.DMA((COPIES,)),
        pltpu.SemaphoreType.DMA((COPIES,)),
        pltpu.VMEM((6, B, B), BF16),
        pltpu.VMEM((6, 2 * B, B), BF16),
        pltpu.VMEM((11, B, B), BF16),
        pltpu.VMEM((11, B, B), BF16),
        pltpu.VMEM((11, B, B), BF16),
        pltpu.VMEM((11, B, 1), F32),
        pltpu.VMEM((11, B, B), BF16),
        pltpu.VMEM((4, B, B), BF16),
        pltpu.VMEM((3, B, B), BF16),
        pltpu.VMEM((3, B, B), BF16),
        pltpu.VMEM((3, B, 1), F32),
        pltpu.VMEM((B, B), BF16),
        pltpu.VMEM((2 * B, B), BF16),
        pltpu.VMEM((2 * B, B), BF16),
        pltpu.VMEM((5, B, B), F32),
        pltpu.VMEM((4, 2, H, B), BF16),
        pltpu.VMEM((4, 2, H, B), BF16),
        pltpu.VMEM((4, H, B), BF16),
        pltpu.VMEM((2, H, B), BF16),
        pltpu.VMEM((3, B, B), BF16),
        pltpu.VMEM((16, B), F32),
        pltpu.VMEM((16, B), F32),
        pltpu.VMEM((3, 4, 16, B), F32),
        pltpu.VMEM((16, H), jnp.int32),
        pltpu.VMEM((16, B), jnp.int32),
        pltpu.SemaphoreType.DMA((12,)),
        pltpu.VMEM((B, B), BF16),
        pltpu.VMEM((B, B), BF16),
        pltpu.VMEM((B, B), BF16),
        pltpu.VMEM((4, H), jnp.int32),
        pltpu.VMEM((6, H), jnp.int32),
        pltpu.VMEM((2, H), jnp.int32),
        pltpu.VMEM((12, H), jnp.int32),
        pltpu.VMEM((3, 6, B, B), BF16),
        pltpu.VMEM((3, 4, B), F32),
    ]
    for _, first, end, shared in GROUPS:
        scratch += group_scratch(end - first, shared)
    vmem = pl.BlockSpec(memory_space=pltpu.VMEM)

    def body(*refs):
        kernel(total_fine, *refs)

    fine_out, lifted, grads, gbias = pl.pallas_call(
        body,
        out_shape=(
            jax.ShapeDtypeStruct((B, B), BF16),
            jax.ShapeDtypeStruct((B, B), F32),
            jax.ShapeDtypeStruct((18, B, B), BF16),
            jax.ShapeDtypeStruct((16, B), F32),
        ),
        in_specs=[pl.BlockSpec(memory_space=pltpu.HBM)] * 9,
        out_specs=(vmem,) * 4,
        scratch_shapes=scratch,
        compiler_params=pltpu.CompilerParams(
            collective_id=0, has_side_effects=True, vmem_limit_bytes=32 << 20
        ),
        name="sweep",
    )(*[
        pltpu.with_memory_space_constraint(value, pltpu.HBM)
        for value in (
            fine_state, coarse_state, fine_cotangent, up_target.reshape(4, H), down_source.reshape(6, H), halo_lists,
            same_source.reshape(12, H), matrices, biases,
        )
    ])
    hbm = pl.BlockSpec(memory_space=pl.ANY)
    return pl.pallas_call(
        finish,
        out_shape=(
            jax.ShapeDtypeStruct((B, B), BF16),
            jax.ShapeDtypeStruct((B, B), F32),
            jax.ShapeDtypeStruct((3, 6, B, B), F32),
            jax.ShapeDtypeStruct((3, 4, B), F32),
        ),
        in_specs=[vmem] * 4,
        out_specs=(hbm, hbm, hbm, vmem),
        scratch_shapes=[pltpu.VMEM((18, B, B), F32), pltpu.SemaphoreType.DMA((20,))],
        compiler_params=pltpu.CompilerParams(vmem_limit_bytes=16 << 20),
        name="finish",
    )(fine_out, lifted, grads, gbias)


def solution(mesh):
    in_specs = (
        P(("gx", "gy"), None),
        P("gy", None),
        P(("gx", "gy")),
        P(("gx", "gy")),
        P("gy", None),
        P("gy"),
        P(),
        P(),
        P(("gx", "gy"), None),
    )
    out_specs = (P(("gx", "gy"), None), P("gy", None), P(), P())
    return jax.shard_map(local, mesh=mesh, in_specs=in_specs, out_specs=out_specs, check_vma=False)
```

```python
import math

import jax
import jax.numpy as jnp
from jax import lax
from jax.experimental import pallas as pl
from jax.experimental.pallas import tpu as pltpu
from jax.sharding import PartitionSpec as P

MESH = pl.DeviceIdType.MESH
F32 = jnp.float32
BF16 = jnp.bfloat16
B = 256
H = 128
UP, DOWN, SAME = (0, 2), (2, 5), (5, 11)
COPIES = 160
PIECES = 4
GROUPS = (
    ("quick", ("x", "y", "z"), 0, 1),
    ("quick", ("z", "x", "y"), 1, 2),
    ("quick", ("y", "z", "x"), 2, 3),
    ("same", ("y", "x", "z"), 3, 6),
    ("same", ("y", "z", "x"), 6, 12),
    ("fine", ("x", "z", "y"), 12, 15),
    ("fine", ("z", "x", "y"), 15, 18),
)


def dot_plain(a, b):
    return jnp.dot(a, b, preferred_element_type=F32)


def dot_rows(a, b):
    return lax.dot_general(a, b, (((0,), (0,)), ((), ())), preferred_element_type=F32)


def dot_cols(a, b):
    return lax.dot_general(a, b, (((1,), (1,)), ((), ())), preferred_element_type=F32)


def silu_parts(x):
    gate = 0.5 * jnp.tanh(0.5 * x) + 0.5
    active = x * gate
    return active, gate + active * (1.0 - gate)


def row_mean(x):
    return jnp.mean(x, axis=-1, keepdims=True)


def normed(y):
    centred = y - row_mean(y)
    scale = lax.rsqrt(row_mean(centred * centred) + 1e-05)
    return centred * scale, scale


def norm_back(g, unit, scale):
    return scale * (g - row_mean(g) - unit * row_mean(g * unit))


def col_sum(x):
    return jnp.sum(x, axis=0, keepdims=True)


class Group:
    def __init__(self, post, place, axes, rows, shared, refs, out):
        self.shared = shared
        self.post, self.place, self.axes, self.rows, self.out = post, place, axes, rows, out
        self.g, self.rc, self.s1, self.r1, self.s2, self.r2, self.s3, self.r3, self.s4 = refs
        self.count = rows.stop - rows.start
        self.step = 0
        self.copies = []

    def put(self, i, value):
        half = value.astype(BF16)
        self.g[0, i] = half[:, :H]
        self.g[1, i] = half[:, H:]

    def landed(self):
        for copy in self.copies:
            copy.wait_recv()
        self.copies = []

    def advance(self):
        getattr(self, "step%d" % self.step)()
        self.step += 1

    def quarter(self):
        return pl.ds(pl.multiple_of(self.place.at(self.axes[0]) * 64, 64), 64)

    def step0(self):
        other = 1 - self.place.core
        src = self.g.at[other, :, self.quarter(), :] if self.shared else self.g.at[other]
        self.copies = [self.post(src, self.rc, self.place.partner())]

    def step1(self):
        self.landed()
        core = self.place.core
        if self.shared:
            for i in range(self.count):
                own = self.g[core, i, self.quarter(), :].astype(F32)
                self.s2[i] = (own + self.rc[i].astype(F32)).astype(BF16)
            self.scatter(self.axes[1], 16, self.s2, self.r2)
            self.step = 2
            return
        for i in range(self.count):
            self.s1[i] = (self.g[core, i].astype(F32) + self.rc[i].astype(F32)).astype(BF16)
        self.scatter(self.axes[0], 64, self.s1, self.r1)

    def scatter(self, axis, size, src, landing):
        at = self.place.at(axis)
        for d in (1, 2, 3):
            to = lax.rem(at + d, 4)
            rows = pl.ds(pl.multiple_of(to * size, size), size)
            self.copies.append(self.post(src.at[:, rows, :], landing.at[d - 1], self.place.peer(axis, d)))

    def gather_sum(self, axis, size, src, landing, out):
        at = self.place.at(axis)
        rows = pl.ds(pl.multiple_of(at * size, size), size)
        for i in range(self.count):
            total = src[i, rows, :].astype(F32)
            for d in range(3):
                total += landing[d, i].astype(F32)
            out[i] = total.astype(BF16)

    def step2(self):
        self.landed()
        self.gather_sum(self.axes[0], 64, self.s1, self.r1, self.s2)
        self.scatter(self.axes[1], 16, self.s2, self.r2)

    def step3(self):
        self.landed()
        self.gather_sum(self.axes[1], 16, self.s2, self.r2, self.s3)
        self.share(self.axes[2], self.s3, self.r3)

    def share(self, axis, src, slots):
        at = self.place.at(axis)
        for d in (1, 2, 3):
            self.copies.append(self.post(src, slots.at[at], self.place.peer(axis, d)))
        slots[at] = src[...]

    def slot_sum(self, slots, out):
        for i in range(self.count):
            total = slots[0, i].astype(F32)
            for j in (1, 2, 3):
                total += slots[j, i].astype(F32)
            out[i] = total.astype(BF16)

    def step4(self):
        self.landed()
        self.slot_sum(self.r3, self.s4)
        start = self.place.at(self.axes[0]) * 64 + self.place.at(self.axes[1]) * 16
        rows = pl.ds(pl.multiple_of(start, 16), 16)
        spot = self.out.at[self.place.core, self.rows, rows, :]
        for d in (1, 2, 3):
            self.copies.append(self.post(self.s4, spot, self.place.peer(self.axes[1], d)))
        for i in range(self.count):
            self.out[self.place.core, self.rows.start + i, rows, :] = self.s4[i]

    def step5(self):
        self.landed()
        spot = self.out.at[self.place.core, self.rows, self.quarter(), :]
        for d in (1, 2, 3):
            self.copies.append(self.post(spot, spot, self.place.peer(self.axes[0], d)))

    def step6(self):
        self.landed()
        spot = self.out.at[self.place.core, self.rows, :, :]
        self.copies = [self.post(spot, spot, self.place.partner())]

    def step7(self):
        self.landed()


class Quick(Group):
    def step2(self):
        self.landed()
        self.gather_sum(self.axes[0], 64, self.s1, self.r1, self.s2)
        self.share(self.axes[1], self.s2, self.r2)

    def step3(self):
        self.landed()
        self.slot_sum(self.r2, self.s3)
        self.share(self.axes[2], self.s3, self.r3)

    def step4(self):
        self.landed()
        self.slot_sum(self.r3, self.s4)
        spot = self.out.at[self.place.core, self.rows, self.quarter(), :]
        for d in (1, 2, 3):
            self.copies.append(self.post(self.s4, spot, self.place.peer(self.axes[0], d)))
        for i in range(self.count):
            self.out[self.place.core, self.rows.start + i, self.quarter(), :] = self.s4[i]
        self.step = 5


class Place:
    def __init__(self):
        self.gx = lax.axis_index("gx")
        self.gy = lax.axis_index("gy")
        self.core = lax.rem(self.gy, 2)
        self.x = lax.rem(self.gy // 2, 4)
        self.z = self.gy // 8

    def at(self, axis):
        return {"x": self.x, "y": self.gx, "z": self.z}[axis]

    def partner(self):
        return (self.gx, self.gy + 1 - 2 * self.core)

    def peer(self, axis, d):
        if axis == "y":
            return (lax.rem(self.gx + d, 4), self.gy)
        if axis == "x":
            return (self.gx, self.z * 8 + lax.rem(self.x + d, 4) * 2 + self.core)
        return (self.gx, lax.rem(self.z + d, 4) * 8 + self.x * 2 + self.core)

    def beside(self, d):
        return (self.gx, lax.rem(self.gy + d + 32, 32))


def deal(source, raw, index, first, end):
    ways = end - first
    raw[:2 * ways, :] = source[...]
    rows = raw[...]
    lane = lax.broadcasted_iota(jnp.int32, rows.shape, 1)
    for k in range(ways):
        place = lane * ways + k
        picked = jnp.take_along_axis(rows, lax.rem(place, H), axis=1, mode="promise_in_bounds")
        line = place[0:1] // H
        for half in (0, 1):
            row = picked[ways * half:ways * half + 1]
            for i in range(1, ways):
                row = jnp.where(line == i, picked[ways * half + i:ways * half + i + 1], row)
            index[first + k:first + k + 1, half * H:half * H + H] = row


def kernel(total_fine, *refs):
    inputs, (fine_out, lifted_cot, grads, gbias) = refs[:9], refs[9:13]
    (send_sems, recv_sems, onehot, samehot, act, slope, unit, scale, dys, nact, nslope, nunit, nscale,
     table, ext, gtab, pres, csend, crecv, hsend, hback, node_in, bias_acc, bias_core, bias_slots, raw, index, load_sems, summed,
     fine, coarse, cot, up_raw, down_raw, halo_raw, same_raw, mats, bias) = refs[13:51]
    group_refs = refs[51:]
    place = Place()
    posted = []

    def post(src, dst, device):
        i = len(posted)
        copy = pltpu.make_async_remote_copy(
            src_ref=src, dst_ref=dst, send_sem=send_sems.at[i], recv_sem=recv_sems.at[i],
            device_id=device, device_id_type=MESH,
        )
        copy.start()
        posted.append(copy)
        return copy

    barrier = pltpu.get_barrier_semaphore()
    near = [place.peer(a, d) for a in ("x", "y", "z") for d in (1, 2, 3)]
    near += [place.partner(), place.beside(1), place.beside(-1)]
    for device in near:
        pl.semaphore_signal(barrier, inc=1, device_id=device, device_id_type=MESH)

    loads = []
    for i, (src, dst) in enumerate([
        (inputs[3], up_raw), (inputs[0], fine), (inputs[1], coarse), (inputs[8], bias),
        (inputs[7].at[0, 0:3], mats.at[0, 0:3]), (inputs[4], down_raw), (inputs[6], same_raw), (inputs[5], halo_raw),
        (inputs[7].at[0, 3:6], mats.at[0, 3:6]), (inputs[7].at[2], mats.at[2]), (inputs[7].at[1], mats.at[1]),
        (inputs[2], cot),
    ]):
        loads.append(pltpu.make_async_copy(src, dst, load_sems.at[i]))
        loads[-1].start()

    groups = [
        (Quick if kind == "quick" else Group)(
            post, place, axes, slice(first, end), kind == "same", group_refs[9 * at:9 * at + 9], grads
        )
        for at, (kind, axes, first, end) in enumerate(GROUPS)
    ]
    edge0, (node0, layer1, layer2a, layer2b) = groups[:3], groups[3:]

    bias_acc[...] = jnp.zeros_like(bias_acc)
    for load in loads[:5]:
        load.wait()
    deal(up_raw, raw, index, *UP)

    def step_on(*groups):
        for group in groups:
            if group.step < 8:
                group.advance()

    def add_bias(row, value):
        bias_acc[row:row + 1, :] += value

    def w(layer, i):
        return mats[layer, i]

    def b(layer, i):
        return bias[layer, i:i + 1, :]

    def hot_rows(block, size):
        nodes = lax.broadcasted_iota(jnp.int32, (size, B), 0)
        return jnp.where(nodes == index[block:block + 1, :], 1.0, 0.0).astype(BF16)

    def edge_forward(block, pre, layer):
        active, slope_now = silu_parts(pre)
        half = active.astype(BF16)
        act[block] = half
        slope[block] = slope_now.astype(BF16)
        message, scale_now = normed(dot_plain(half, w(layer, 2)) + b(layer, 1))
        unit[block] = message.astype(BF16)
        scale[block] = scale_now
        return message

    def edge_backward(block, g, layer):
        dy = norm_back(g, unit[block].astype(F32), scale[block])
        half = dy.astype(BF16)
        dys[block] = half
        dp = slope[block].astype(F32) * dot_cols(half, w(layer, 2))
        return dp, col_sum(dy), col_sum(dp)

    def node_forward(layer, state, agg, pre):
        node_in[layer] = agg
        active, slope_now = silu_parts(pre + dot_plain(agg, w(layer, 4)))
        half = active.astype(BF16)
        nact[layer] = half
        nslope[layer] = slope_now.astype(BF16)
        unit_now, scale_now = normed(dot_plain(half, w(layer, 5)) + b(layer, 3))
        nunit[layer] = unit_now.astype(BF16)
        nscale[layer] = scale_now
        return (state.astype(F32) + unit_now).astype(BF16)

    def node_backward(layer, g, share):
        dz = norm_back(g, nunit[layer].astype(F32), nscale[layer])
        dz16 = dz.astype(BF16)
        dq = nslope[layer].astype(F32) * dot_cols(dz16, w(layer, 5))
        dq16 = dq.astype(BF16)
        add_bias(4 * layer + 3, share * col_sum(dz))
        add_bias(4 * layer + 2, share * col_sum(dq))
        return dz16, dq16

    def piece(i):
        return pl.ds(i * (H // PIECES), H // PIECES)

    def sum_start(first, value):
        half = value.astype(BF16)
        csend[first, 0] = half[:H]
        csend[first, 1] = half[H:]
        odd = lax.rem(place.gx, 2)
        one = (place.gx + 1 - 2 * odd, place.gy)
        two = (lax.rem(place.gx + 2 * odd + 3, 4), place.gy)
        waits = []
        for i in range(PIECES):
            for side, device in ((0, one), (1, two)):
                waits.append(post(csend.at[first, side, piece(i)], crecv.at[first, side, piece(i)], device))
        return waits, one, two

    def sum_pieces(at, waits, out, then):
        for i in range(PIECES):
            for side in (0, 1):
                waits[2 * i + side].wait_recv()
                both = csend[at, side, piece(i)].astype(F32) + crecv[at, side, piece(i)].astype(F32)
                out[side, piece(i)] = both.astype(BF16)
                then(i, side)

    def sum_middle(first, state):
        waits, one, two = state
        later = []

        def send_on(i, side):
            device = (two, one)[side]
            later.append(post(csend.at[first + 1, side, piece(i)], crecv.at[first + 1, side, piece(i)], device))

        sum_pieces(first, waits, csend.at[first + 1], send_on)
        return later

    def sum_end(first, waits):
        sum_pieces(first + 1, waits, summed, lambda i, side: None)
        return summed[...].reshape(B, B)

    for block in range(*UP):
        onehot[block] = hot_rows(block, B)
    sent = dot_plain(fine[...], w(0, 0)) + b(0, 0)
    table[...] = dot_plain(coarse[...], w(0, 1)).astype(BF16)
    up_sum = None
    for block in range(*UP):
        message = edge_forward(block, sent + dot_rows(onehot[block], table[...]), 0)
        part = dot_plain(onehot[block], message.astype(BF16))
        up_sum = part if up_sum is None else up_sum + part

    pl.semaphore_wait(barrier, len(near))
    state = sum_start(0, up_sum)
    for load in loads[5:]:
        load.wait()
    pres[0] = dot_plain(coarse[...], w(0, 3)) + b(0, 2)
    deal(down_raw, raw, index, *DOWN)
    deal(same_raw, raw, index, *SAME)
    index[11:12, :H] = halo_raw[0:1, :]
    index[11:12, H:] = halo_raw[1:2, :]
    for block in range(*DOWN):
        onehot[block] = hot_rows(block, B)
    onehot[5] = hot_rows(11, B)
    state = sum_middle(0, state)
    for block in range(*SAME):
        samehot[block - 5] = hot_rows(block, 2 * B)
    pres[1] = dot_plain(fine[...], w(2, 3)) + b(2, 2)
    pres[2] = dot_plain(fine[...], w(2, 1)) + b(2, 0)
    agg = sum_end(0, state)
    lifted = node_forward(0, coarse[...], agg, pres[0])
    ext[H:H + B] = lifted
    payload = dot_rows(onehot[5], lifted).astype(BF16)
    hsend[0] = payload[:H]
    hsend[1] = payload[H:]
    halo = [
        post(hsend.at[0], ext.at[H + B:], place.beside(-1)),
        post(hsend.at[1], ext.at[:H], place.beside(1)),
    ]

    pres[3] = dot_plain(lifted, w(1, 1)) + b(1, 0)
    pres[4] = dot_plain(lifted, w(1, 3)) + b(1, 2)
    for copy in halo:
        copy.wait_recv()
    gtab[...] = dot_plain(ext[...], w(1, 0)).astype(BF16)
    same_sum = None
    for block in range(*SAME):
        message = edge_forward(block, pres[3] + dot_rows(samehot[block - 5], gtab[...]), 1)
        same_sum = message if same_sum is None else same_sum + message
    mixed = node_forward(1, ext[H:H + B], same_sum.astype(BF16), pres[4])
    nact[3] = mixed

    table[...] = dot_plain(mixed, w(2, 0)).astype(BF16)
    down_sum = None
    for block in range(*DOWN):
        message = edge_forward(block, pres[2] + dot_rows(onehot[block], table[...]), 2)
        down_sum = message if down_sum is None else down_sum + message
    fine_out[...] = node_forward(2, fine[...], down_sum.astype(BF16), pres[1])
    dz2, dq2 = node_backward(2, cot[...].astype(F32) * (1.0 / math.sqrt(total_fine)), 1.0)
    g = dot_cols(dq2, w(2, 4))
    taken = back = None
    for block in range(*DOWN):
        dp, db2, db1 = edge_backward(block, g, 2)
        add_bias(8, db1)
        add_bias(9, db2)
        part = dot_plain(onehot[block], dp.astype(BF16))
        taken = dp if taken is None else taken + dp
        back = part if back is None else back + part
    state = sum_start(2, back)
    layer2a.put(1, dot_rows(fine[...], taken.astype(BF16)))
    layer2a.put(2, dot_rows(act[2:5].reshape(3 * B, B), dys[2:5].reshape(3 * B, B)))
    state = sum_middle(2, state)
    layer2b.put(0, dot_rows(fine[...], dq2))
    layer2b.put(1, dot_rows(node_in[2], dq2))
    layer2b.put(2, dot_rows(nact[2], dz2))
    sent_half = sum_end(2, state)
    grad_mixed = dot_cols(sent_half, w(2, 0))
    layer2a.put(0, 0.25 * dot_rows(nact[3], sent_half))
    step_on(layer2a, layer2b)

    dz1, dq1 = node_backward(1, grad_mixed, 0.25)
    pres[0] = grad_mixed + dot_cols(dq1, w(1, 3))
    g = dot_cols(dq1, w(1, 4))
    taken = back = None
    for block in range(*SAME):
        dp, db2, db1 = edge_backward(block, g, 1)
        add_bias(4, 0.25 * db1)
        add_bias(5, 0.25 * db2)
        part = dot_plain(samehot[block - 5], dp.astype(BF16))
        taken = dp if taken is None else taken + dp
        back = part if back is None else back + part
    hsend[2] = back[:H].astype(BF16)
    hsend[3] = back[H + B:].astype(BF16)
    returns = [
        post(hsend.at[2], hback.at[1], place.beside(-1)),
        post(hsend.at[3], hback.at[0], place.beside(1)),
    ]
    own = back[H:H + B]
    step_on(layer2a, layer2b)
    lifted = ext[H:H + B]
    taken_half = taken.astype(BF16)
    layer1.put(1, 1.0 * dot_rows(lifted, taken_half))
    layer1.put(2, dot_rows(act[5:11].reshape(6 * B, B), dys[5:11].reshape(6 * B, B)))
    layer1.put(3, dot_rows(lifted, dq1))
    layer1.put(4, dot_rows(node_in[1], dq1))
    layer1.put(5, dot_rows(nact[1], dz1))
    grad_lifted = pres[0] + dot_cols(taken_half, w(1, 1))
    for copy in returns:
        copy.wait_recv()
    own += dot_plain(onehot[5], hback[...].reshape(B, B))
    own_half = own.astype(BF16)
    grad_lifted += dot_cols(own_half, w(1, 0))
    lifted_cot[...] = grad_lifted * math.sqrt(total_fine)
    layer1.put(0, dot_rows(lifted, own_half))
    step_on(layer1)

    dz0, dq0 = node_backward(0, grad_lifted, 0.25)
    table[...] = dot_cols(dq0, w(0, 4)).astype(BF16)
    step_on(layer2a, layer2b)
    taken = back = None
    for block in range(*UP):
        dp, db2, db1 = edge_backward(block, dot_rows(onehot[block], table[...]), 0)
        add_bias(0, db1)
        add_bias(1, db2)
        part = dot_plain(onehot[block], dp.astype(BF16))
        taken = dp if taken is None else taken + dp
        back = part if back is None else back + part
    edge0[0].put(0, dot_rows(fine[...], taken.astype(BF16)))
    edge0[1].put(0, dot_rows(coarse[...], back.astype(BF16)))
    edge0[2].put(0, dot_rows(act[0:2].reshape(2 * B, B), dys[0:2].reshape(2 * B, B)))
    step_on(*edge0)
    bias_waits = [post(bias_acc, bias_core, place.partner())]
    node0.put(0, dot_rows(coarse[...], dq0))
    node0.put(1, dot_rows(node_in[0], dq0))
    node0.put(2, dot_rows(nact[0], dz0))
    step_on(node0)

    def bias_step(step):
        for copy in bias_waits:
            copy.wait_recv()
        bias_waits.clear()
        if step == 0:
            total = bias_acc[...] + bias_core[...]
        else:
            total = bias_slots[step - 1, 0] + bias_slots[step - 1, 1]
            total = total + bias_slots[step - 1, 2] + bias_slots[step - 1, 3]
        if step == 3:
            gbias[...] = total
            return
        axis = "yxz"[step]
        at = place.at(axis)
        bias_slots[step, at] = total
        for d in (1, 2, 3):
            spot = bias_slots.at[step, at]
            bias_waits.append(post(spot, spot, place.peer(axis, d)))

    for step in range(6):
        step_on(*edge0, node0, layer1, layer2a, layer2b)
        if step < 4:
            bias_step(step)
    assert all(group.step == 8 for group in groups)
    assert len(posted) <= COPIES
    for copy in posted:
        copy.wait_send()


def finish(fine_in, lifted_in, grads, gbias, fine_out, lifted_out, matrices_out, biases_out, wide, sems):
    copies = [
        pltpu.make_async_copy(fine_in, fine_out, sems.at[18]),
        pltpu.make_async_copy(lifted_in, lifted_out, sems.at[19]),
    ]
    for copy in copies:
        copy.start()
    for i in range(18):
        wide[i, :, :H] = grads[0, i].astype(F32)
        wide[i, :, H:] = grads[1, i].astype(F32)
        copies.append(pltpu.make_async_copy(wide.at[i], matrices_out.at[i // 6, i % 6], sems.at[i]))
        copies[-1].start()
    for layer in range(3):
        biases_out[layer] = gbias[4 * layer:4 * layer + 4, :]
    for copy in copies:
        copy.wait()


def group_scratch(kind, count):
    whole = 64 if kind == "same" else B
    spare = 16 if kind == "same" else B
    small = 64 if kind == "quick" else 16
    slots = 4 if kind == "quick" else 3
    return [
        pltpu.VMEM((2, count, B, H), BF16),
        pltpu.VMEM((count, whole, H), BF16),
        pltpu.VMEM((count, spare, H), BF16),
        pltpu.VMEM((3, count, spare // 4, H), BF16),
        pltpu.VMEM((count, 64, H), BF16),
        pltpu.VMEM((slots, count, small, H), BF16),
        pltpu.VMEM((count, small, H), BF16),
        pltpu.VMEM((4, count, small, H), BF16),
        pltpu.VMEM((count, small, H), BF16),
    ]


def local(fine_state, coarse_state, up_target, down_source, halo_lists, same_source, matrices, biases, fine_cotangent):
    total_fine = fine_state.shape[0] * lax.axis_size("gx") * lax.axis_size("gy")
    scratch = [
        pltpu.SemaphoreType.DMA((COPIES,)),
        pltpu.SemaphoreType.DMA((COPIES,)),
        pltpu.VMEM((6, B, B), BF16),
        pltpu.VMEM((6, 2 * B, B), BF16),
        pltpu.VMEM((11, B, B), BF16),
        pltpu.VMEM((11, B, B), BF16),
        pltpu.VMEM((11, B, B), BF16),
        pltpu.VMEM((11, B, 1), F32),
        pltpu.VMEM((11, B, B), BF16),
        pltpu.VMEM((4, B, B), BF16),
        pltpu.VMEM((3, B, B), BF16),
        pltpu.VMEM((3, B, B), BF16),
        pltpu.VMEM((3, B, 1), F32),
        pltpu.VMEM((B, B), BF16),
        pltpu.VMEM((2 * B, B), BF16),
        pltpu.VMEM((2 * B, B), BF16),
        pltpu.VMEM((5, B, B), F32),
        pltpu.VMEM((4, 2, H, B), BF16),
        pltpu.VMEM((4, 2, H, B), BF16),
        pltpu.VMEM((4, H, B), BF16),
        pltpu.VMEM((2, H, B), BF16),
        pltpu.VMEM((3, B, B), BF16),
        pltpu.VMEM((16, B), F32),
        pltpu.VMEM((16, B), F32),
        pltpu.VMEM((3, 4, 16, B), F32),
        pltpu.VMEM((16, H), jnp.int32),
        pltpu.VMEM((16, B), jnp.int32),
        pltpu.SemaphoreType.DMA((12,)),
        pltpu.VMEM((2, H, B), BF16),
        pltpu.VMEM((B, B), BF16),
        pltpu.VMEM((B, B), BF16),
        pltpu.VMEM((B, B), BF16),
        pltpu.VMEM((4, H), jnp.int32),
        pltpu.VMEM((6, H), jnp.int32),
        pltpu.VMEM((2, H), jnp.int32),
        pltpu.VMEM((12, H), jnp.int32),
        pltpu.VMEM((3, 6, B, B), BF16),
        pltpu.VMEM((3, 4, B), F32),
    ]
    for kind, _, first, end in GROUPS:
        scratch += group_scratch(kind, end - first)
    vmem = pl.BlockSpec(memory_space=pltpu.VMEM)

    def body(*refs):
        kernel(total_fine, *refs)

    fine_out, lifted, grads, gbias = pl.pallas_call(
        body,
        out_shape=(
            jax.ShapeDtypeStruct((B, B), BF16),
            jax.ShapeDtypeStruct((B, B), F32),
            jax.ShapeDtypeStruct((2, 18, B, H), BF16),
            jax.ShapeDtypeStruct((16, B), F32),
        ),
        in_specs=[pl.BlockSpec(memory_space=pltpu.HBM)] * 9,
        out_specs=(vmem,) * 4,
        scratch_shapes=scratch,
        compiler_params=pltpu.CompilerParams(
            collective_id=0, has_side_effects=True, vmem_limit_bytes=32 << 20
        ),
        name="sweep",
    )(*[
        pltpu.with_memory_space_constraint(value, pltpu.HBM)
        for value in (
            fine_state, coarse_state, fine_cotangent, up_target.reshape(4, H), down_source.reshape(6, H), halo_lists,
            same_source.reshape(12, H), matrices, biases,
        )
    ])
    hbm = pl.BlockSpec(memory_space=pl.ANY)
    return pl.pallas_call(
        finish,
        out_shape=(
            jax.ShapeDtypeStruct((B, B), BF16),
            jax.ShapeDtypeStruct((B, B), F32),
            jax.ShapeDtypeStruct((3, 6, B, B), F32),
            jax.ShapeDtypeStruct((3, 4, B), F32),
        ),
        in_specs=[vmem] * 4,
        out_specs=(hbm, hbm, hbm, vmem),
        scratch_shapes=[pltpu.VMEM((18, B, B), F32), pltpu.SemaphoreType.DMA((20,))],
        compiler_params=pltpu.CompilerParams(vmem_limit_bytes=16 << 20),
        name="finish",
    )(fine_out, lifted, grads, gbias)


def solution(mesh):
    in_specs = (
        P(("gx", "gy"), None),
        P("gy", None),
        P(("gx", "gy")),
        P(("gx", "gy")),
        P("gy", None),
        P("gy"),
        P(),
        P(),
        P(("gx", "gy"), None),
    )
    out_specs = (P(("gx", "gy"), None), P("gy", None), P(), P())
    return jax.shard_map(local, mesh=mesh, in_specs=in_specs, out_specs=out_specs, check_vma=False)
```

```python
import math

import jax
import jax.numpy as jnp
from jax import lax
from jax.experimental import pallas as pl
from jax.experimental.pallas import tpu as pltpu
from jax.sharding import PartitionSpec as P

MESH = pl.DeviceIdType.MESH
F32 = jnp.float32
BF16 = jnp.bfloat16
B = 256
H = 128
UP, DOWN, SAME = (0, 2), (2, 5), (5, 11)
COPIES = 160
PIECES = 4
GROUPS = (
    ("quick", ("x", "y", "z"), 0, 1),
    ("quick", ("z", "x", "y"), 1, 2),
    ("quick", ("y", "z", "x"), 2, 3),
    ("same", ("y", "x", "z"), 3, 6),
    ("same", ("y", "z", "x"), 6, 12),
    ("fine", ("x", "z", "y"), 12, 15),
    ("fine", ("z", "x", "y"), 15, 18),
)


def dot_plain(a, b):
    return jnp.dot(a, b, preferred_element_type=F32)


def dot_rows(a, b):
    return lax.dot_general(a, b, (((0,), (0,)), ((), ())), preferred_element_type=F32)


def dot_cols(a, b):
    return lax.dot_general(a, b, (((1,), (1,)), ((), ())), preferred_element_type=F32)


def silu_parts(x):
    gate = 0.5 * jnp.tanh(0.5 * x) + 0.5
    active = x * gate
    return active, gate + active * (1.0 - gate)


def row_mean(x):
    return jnp.mean(x, axis=-1, keepdims=True)


def normed(y):
    centred = y - row_mean(y)
    scale = lax.rsqrt(row_mean(centred * centred) + 1e-05)
    return centred * scale, scale


def norm_back(g, unit, scale):
    return scale * (g - row_mean(g) - unit * row_mean(g * unit))


def col_sum(x):
    return jnp.sum(x, axis=0, keepdims=True)


class Group:
    def __init__(self, post, place, axes, rows, shared, refs, out):
        self.shared = shared
        self.post, self.place, self.axes, self.rows, self.out = post, place, axes, rows, out
        self.g, self.rc, self.s1, self.r1, self.s2, self.r2, self.s3, self.r3, self.s4 = refs
        self.count = rows.stop - rows.start
        self.step = 0
        self.copies = []

    def put(self, i, value):
        half = value.astype(BF16)
        self.g[0, i] = half[:, :H]
        self.g[1, i] = half[:, H:]

    def landed(self):
        for copy in self.copies:
            copy.wait_recv()
        self.copies = []

    def advance(self):
        getattr(self, "step%d" % self.step)()
        self.step += 1

    def quarter(self):
        return pl.ds(pl.multiple_of(self.place.at(self.axes[0]) * 64, 64), 64)

    def step0(self):
        other = 1 - self.place.core
        src = self.g.at[other, :, self.quarter(), :] if self.shared else self.g.at[other]
        self.copies = [self.post(src, self.rc, self.place.partner())]

    def step1(self):
        self.landed()
        core = self.place.core
        if self.shared:
            for i in range(self.count):
                own = self.g[core, i, self.quarter(), :].astype(F32)
                self.s2[i] = (own + self.rc[i].astype(F32)).astype(BF16)
            self.scatter(self.axes[1], 16, self.s2, self.r2)
            self.step = 2
            return
        for i in range(self.count):
            self.s1[i] = (self.g[core, i].astype(F32) + self.rc[i].astype(F32)).astype(BF16)
        self.scatter(self.axes[0], 64, self.s1, self.r1)

    def scatter(self, axis, size, src, landing):
        at = self.place.at(axis)
        for d in (1, 2, 3):
            to = lax.rem(at + d, 4)
            rows = pl.ds(pl.multiple_of(to * size, size), size)
            self.copies.append(self.post(src.at[:, rows, :], landing.at[d - 1], self.place.peer(axis, d)))

    def gather_sum(self, axis, size, src, landing, out):
        at = self.place.at(axis)
        rows = pl.ds(pl.multiple_of(at * size, size), size)
        for i in range(self.count):
            total = src[i, rows, :].astype(F32)
            for d in range(3):
                total += landing[d, i].astype(F32)
            out[i] = total.astype(BF16)

    def step2(self):
        self.landed()
        self.gather_sum(self.axes[0], 64, self.s1, self.r1, self.s2)
        self.scatter(self.axes[1], 16, self.s2, self.r2)

    def step3(self):
        self.landed()
        self.gather_sum(self.axes[1], 16, self.s2, self.r2, self.s3)
        self.share(self.axes[2], self.s3, self.r3)

    def share(self, axis, src, slots):
        at = self.place.at(axis)
        for d in (1, 2, 3):
            self.copies.append(self.post(src, slots.at[at], self.place.peer(axis, d)))
        slots[at] = src[...]

    def slot_sum(self, slots, out):
        for i in range(self.count):
            total = slots[0, i].astype(F32)
            for j in (1, 2, 3):
                total += slots[j, i].astype(F32)
            out[i] = total.astype(BF16)

    def step4(self):
        self.landed()
        self.slot_sum(self.r3, self.s4)
        start = self.place.at(self.axes[0]) * 64 + self.place.at(self.axes[1]) * 16
        rows = pl.ds(pl.multiple_of(start, 16), 16)
        spot = self.out.at[self.place.core, self.rows, rows, :]
        for d in (1, 2, 3):
            self.copies.append(self.post(self.s4, spot, self.place.peer(self.axes[1], d)))
        for i in range(self.count):
            self.out[self.place.core, self.rows.start + i, rows, :] = self.s4[i]

    def step5(self):
        self.landed()
        spot = self.out.at[self.place.core, self.rows, self.quarter(), :]
        for d in (1, 2, 3):
            self.copies.append(self.post(spot, spot, self.place.peer(self.axes[0], d)))

    def step6(self):
        self.landed()
        spot = self.out.at[self.place.core, self.rows, :, :]
        self.copies = [self.post(spot, spot, self.place.partner())]

    def step7(self):
        self.landed()


class Quick(Group):
    def step2(self):
        self.landed()
        self.gather_sum(self.axes[0], 64, self.s1, self.r1, self.s2)
        self.share(self.axes[1], self.s2, self.r2)

    def step3(self):
        self.landed()
        self.slot_sum(self.r2, self.s3)
        self.share(self.axes[2], self.s3, self.r3)

    def step4(self):
        self.landed()
        self.slot_sum(self.r3, self.s4)
        spot = self.out.at[self.place.core, self.rows, self.quarter(), :]
        for d in (1, 2, 3):
            self.copies.append(self.post(self.s4, spot, self.place.peer(self.axes[0], d)))
        for i in range(self.count):
            self.out[self.place.core, self.rows.start + i, self.quarter(), :] = self.s4[i]
        self.step = 5


class Place:
    def __init__(self):
        self.gx = lax.axis_index("gx")
        self.gy = lax.axis_index("gy")
        self.core = lax.rem(self.gy, 2)
        self.x = lax.rem(self.gy // 2, 4)
        self.z = self.gy // 8

    def at(self, axis):
        return {"x": self.x, "y": self.gx, "z": self.z}[axis]

    def partner(self):
        return (self.gx, self.gy + 1 - 2 * self.core)

    def peer(self, axis, d):
        if axis == "y":
            return (lax.rem(self.gx + d, 4), self.gy)
        if axis == "x":
            return (self.gx, self.z * 8 + lax.rem(self.x + d, 4) * 2 + self.core)
        return (self.gx, lax.rem(self.z + d, 4) * 8 + self.x * 2 + self.core)

    def beside(self, d):
        return (self.gx, lax.rem(self.gy + d + 32, 32))


def deal(source, raw, index, first, end):
    ways = end - first
    raw[:2 * ways, :] = source[...]
    rows = raw[...]
    lane = lax.broadcasted_iota(jnp.int32, rows.shape, 1)
    for k in range(ways):
        place = lane * ways + k
        picked = jnp.take_along_axis(rows, lax.rem(place, H), axis=1, mode="promise_in_bounds")
        line = place[0:1] // H
        for half in (0, 1):
            row = picked[ways * half:ways * half + 1]
            for i in range(1, ways):
                row = jnp.where(line == i, picked[ways * half + i:ways * half + i + 1], row)
            index[first + k:first + k + 1, half * H:half * H + H] = row


def kernel(total_fine, *refs):
    inputs, (fine_out, lifted_cot, grads, gbias) = refs[:9], refs[9:13]
    (send_sems, recv_sems, onehot, samehot, act, slope, unit, scale, dys, nact, nslope, nunit, nscale,
     table, ext, gtab, pres, csend, crecv, hsend, hback, node_in, bias_acc, bias_core, bias_slots, raw, index, load_sems, summed, own_part,
     fine, coarse, cot, up_raw, down_raw, halo_raw, same_raw, mats, bias) = refs[13:52]
    group_refs = refs[52:]
    place = Place()
    posted = []

    def post(src, dst, device):
        i = len(posted)
        copy = pltpu.make_async_remote_copy(
            src_ref=src, dst_ref=dst, send_sem=send_sems.at[i], recv_sem=recv_sems.at[i],
            device_id=device, device_id_type=MESH,
        )
        copy.start()
        posted.append(copy)
        return copy

    loads = []
    for i, (src, dst) in enumerate([
        (inputs[3], up_raw), (inputs[0], fine), (inputs[1], coarse), (inputs[8], bias),
        (inputs[7].at[0, 0:3], mats.at[0, 0:3]), (inputs[4], down_raw), (inputs[6], same_raw), (inputs[5], halo_raw),
        (inputs[7].at[0, 3:6], mats.at[0, 3:6]), (inputs[7].at[2], mats.at[2]), (inputs[7].at[1], mats.at[1]),
        (inputs[2], cot),
    ]):
        loads.append(pltpu.make_async_copy(src, dst, load_sems.at[i]))
    for load in loads[:5]:
        load.start()

    barrier = pltpu.get_barrier_semaphore()
    near = [place.peer(a, d) for a in ("x", "y", "z") for d in (1, 2, 3)]
    near += [place.partner(), place.beside(1), place.beside(-1)]
    for device in near:
        pl.semaphore_signal(barrier, inc=1, device_id=device, device_id_type=MESH)
    for load in loads[5:]:
        load.start()

    groups = [
        (Quick if kind == "quick" else Group)(
            post, place, axes, slice(first, end), kind == "same", group_refs[9 * at:9 * at + 9], grads
        )
        for at, (kind, axes, first, end) in enumerate(GROUPS)
    ]
    edge0, (node0, layer1, layer2a, layer2b) = groups[:3], groups[3:]

    bias_acc[...] = jnp.zeros_like(bias_acc)
    loads[0].wait()
    deal(up_raw, raw, index, *UP)

    def step_on(*groups):
        for group in groups:
            if group.step < 8:
                group.advance()

    def add_bias(row, value):
        bias_acc[row:row + 1, :] += value

    def w(layer, i):
        return mats[layer, i]

    def b(layer, i):
        return bias[layer, i:i + 1, :]

    def hot_rows(block, size):
        nodes = lax.broadcasted_iota(jnp.int32, (size, B), 0)
        return jnp.where(nodes == index[block:block + 1, :], 1.0, 0.0).astype(BF16)

    def edge_forward(block, pre, layer):
        active, slope_now = silu_parts(pre)
        half = active.astype(BF16)
        act[block] = half
        slope[block] = slope_now.astype(BF16)
        message, scale_now = normed(dot_plain(half, w(layer, 2)) + b(layer, 1))
        unit[block] = message.astype(BF16)
        scale[block] = scale_now
        return message

    def edge_backward(block, g, layer):
        dy = norm_back(g, unit[block].astype(F32), scale[block])
        half = dy.astype(BF16)
        dys[block] = half
        dp = slope[block].astype(F32) * dot_cols(half, w(layer, 2))
        return dp, col_sum(dy), col_sum(dp)

    def node_forward(layer, state, agg, pre):
        node_in[layer] = agg
        active, slope_now = silu_parts(pre + dot_plain(agg, w(layer, 4)))
        half = active.astype(BF16)
        nact[layer] = half
        nslope[layer] = slope_now.astype(BF16)
        unit_now, scale_now = normed(dot_plain(half, w(layer, 5)) + b(layer, 3))
        nunit[layer] = unit_now.astype(BF16)
        nscale[layer] = scale_now
        return (state.astype(F32) + unit_now).astype(BF16)

    def node_backward(layer, g, share):
        dz = norm_back(g, nunit[layer].astype(F32), nscale[layer])
        dz16 = dz.astype(BF16)
        dq = nslope[layer].astype(F32) * dot_cols(dz16, w(layer, 5))
        dq16 = dq.astype(BF16)
        add_bias(4 * layer + 3, share * col_sum(dz))
        add_bias(4 * layer + 2, share * col_sum(dq))
        return dz16, dq16

    def piece(i):
        return pl.ds(i * (H // PIECES), H // PIECES)

    def sum_start(first, value):
        half = value.astype(BF16)
        csend[first, 0] = half[:H]
        csend[first, 1] = half[H:]
        odd = lax.rem(place.gx, 2)
        one = (place.gx + 1 - 2 * odd, place.gy)
        two = (lax.rem(place.gx + 2 * odd + 3, 4), place.gy)
        waits = []
        for i in range(PIECES):
            for side, device in ((0, one), (1, two)):
                waits.append(post(csend.at[first, side, piece(i)], crecv.at[first, side, piece(i)], device))
        return waits, one, two

    def sum_pieces(at, waits, out, then):
        for i in range(PIECES):
            for side in (0, 1):
                waits[2 * i + side].wait_recv()
                both = csend[at, side, piece(i)].astype(F32) + crecv[at, side, piece(i)].astype(F32)
                out[side, piece(i)] = both.astype(BF16)
                then(i, side)

    def sum_middle(first, state):
        waits, one, two = state
        later = []

        def send_on(i, side):
            device = (two, one)[side]
            later.append(post(csend.at[first + 1, side, piece(i)], crecv.at[first + 1, side, piece(i)], device))

        sum_pieces(first, waits, csend.at[first + 1], send_on)
        return later

    def sum_end(first, waits):
        sum_pieces(first + 1, waits, summed, lambda i, side: None)
        return summed[...].reshape(B, B)

    for block in range(*UP):
        onehot[block] = hot_rows(block, B)
    for load in loads[1:5]:
        load.wait()
    sent = dot_plain(fine[...], w(0, 0)) + b(0, 0)
    table[...] = dot_plain(coarse[...], w(0, 1)).astype(BF16)
    up_sum = None
    for block in range(*UP):
        message = edge_forward(block, sent + dot_rows(onehot[block], table[...]), 0)
        part = dot_plain(onehot[block], message.astype(BF16))
        up_sum = part if up_sum is None else up_sum + part

    pl.semaphore_wait(barrier, len(near))
    state = sum_start(0, up_sum)
    for load in loads[5:]:
        load.wait()
    pres[0] = dot_plain(coarse[...], w(0, 3)) + b(0, 2)
    deal(down_raw, raw, index, *DOWN)
    deal(same_raw, raw, index, *SAME)
    place_in = index[SAME[0]:SAME[1], :]
    moved = jnp.where(place_in < H, place_in + B, place_in - H)
    index[SAME[0]:SAME[1], :] = jnp.where(place_in < H + B, moved, place_in)
    index[11:12, :H] = halo_raw[0:1, :]
    index[11:12, H:] = halo_raw[1:2, :]
    for block in range(*DOWN):
        onehot[block] = hot_rows(block, B)
    onehot[5] = hot_rows(11, B)
    state = sum_middle(0, state)
    for block in range(*SAME):
        samehot[block - 5] = hot_rows(block, 2 * B)
    pres[1] = dot_plain(fine[...], w(2, 3)) + b(2, 2)
    pres[2] = dot_plain(fine[...], w(2, 1)) + b(2, 0)
    agg = sum_end(0, state)
    lifted = node_forward(0, coarse[...], agg, pres[0])
    ext[:B] = lifted
    payload = dot_rows(onehot[5], lifted).astype(BF16)
    hsend[0] = payload[:H]
    hsend[1] = payload[H:]
    halo = [
        post(hsend.at[0], ext.at[B + H:], place.beside(-1)),
        post(hsend.at[1], ext.at[B:B + H], place.beside(1)),
    ]

    pres[3] = dot_plain(lifted, w(1, 1)) + b(1, 0)
    gtab[:B] = dot_plain(lifted, w(1, 0)).astype(BF16)
    for block in range(*SAME):
        own_part[block - 5] = pres[3] + dot_rows(samehot[block - 5, :B], gtab[:B])
    pres[4] = dot_plain(lifted, w(1, 3)) + b(1, 2)
    for copy in halo:
        copy.wait_recv()
    gtab[B:] = dot_plain(ext[B:], w(1, 0)).astype(BF16)
    same_sum = None
    for block in range(*SAME):
        message = edge_forward(
            block, own_part[block - 5] + dot_rows(samehot[block - 5, B:], gtab[B:]), 1
        )
        same_sum = message if same_sum is None else same_sum + message
    mixed = node_forward(1, ext[:B], same_sum.astype(BF16), pres[4])
    nact[3] = mixed

    table[...] = dot_plain(mixed, w(2, 0)).astype(BF16)
    down_sum = None
    for block in range(*DOWN):
        message = edge_forward(block, pres[2] + dot_rows(onehot[block], table[...]), 2)
        down_sum = message if down_sum is None else down_sum + message
    fine_out[...] = node_forward(2, fine[...], down_sum.astype(BF16), pres[1])
    dz2, dq2 = node_backward(2, cot[...].astype(F32) * (1.0 / math.sqrt(total_fine)), 1.0)
    g = dot_cols(dq2, w(2, 4))
    taken = back = None
    for block in range(*DOWN):
        dp, db2, db1 = edge_backward(block, g, 2)
        add_bias(8, db1)
        add_bias(9, db2)
        part = dot_plain(onehot[block], dp.astype(BF16))
        taken = dp if taken is None else taken + dp
        back = part if back is None else back + part
    state = sum_start(2, back)
    layer2a.put(1, dot_rows(fine[...], taken.astype(BF16)))
    layer2a.put(2, dot_rows(act[2:5].reshape(3 * B, B), dys[2:5].reshape(3 * B, B)))
    state = sum_middle(2, state)
    layer2b.put(0, dot_rows(fine[...], dq2))
    layer2b.put(1, dot_rows(node_in[2], dq2))
    layer2b.put(2, dot_rows(nact[2], dz2))
    sent_half = sum_end(2, state)
    grad_mixed = dot_cols(sent_half, w(2, 0))
    layer2a.put(0, 0.25 * dot_rows(nact[3], sent_half))
    step_on(layer2a, layer2b)

    dz1, dq1 = node_backward(1, grad_mixed, 0.25)
    pres[0] = grad_mixed + dot_cols(dq1, w(1, 3))
    g = dot_cols(dq1, w(1, 4))
    taken = back = None
    for block in range(*SAME):
        dp, db2, db1 = edge_backward(block, g, 1)
        add_bias(4, 0.25 * db1)
        add_bias(5, 0.25 * db2)
        part = dot_plain(samehot[block - 5], dp.astype(BF16))
        taken = dp if taken is None else taken + dp
        back = part if back is None else back + part
    hsend[2] = back[B:B + H].astype(BF16)
    hsend[3] = back[B + H:].astype(BF16)
    returns = [
        post(hsend.at[2], hback.at[1], place.beside(-1)),
        post(hsend.at[3], hback.at[0], place.beside(1)),
    ]
    own = back[:B]
    step_on(layer2a, layer2b)
    lifted = ext[:B]
    taken_half = taken.astype(BF16)
    layer1.put(1, 1.0 * dot_rows(lifted, taken_half))
    layer1.put(2, dot_rows(act[5:11].reshape(6 * B, B), dys[5:11].reshape(6 * B, B)))
    layer1.put(3, dot_rows(lifted, dq1))
    layer1.put(4, dot_rows(node_in[1], dq1))
    layer1.put(5, dot_rows(nact[1], dz1))
    grad_lifted = pres[0] + dot_cols(taken_half, w(1, 1))
    for copy in returns:
        copy.wait_recv()
    own += dot_plain(onehot[5], hback[...].reshape(B, B))
    own_half = own.astype(BF16)
    grad_lifted += dot_cols(own_half, w(1, 0))
    lifted_cot[...] = grad_lifted * math.sqrt(total_fine)
    layer1.put(0, dot_rows(lifted, own_half))
    step_on(layer1)

    dz0, dq0 = node_backward(0, grad_lifted, 0.25)
    table[...] = dot_cols(dq0, w(0, 4)).astype(BF16)
    taken = back = None
    for block in range(*UP):
        if block == UP[1] - 1:
            step_on(layer2a, layer2b, layer1)
        dp, db2, db1 = edge_backward(block, dot_rows(onehot[block], table[...]), 0)
        add_bias(0, db1)
        add_bias(1, db2)
        part = dot_plain(onehot[block], dp.astype(BF16))
        taken = dp if taken is None else taken + dp
        back = part if back is None else back + part
    edge0[0].put(0, dot_rows(fine[...], taken.astype(BF16)))
    edge0[1].put(0, dot_rows(coarse[...], back.astype(BF16)))
    edge0[2].put(0, dot_rows(act[0:2].reshape(2 * B, B), dys[0:2].reshape(2 * B, B)))
    step_on(*edge0)
    bias_waits = [post(bias_acc, bias_core, place.partner())]
    node0.put(0, dot_rows(coarse[...], dq0))
    node0.put(1, dot_rows(node_in[0], dq0))
    node0.put(2, dot_rows(nact[0], dz0))
    step_on(node0)

    retired, marks = [0], [0]

    def retire():
        for copy in posted[retired[0]:marks[-1]]:
            copy.wait_send()
        retired[0] = marks[-1]
        marks.append(len(posted))

    def bias_step(step):
        for copy in bias_waits:
            copy.wait_recv()
        bias_waits.clear()
        if step == 0:
            total = bias_acc[...] + bias_core[...]
        else:
            total = bias_slots[step - 1, 0] + bias_slots[step - 1, 1]
            total = total + bias_slots[step - 1, 2] + bias_slots[step - 1, 3]
        if step == 3:
            gbias[...] = total
            return
        axis = "yxz"[step]
        at = place.at(axis)
        bias_slots[step, at] = total
        for d in (1, 2, 3):
            spot = bias_slots.at[step, at]
            bias_waits.append(post(spot, spot, place.peer(axis, d)))

    for step in range(6):
        step_on(*edge0, node0, layer1, layer2a, layer2b)
        if step < 4:
            bias_step(step)
        retire()
    assert all(group.step == 8 for group in groups)
    assert len(posted) <= COPIES
    retire()
    retire()
    assert retired[0] == len(posted)


def finish(fine_in, lifted_in, grads, gbias, fine_out, lifted_out, matrices_out, biases_out, wide, sems):
    copies = [
        pltpu.make_async_copy(fine_in, fine_out, sems.at[18]),
        pltpu.make_async_copy(lifted_in, lifted_out, sems.at[19]),
    ]
    for copy in copies:
        copy.start()
    for i in range(18):
        wide[i, :, :H] = grads[0, i].astype(F32)
        wide[i, :, H:] = grads[1, i].astype(F32)
        copies.append(pltpu.make_async_copy(wide.at[i], matrices_out.at[i // 6, i % 6], sems.at[i]))
        copies[-1].start()
    for layer in range(3):
        biases_out[layer] = gbias[4 * layer:4 * layer + 4, :]
    for copy in copies:
        copy.wait()


def group_scratch(kind, count):
    whole = 64 if kind == "same" else B
    spare = 16 if kind == "same" else B
    small = 64 if kind == "quick" else 16
    slots = 4 if kind == "quick" else 3
    return [
        pltpu.VMEM((2, count, B, H), BF16),
        pltpu.VMEM((count, whole, H), BF16),
        pltpu.VMEM((count, spare, H), BF16),
        pltpu.VMEM((3, count, spare // 4, H), BF16),
        pltpu.VMEM((count, 64, H), BF16),
        pltpu.VMEM((slots, count, small, H), BF16),
        pltpu.VMEM((count, small, H), BF16),
        pltpu.VMEM((4, count, small, H), BF16),
        pltpu.VMEM((count, small, H), BF16),
    ]


def local(fine_state, coarse_state, up_target, down_source, halo_lists, same_source, matrices, biases, fine_cotangent):
    total_fine = fine_state.shape[0] * lax.axis_size("gx") * lax.axis_size("gy")
    scratch = [
        pltpu.SemaphoreType.DMA((COPIES,)),
        pltpu.SemaphoreType.DMA((COPIES,)),
        pltpu.VMEM((6, B, B), BF16),
        pltpu.VMEM((6, 2 * B, B), BF16),
        pltpu.VMEM((11, B, B), BF16),
        pltpu.VMEM((11, B, B), BF16),
        pltpu.VMEM((11, B, B), BF16),
        pltpu.VMEM((11, B, 1), F32),
        pltpu.VMEM((11, B, B), BF16),
        pltpu.VMEM((4, B, B), BF16),
        pltpu.VMEM((3, B, B), BF16),
        pltpu.VMEM((3, B, B), BF16),
        pltpu.VMEM((3, B, 1), F32),
        pltpu.VMEM((B, B), BF16),
        pltpu.VMEM((2 * B, B), BF16),
        pltpu.VMEM((2 * B, B), BF16),
        pltpu.VMEM((5, B, B), F32),
        pltpu.VMEM((4, 2, H, B), BF16),
        pltpu.VMEM((4, 2, H, B), BF16),
        pltpu.VMEM((4, H, B), BF16),
        pltpu.VMEM((2, H, B), BF16),
        pltpu.VMEM((3, B, B), BF16),
        pltpu.VMEM((16, B), F32),
        pltpu.VMEM((16, B), F32),
        pltpu.VMEM((3, 4, 16, B), F32),
        pltpu.VMEM((16, H), jnp.int32),
        pltpu.VMEM((16, B), jnp.int32),
        pltpu.SemaphoreType.DMA((12,)),
        pltpu.VMEM((2, H, B), BF16),
        pltpu.VMEM((6, B, B), F32),
        pltpu.VMEM((B, B), BF16),
        pltpu.VMEM((B, B), BF16),
        pltpu.VMEM((B, B), BF16),
        pltpu.VMEM((4, H), jnp.int32),
        pltpu.VMEM((6, H), jnp.int32),
        pltpu.VMEM((2, H), jnp.int32),
        pltpu.VMEM((12, H), jnp.int32),
        pltpu.VMEM((3, 6, B, B), BF16),
        pltpu.VMEM((3, 4, B), F32),
    ]
    for kind, _, first, end in GROUPS:
        scratch += group_scratch(kind, end - first)
    vmem = pl.BlockSpec(memory_space=pltpu.VMEM)

    def body(*refs):
        kernel(total_fine, *refs)

    fine_out, lifted, grads, gbias = pl.pallas_call(
        body,
        out_shape=(
            jax.ShapeDtypeStruct((B, B), BF16),
            jax.ShapeDtypeStruct((B, B), F32),
            jax.ShapeDtypeStruct((2, 18, B, H), BF16),
            jax.ShapeDtypeStruct((16, B), F32),
        ),
        in_specs=[pl.BlockSpec(memory_space=pltpu.HBM)] * 9,
        out_specs=(vmem,) * 4,
        scratch_shapes=scratch,
        compiler_params=pltpu.CompilerParams(
            collective_id=0, has_side_effects=True, vmem_limit_bytes=32 << 20
        ),
        name="sweep",
    )(*[
        pltpu.with_memory_space_constraint(value, pltpu.HBM)
        for value in (
            fine_state, coarse_state, fine_cotangent, up_target.reshape(4, H), down_source.reshape(6, H), halo_lists,
            same_source.reshape(12, H), matrices, biases,
        )
    ])
    hbm = pl.BlockSpec(memory_space=pl.ANY)
    return pl.pallas_call(
        finish,
        out_shape=(
            jax.ShapeDtypeStruct((B, B), BF16),
            jax.ShapeDtypeStruct((B, B), F32),
            jax.ShapeDtypeStruct((3, 6, B, B), F32),
            jax.ShapeDtypeStruct((3, 4, B), F32),
        ),
        in_specs=[vmem] * 4,
        out_specs=(hbm, hbm, hbm, vmem),
        scratch_shapes=[pltpu.VMEM((18, B, B), F32), pltpu.SemaphoreType.DMA((20,))],
        compiler_params=pltpu.CompilerParams(vmem_limit_bytes=16 << 20),
        name="finish",
    )(fine_out, lifted, grads, gbias)


def solution(mesh):
    in_specs = (
        P(("gx", "gy"), None),
        P("gy", None),
        P(("gx", "gy")),
        P(("gx", "gy")),
        P("gy", None),
        P("gy"),
        P(),
        P(),
        P(("gx", "gy"), None),
    )
    out_specs = (P(("gx", "gy"), None), P("gy", None), P(), P())
    return jax.shard_map(local, mesh=mesh, in_specs=in_specs, out_specs=out_specs, check_vma=False)
```

```python
import math

import jax
import jax.numpy as jnp
from jax import lax
from jax.experimental import pallas as pl
from jax.experimental.pallas import tpu as pltpu
from jax.sharding import PartitionSpec as P

MESH = pl.DeviceIdType.MESH
F32 = jnp.float32
BF16 = jnp.bfloat16
B = 256
H = 128
UP, DOWN, SAME = (0, 2), (2, 5), (5, 11)
BATCHES = 58
SENDS = 3
UNIT = 4096
RULER = 512
PIECES = 2
GROUPS = (
    ("quick", ("x", "y", "z"), 0, 1),
    ("quick", ("z", "x", "y"), 1, 2),
    ("quick", ("y", "z", "x"), 2, 3),
    ("same", ("y", "x", "z"), 3, 6),
    ("same", ("y", "z", "x"), 6, 12),
    ("fine", ("x", "z", "y"), 12, 15),
    ("fine", ("z", "x", "y"), 15, 18),
)


def dot_plain(a, b):
    return jnp.dot(a, b, preferred_element_type=F32)


def dot_rows(a, b):
    return lax.dot_general(a, b, (((0,), (0,)), ((), ())), preferred_element_type=F32)


def dot_cols(a, b):
    return lax.dot_general(a, b, (((1,), (1,)), ((), ())), preferred_element_type=F32)


def silu_parts(x):
    gate = 0.5 * jnp.tanh(0.5 * x) + 0.5
    active = x * gate
    return active, gate + active * (1.0 - gate)


def row_mean(x):
    return jnp.mean(x, axis=-1, keepdims=True)


def normed(y):
    centred = y - row_mean(y)
    scale = lax.rsqrt(row_mean(centred * centred) + 1e-05)
    return centred * scale, scale


def norm_back(g, unit, scale):
    return scale * (g - row_mean(g) - unit * row_mean(g * unit))


def col_sum(x):
    return jnp.sum(x, axis=0, keepdims=True)


class Batch:
    def __init__(self, sem, ruler):
        self.sem, self.ruler, self.size = sem, ruler, 0

    def wait(self):
        span = self.ruler.at[:self.size // UNIT]
        pltpu.make_async_copy(span, span, self.sem).wait()


class Group:
    def __init__(self, post, place, axes, rows, shared, refs, out):
        self.shared = shared
        self.post, self.place, self.axes, self.rows, self.out = post, place, axes, rows, out
        self.g, self.rc, self.s1, self.r1, self.s2, self.r2, self.s3, self.r3, self.s4 = refs
        self.count = rows.stop - rows.start
        self.step = 0
        self.batch = None

    def put(self, i, value):
        half = value.astype(BF16)
        self.g[0, i] = half[:, :H]
        self.g[1, i] = half[:, H:]

    def send(self, src, dst, device):
        self.batch = self.post(src, dst, device, self.batch)

    def landed(self):
        self.batch.wait()
        self.batch = None

    def advance(self):
        getattr(self, "step%d" % self.step)()
        self.step += 1

    def quarter(self):
        return pl.ds(pl.multiple_of(self.place.at(self.axes[0]) * 64, 64), 64)

    def step0(self):
        other = 1 - self.place.core
        src = self.g.at[other, :, self.quarter(), :] if self.shared else self.g.at[other]
        self.send(src, self.rc, self.place.partner())

    def step1(self):
        self.landed()
        core = self.place.core
        if self.shared:
            for i in range(self.count):
                own = self.g[core, i, self.quarter(), :].astype(F32)
                self.s2[i] = (own + self.rc[i].astype(F32)).astype(BF16)
            self.scatter(self.axes[1], 16, self.s2, self.r2)
            self.step = 2
            return
        for i in range(self.count):
            self.s1[i] = (self.g[core, i].astype(F32) + self.rc[i].astype(F32)).astype(BF16)
        self.scatter(self.axes[0], 64, self.s1, self.r1)

    def scatter(self, axis, size, src, landing):
        at = self.place.at(axis)
        for d in (1, 2, 3):
            to = lax.rem(at + d, 4)
            rows = pl.ds(pl.multiple_of(to * size, size), size)
            self.send(src.at[:, rows, :], landing.at[d - 1], self.place.peer(axis, d))

    def gather_sum(self, axis, size, src, landing, out):
        at = self.place.at(axis)
        rows = pl.ds(pl.multiple_of(at * size, size), size)
        for i in range(self.count):
            total = src[i, rows, :].astype(F32)
            for d in range(3):
                total += landing[d, i].astype(F32)
            out[i] = total.astype(BF16)

    def step2(self):
        self.landed()
        self.gather_sum(self.axes[0], 64, self.s1, self.r1, self.s2)
        self.scatter(self.axes[1], 16, self.s2, self.r2)

    def step3(self):
        self.landed()
        self.gather_sum(self.axes[1], 16, self.s2, self.r2, self.s3)
        self.share(self.axes[2], self.s3, self.r3)

    def share(self, axis, src, slots):
        at = self.place.at(axis)
        for d in (1, 2, 3):
            self.send(src, slots.at[at], self.place.peer(axis, d))
        slots[at] = src[...]

    def slot_sum(self, slots, out):
        for i in range(self.count):
            total = slots[0, i].astype(F32)
            for j in (1, 2, 3):
                total += slots[j, i].astype(F32)
            out[i] = total.astype(BF16)

    def step4(self):
        self.landed()
        self.slot_sum(self.r3, self.s4)
        start = self.place.at(self.axes[0]) * 64 + self.place.at(self.axes[1]) * 16
        rows = pl.ds(pl.multiple_of(start, 16), 16)
        spot = self.out.at[self.place.core, self.rows, rows, :]
        for d in (1, 2, 3):
            self.send(self.s4, spot, self.place.peer(self.axes[1], d))
        for i in range(self.count):
            self.out[self.place.core, self.rows.start + i, rows, :] = self.s4[i]

    def step5(self):
        self.landed()
        spot = self.out.at[self.place.core, self.rows, self.quarter(), :]
        for d in (1, 2, 3):
            self.send(spot, spot, self.place.peer(self.axes[0], d))

    def step6(self):
        self.landed()
        spot = self.out.at[self.place.core, self.rows, :, :]
        self.send(spot, spot, self.place.partner())

    def step7(self):
        self.landed()


class Quick(Group):
    def step2(self):
        self.landed()
        self.gather_sum(self.axes[0], 64, self.s1, self.r1, self.s2)
        self.share(self.axes[1], self.s2, self.r2)

    def step3(self):
        self.landed()
        self.slot_sum(self.r2, self.s3)
        self.share(self.axes[2], self.s3, self.r3)

    def step4(self):
        self.landed()
        self.slot_sum(self.r3, self.s4)
        spot = self.out.at[self.place.core, self.rows, self.quarter(), :]
        for d in (1, 2, 3):
            self.send(self.s4, spot, self.place.peer(self.axes[0], d))
        for i in range(self.count):
            self.out[self.place.core, self.rows.start + i, self.quarter(), :] = self.s4[i]
        self.step = 5


class Place:
    def __init__(self):
        self.gx = lax.axis_index("gx")
        self.gy = lax.axis_index("gy")
        self.core = lax.rem(self.gy, 2)
        self.x = lax.rem(self.gy // 2, 4)
        self.z = self.gy // 8

    def at(self, axis):
        return {"x": self.x, "y": self.gx, "z": self.z}[axis]

    def partner(self):
        return (self.gx, self.gy + 1 - 2 * self.core)

    def peer(self, axis, d):
        if axis == "y":
            return (lax.rem(self.gx + d, 4), self.gy)
        if axis == "x":
            return (self.gx, self.z * 8 + lax.rem(self.x + d, 4) * 2 + self.core)
        return (self.gx, lax.rem(self.z + d, 4) * 8 + self.x * 2 + self.core)

    def beside(self, d):
        return (self.gx, lax.rem(self.gy + d + 32, 32))


def deal(source, raw, index, first, end):
    ways = end - first
    raw[:2 * ways, :] = source[...]
    rows = raw[...]
    lane = lax.broadcasted_iota(jnp.int32, rows.shape, 1)
    for k in range(ways):
        place = lane * ways + k
        picked = jnp.take_along_axis(rows, lax.rem(place, H), axis=1, mode="promise_in_bounds")
        line = place[0:1] // H
        for half in (0, 1):
            row = picked[ways * half:ways * half + 1]
            for i in range(1, ways):
                row = jnp.where(line == i, picked[ways * half + i:ways * half + i + 1], row)
            index[first + k:first + k + 1, half * H:half * H + H] = row


def kernel(total_fine, *refs):
    inputs, (fine_out, lifted_cot, grads, gbias) = refs[:9], refs[9:13]
    (send_sems, recv_sems, onehot, samehot, act, slope, unit, scale, dys, nact, nslope, nunit, nscale,
     table, ext, gtab, pres, csend, crecv, hsend, hback, node_in, bias_acc, bias_core, bias_slots, raw, index, load_sems, summed, own_part, ruler,
     fine, coarse, cot, up_raw, down_raw, halo_raw, same_raw, mats, bias) = refs[13:53]
    group_refs = refs[53:]
    place = Place()
    batches = []
    leaving = []

    def next_sends():
        leaving.append(Batch(send_sems.at[len(leaving)], ruler))

    def post(src, dst, device, batch=None):
        if batch is None:
            batch = Batch(recv_sems.at[len(batches)], ruler)
            batches.append(batch)
        pltpu.make_async_remote_copy(
            src_ref=src, dst_ref=dst, send_sem=leaving[-1].sem, recv_sem=batch.sem,
            device_id=device, device_id_type=MESH,
        ).start()
        size = math.prod(dst.shape) * dst.dtype.itemsize
        assert size % UNIT == 0
        batch.size += size
        leaving[-1].size += size
        return batch

    next_sends()
    loads = []
    for i, (src, dst) in enumerate([
        (inputs[3], up_raw), (inputs[0], fine), (inputs[1], coarse), (inputs[8], bias),
        (inputs[7].at[0, 0:3], mats.at[0, 0:3]), (inputs[4], down_raw), (inputs[6], same_raw), (inputs[5], halo_raw),
        (inputs[7].at[0, 3:6], mats.at[0, 3:6]), (inputs[7].at[2], mats.at[2]), (inputs[7].at[1], mats.at[1]),
        (inputs[2], cot),
    ]):
        loads.append(pltpu.make_async_copy(src, dst, load_sems.at[i]))
    for load in loads[:5]:
        load.start()

    barrier = pltpu.get_barrier_semaphore()
    near = [place.peer(a, d) for a in ("x", "y", "z") for d in (1, 2, 3)]
    near += [place.partner(), place.beside(1), place.beside(-1)]
    for device in near:
        pl.semaphore_signal(barrier, inc=1, device_id=device, device_id_type=MESH)
    for load in loads[5:]:
        load.start()

    groups = [
        (Quick if kind == "quick" else Group)(
            post, place, axes, slice(first, end), kind == "same", group_refs[9 * at:9 * at + 9], grads
        )
        for at, (kind, axes, first, end) in enumerate(GROUPS)
    ]
    edge0, (node0, layer1, layer2a, layer2b) = groups[:3], groups[3:]

    bias_acc[...] = jnp.zeros_like(bias_acc)
    loads[0].wait()
    deal(up_raw, raw, index, *UP)

    def step_on(*groups):
        for group in groups:
            if group.step < 8:
                group.advance()

    def add_bias(row, value):
        bias_acc[row:row + 1, :] += value

    def w(layer, i):
        return mats[layer, i]

    def b(layer, i):
        return bias[layer, i:i + 1, :]

    def hot_rows(block, size):
        nodes = lax.broadcasted_iota(jnp.int32, (size, B), 0)
        return jnp.where(nodes == index[block:block + 1, :], 1.0, 0.0).astype(BF16)

    def edge_forward(block, pre, layer):
        active, slope_now = silu_parts(pre)
        half = active.astype(BF16)
        act[block] = half
        slope[block] = slope_now.astype(BF16)
        message, scale_now = normed(dot_plain(half, w(layer, 2)) + b(layer, 1))
        unit[block] = message.astype(BF16)
        scale[block] = scale_now
        return message

    def edge_backward(block, g, layer):
        dy = norm_back(g, unit[block].astype(F32), scale[block])
        half = dy.astype(BF16)
        dys[block] = half
        dp = slope[block].astype(F32) * dot_cols(half, w(layer, 2))
        return dp, col_sum(dy), col_sum(dp)

    def node_forward(layer, state, agg, pre):
        node_in[layer] = agg
        active, slope_now = silu_parts(pre + dot_plain(agg, w(layer, 4)))
        half = active.astype(BF16)
        nact[layer] = half
        nslope[layer] = slope_now.astype(BF16)
        unit_now, scale_now = normed(dot_plain(half, w(layer, 5)) + b(layer, 3))
        nunit[layer] = unit_now.astype(BF16)
        nscale[layer] = scale_now
        return (state.astype(F32) + unit_now).astype(BF16)

    def node_backward(layer, g, share):
        dz = norm_back(g, nunit[layer].astype(F32), nscale[layer])
        dz16 = dz.astype(BF16)
        dq = nslope[layer].astype(F32) * dot_cols(dz16, w(layer, 5))
        dq16 = dq.astype(BF16)
        add_bias(4 * layer + 3, share * col_sum(dz))
        add_bias(4 * layer + 2, share * col_sum(dq))
        return dz16, dq16

    def piece(i):
        return pl.ds(i * (H // PIECES), H // PIECES)

    def sum_start(first, value):
        half = value.astype(BF16)
        csend[first, 0] = half[:H]
        csend[first, 1] = half[H:]
        odd = lax.rem(place.gx, 2)
        one = (place.gx + 1 - 2 * odd, place.gy)
        two = (lax.rem(place.gx + 2 * odd + 3, 4), place.gy)
        waits = []
        for i in range(PIECES):
            batch = None
            for side, device in ((0, one), (1, two)):
                batch = post(csend.at[first, side, piece(i)], crecv.at[first, side, piece(i)], device, batch)
            waits.append(batch)
        return waits, one, two

    def add_piece(at, i, side):
        both = csend[at, side, piece(i)].astype(F32) + crecv[at, side, piece(i)].astype(F32)
        return both.astype(BF16)

    def sum_middle(first, state):
        waits, one, two = state
        later = []
        for i in range(PIECES):
            waits[i].wait()
            batch = None
            for side, device in ((0, two), (1, one)):
                csend[first + 1, side, piece(i)] = add_piece(first, i, side)
                batch = post(csend.at[first + 1, side, piece(i)], crecv.at[first + 1, side, piece(i)], device, batch)
            later.append(batch)
        return later

    def sum_end(first, waits):
        for i in range(PIECES):
            waits[i].wait()
            for side in (0, 1):
                summed[side, piece(i)] = add_piece(first + 1, i, side)
        return summed[...].reshape(B, B)

    for block in range(*UP):
        onehot[block] = hot_rows(block, B)
    for load in loads[1:5]:
        load.wait()
    sent = dot_plain(fine[...], w(0, 0)) + b(0, 0)
    table[...] = dot_plain(coarse[...], w(0, 1)).astype(BF16)
    up_sum = None
    for block in range(*UP):
        message = edge_forward(block, sent + dot_rows(onehot[block], table[...]), 0)
        part = dot_plain(onehot[block], message.astype(BF16))
        up_sum = part if up_sum is None else up_sum + part

    pl.semaphore_wait(barrier, len(near))
    state = sum_start(0, up_sum)
    for load in loads[5:]:
        load.wait()
    pres[0] = dot_plain(coarse[...], w(0, 3)) + b(0, 2)
    deal(down_raw, raw, index, *DOWN)
    deal(same_raw, raw, index, *SAME)
    place_in = index[SAME[0]:SAME[1], :]
    moved = jnp.where(place_in < H, place_in + B, place_in - H)
    index[SAME[0]:SAME[1], :] = jnp.where(place_in < H + B, moved, place_in)
    index[11:12, :H] = halo_raw[0:1, :]
    index[11:12, H:] = halo_raw[1:2, :]
    for block in range(*DOWN):
        onehot[block] = hot_rows(block, B)
    onehot[5] = hot_rows(11, B)
    state = sum_middle(0, state)
    for block in range(*SAME):
        samehot[block - 5] = hot_rows(block, 2 * B)
    pres[1] = dot_plain(fine[...], w(2, 3)) + b(2, 2)
    pres[2] = dot_plain(fine[...], w(2, 1)) + b(2, 0)
    agg = sum_end(0, state)
    lifted = node_forward(0, coarse[...], agg, pres[0])
    ext[:B] = lifted
    payload = dot_rows(onehot[5], lifted).astype(BF16)
    hsend[0] = payload[:H]
    hsend[1] = payload[H:]
    halo = post(hsend.at[0], ext.at[B + H:], place.beside(-1))
    post(hsend.at[1], ext.at[B:B + H], place.beside(1), halo)

    pres[3] = dot_plain(lifted, w(1, 1)) + b(1, 0)
    gtab[:B] = dot_plain(lifted, w(1, 0)).astype(BF16)
    for block in range(*SAME):
        own_part[block - 5] = pres[3] + dot_rows(samehot[block - 5, :B], gtab[:B])
    pres[4] = dot_plain(lifted, w(1, 3)) + b(1, 2)
    halo.wait()
    gtab[B:] = dot_plain(ext[B:], w(1, 0)).astype(BF16)
    same_sum = None
    for block in range(*SAME):
        message = edge_forward(
            block, own_part[block - 5] + dot_rows(samehot[block - 5, B:], gtab[B:]), 1
        )
        same_sum = message if same_sum is None else same_sum + message
    mixed = node_forward(1, ext[:B], same_sum.astype(BF16), pres[4])
    nact[3] = mixed

    table[...] = dot_plain(mixed, w(2, 0)).astype(BF16)
    down_sum = None
    for block in range(*DOWN):
        message = edge_forward(block, pres[2] + dot_rows(onehot[block], table[...]), 2)
        down_sum = message if down_sum is None else down_sum + message
    fine_out[...] = node_forward(2, fine[...], down_sum.astype(BF16), pres[1])
    dz2, dq2 = node_backward(2, cot[...].astype(F32) * (1.0 / math.sqrt(total_fine)), 1.0)
    g = dot_cols(dq2, w(2, 4))
    taken = back = None
    for block in range(*DOWN):
        dp, db2, db1 = edge_backward(block, g, 2)
        add_bias(8, db1)
        add_bias(9, db2)
        part = dot_plain(onehot[block], dp.astype(BF16))
        taken = dp if taken is None else taken + dp
        back = part if back is None else back + part
    state = sum_start(2, back)
    layer2a.put(1, dot_rows(fine[...], taken.astype(BF16)))
    layer2a.put(2, dot_rows(act[2:5].reshape(3 * B, B), dys[2:5].reshape(3 * B, B)))
    state = sum_middle(2, state)
    layer2b.put(0, dot_rows(fine[...], dq2))
    layer2b.put(1, dot_rows(node_in[2], dq2))
    layer2b.put(2, dot_rows(nact[2], dz2))
    sent_half = sum_end(2, state)
    grad_mixed = dot_cols(sent_half, w(2, 0))
    layer2a.put(0, 0.25 * dot_rows(nact[3], sent_half))
    step_on(layer2a, layer2b)

    dz1, dq1 = node_backward(1, grad_mixed, 0.25)
    pres[0] = grad_mixed + dot_cols(dq1, w(1, 3))
    g = dot_cols(dq1, w(1, 4))
    taken = back = None
    for block in range(*SAME):
        dp, db2, db1 = edge_backward(block, g, 1)
        add_bias(4, 0.25 * db1)
        add_bias(5, 0.25 * db2)
        part = dot_plain(samehot[block - 5], dp.astype(BF16))
        taken = dp if taken is None else taken + dp
        back = part if back is None else back + part
    hsend[2] = back[B:B + H].astype(BF16)
    hsend[3] = back[B + H:].astype(BF16)
    returns = post(hsend.at[2], hback.at[1], place.beside(-1))
    post(hsend.at[3], hback.at[0], place.beside(1), returns)
    own = back[:B]
    step_on(layer2a, layer2b)
    lifted = ext[:B]
    taken_half = taken.astype(BF16)
    layer1.put(1, 1.0 * dot_rows(lifted, taken_half))
    layer1.put(2, dot_rows(act[5:11].reshape(6 * B, B), dys[5:11].reshape(6 * B, B)))
    layer1.put(3, dot_rows(lifted, dq1))
    layer1.put(4, dot_rows(node_in[1], dq1))
    layer1.put(5, dot_rows(nact[1], dz1))
    grad_lifted = pres[0] + dot_cols(taken_half, w(1, 1))
    returns.wait()
    next_sends()
    own += dot_plain(onehot[5], hback[...].reshape(B, B))
    own_half = own.astype(BF16)
    grad_lifted += dot_cols(own_half, w(1, 0))
    lifted_cot[...] = grad_lifted * math.sqrt(total_fine)
    layer1.put(0, dot_rows(lifted, own_half))
    step_on(layer1)

    dz0, dq0 = node_backward(0, grad_lifted, 0.25)
    table[...] = dot_cols(dq0, w(0, 4)).astype(BF16)
    taken = back = None
    for block in range(*UP):
        if block == UP[1] - 1:
            step_on(layer2a, layer2b, layer1)
        dp, db2, db1 = edge_backward(block, dot_rows(onehot[block], table[...]), 0)
        add_bias(0, db1)
        add_bias(1, db2)
        part = dot_plain(onehot[block], dp.astype(BF16))
        taken = dp if taken is None else taken + dp
        back = part if back is None else back + part
    edge0[0].put(0, dot_rows(fine[...], taken.astype(BF16)))
    edge0[1].put(0, dot_rows(coarse[...], back.astype(BF16)))
    edge0[2].put(0, dot_rows(act[0:2].reshape(2 * B, B), dys[0:2].reshape(2 * B, B)))
    step_on(*edge0)
    bias_batch = [post(bias_acc, bias_core, place.partner())]
    node0.put(0, dot_rows(coarse[...], dq0))
    node0.put(1, dot_rows(node_in[0], dq0))
    node0.put(2, dot_rows(nact[0], dz0))
    step_on(node0)

    def bias_step(step):
        bias_batch.pop().wait()
        batch = None
        if step == 0:
            total = bias_acc[...] + bias_core[...]
        else:
            total = bias_slots[step - 1, 0] + bias_slots[step - 1, 1]
            total = total + bias_slots[step - 1, 2] + bias_slots[step - 1, 3]
        if step == 3:
            gbias[...] = total
            return
        axis = "yxz"[step]
        at = place.at(axis)
        bias_slots[step, at] = total
        for d in (1, 2, 3):
            spot = bias_slots.at[step, at]
            batch = post(spot, spot, place.peer(axis, d), batch)
        bias_batch.append(batch)

    for step in range(6):
        step_on(*edge0, node0, layer1, layer2a, layer2b)
        if step < 4:
            bias_step(step)
        if step == 2:
            leaving[0].wait()
            next_sends()
        if step == 3:
            leaving[1].wait()
    assert all(group.step == 8 for group in groups)
    leaving[2].wait()
    assert len(batches) == BATCHES and len(leaving) == SENDS
    assert max(batch.size for batch in batches + leaving) <= RULER * UNIT


def finish(fine_in, lifted_in, grads, gbias, fine_out, lifted_out, matrices_out, biases_out, wide, sems):
    copies = [
        pltpu.make_async_copy(fine_in, fine_out, sems.at[3]),
        pltpu.make_async_copy(lifted_in, lifted_out, sems.at[4]),
    ]
    for copy in copies:
        copy.start()
    for i in range(18):
        layer = i // 6
        wide[i, :, :H] = grads[0, i].astype(F32)
        wide[i, :, H:] = grads[1, i].astype(F32)
        pltpu.make_async_copy(wide.at[i], matrices_out.at[layer, i % 6], sems.at[layer]).start()
    for layer in range(3):
        biases_out[layer] = gbias[4 * layer:4 * layer + 4, :]
        copies.append(pltpu.make_async_copy(wide.at[6 * layer:6 * layer + 6], matrices_out.at[layer], sems.at[layer]))
    for copy in copies:
        copy.wait()


def group_scratch(kind, count):
    whole = 64 if kind == "same" else B
    spare = 16 if kind == "same" else B
    small = 64 if kind == "quick" else 16
    slots = 4 if kind == "quick" else 3
    return [
        pltpu.VMEM((2, count, B, H), BF16),
        pltpu.VMEM((count, whole, H), BF16),
        pltpu.VMEM((count, spare, H), BF16),
        pltpu.VMEM((3, count, spare // 4, H), BF16),
        pltpu.VMEM((count, 64, H), BF16),
        pltpu.VMEM((slots, count, small, H), BF16),
        pltpu.VMEM((count, small, H), BF16),
        pltpu.VMEM((4, count, small, H), BF16),
        pltpu.VMEM((count, small, H), BF16),
    ]


def local(fine_state, coarse_state, up_target, down_source, halo_lists, same_source, matrices, biases, fine_cotangent):
    total_fine = fine_state.shape[0] * lax.axis_size("gx") * lax.axis_size("gy")
    scratch = [
        pltpu.SemaphoreType.DMA((SENDS,)),
        pltpu.SemaphoreType.DMA((BATCHES,)),
        pltpu.VMEM((6, B, B), BF16),
        pltpu.VMEM((6, 2 * B, B), BF16),
        pltpu.VMEM((11, B, B), BF16),
        pltpu.VMEM((11, B, B), BF16),
        pltpu.VMEM((11, B, B), BF16),
        pltpu.VMEM((11, B, 1), F32),
        pltpu.VMEM((11, B, B), BF16),
        pltpu.VMEM((4, B, B), BF16),
        pltpu.VMEM((3, B, B), BF16),
        pltpu.VMEM((3, B, B), BF16),
        pltpu.VMEM((3, B, 1), F32),
        pltpu.VMEM((B, B), BF16),
        pltpu.VMEM((2 * B, B), BF16),
        pltpu.VMEM((2 * B, B), BF16),
        pltpu.VMEM((5, B, B), F32),
        pltpu.VMEM((4, 2, H, B), BF16),
        pltpu.VMEM((4, 2, H, B), BF16),
        pltpu.VMEM((4, H, B), BF16),
        pltpu.VMEM((2, H, B), BF16),
        pltpu.VMEM((3, B, B), BF16),
        pltpu.VMEM((16, B), F32),
        pltpu.VMEM((16, B), F32),
        pltpu.VMEM((3, 4, 16, B), F32),
        pltpu.VMEM((16, H), jnp.int32),
        pltpu.VMEM((16, B), jnp.int32),
        pltpu.SemaphoreType.DMA((12,)),
        pltpu.VMEM((2, H, B), BF16),
        pltpu.VMEM((6, B, B), F32),
        pltpu.VMEM((RULER, 16, H), BF16),
        pltpu.VMEM((B, B), BF16),
        pltpu.VMEM((B, B), BF16),
        pltpu.VMEM((B, B), BF16),
        pltpu.VMEM((4, H), jnp.int32),
        pltpu.VMEM((6, H), jnp.int32),
        pltpu.VMEM((2, H), jnp.int32),
        pltpu.VMEM((12, H), jnp.int32),
        pltpu.VMEM((3, 6, B, B), BF16),
        pltpu.VMEM((3, 4, B), F32),
    ]
    for kind, _, first, end in GROUPS:
        scratch += group_scratch(kind, end - first)
    vmem = pl.BlockSpec(memory_space=pltpu.VMEM)

    def body(*refs):
        kernel(total_fine, *refs)

    fine_out, lifted, grads, gbias = pl.pallas_call(
        body,
        out_shape=(
            jax.ShapeDtypeStruct((B, B), BF16),
            jax.ShapeDtypeStruct((B, B), F32),
            jax.ShapeDtypeStruct((2, 18, B, H), BF16),
            jax.ShapeDtypeStruct((16, B), F32),
        ),
        in_specs=[pl.BlockSpec(memory_space=pltpu.HBM)] * 9,
        out_specs=(vmem,) * 4,
        scratch_shapes=scratch,
        compiler_params=pltpu.CompilerParams(
            collective_id=0, has_side_effects=True, vmem_limit_bytes=32 << 20
        ),
        name="sweep",
    )(*[
        pltpu.with_memory_space_constraint(value, pltpu.HBM)
        for value in (
            fine_state, coarse_state, fine_cotangent, up_target.reshape(4, H), down_source.reshape(6, H), halo_lists,
            same_source.reshape(12, H), matrices, biases,
        )
    ])
    hbm = pl.BlockSpec(memory_space=pl.ANY)
    return pl.pallas_call(
        finish,
        out_shape=(
            jax.ShapeDtypeStruct((B, B), BF16),
            jax.ShapeDtypeStruct((B, B), F32),
            jax.ShapeDtypeStruct((3, 6, B, B), F32),
            jax.ShapeDtypeStruct((3, 4, B), F32),
        ),
        in_specs=[vmem] * 4,
        out_specs=(hbm, hbm, hbm, vmem),
        scratch_shapes=[pltpu.VMEM((18, B, B), F32), pltpu.SemaphoreType.DMA((5,))],
        compiler_params=pltpu.CompilerParams(vmem_limit_bytes=16 << 20),
        name="finish",
    )(fine_out, lifted, grads, gbias)


def solution(mesh):
    in_specs = (
        P(("gx", "gy"), None),
        P("gy", None),
        P(("gx", "gy")),
        P(("gx", "gy")),
        P("gy", None),
        P("gy"),
        P(),
        P(),
        P(("gx", "gy"), None),
    )
    out_specs = (P(("gx", "gy"), None), P("gy", None), P(), P())
    return jax.shard_map(local, mesh=mesh, in_specs=in_specs, out_specs=out_specs, check_vma=False)
```

```python
import math

import jax
import jax.numpy as jnp
from jax import lax
from jax.experimental import pallas as pl
from jax.experimental.pallas import tpu as pltpu
from jax.sharding import PartitionSpec as P

MESH = pl.DeviceIdType.MESH
F32 = jnp.float32
BF16 = jnp.bfloat16
B = 256
H = 128
UP, DOWN, SAME = (0, 2), (2, 5), (5, 11)
BATCHES = 66
SENDS = 3
UNIT = 4096
RULER = 512
PIECES = 4
GROUPS = (
    ("quick", ("x", "y", "z"), 0, 1),
    ("quick", ("z", "x", "y"), 1, 2),
    ("quick", ("x", "z", "y"), 2, 3),
    ("same", ("y", "x", "z"), 3, 6),
    ("same", ("y", "z", "x"), 6, 12),
    ("fine", ("x", "z", "y"), 12, 15),
    ("fine", ("z", "x", "y"), 15, 18),
)


def dot_plain(a, b):
    return jnp.dot(a, b, preferred_element_type=F32)


def dot_rows(a, b):
    return lax.dot_general(a, b, (((0,), (0,)), ((), ())), preferred_element_type=F32)


def dot_cols(a, b):
    return lax.dot_general(a, b, (((1,), (1,)), ((), ())), preferred_element_type=F32)


def silu_parts(u):
    twice = 1.0 + jnp.tanh(u)
    active = u * twice
    return active, 0.5 * (twice + active * (2.0 - twice))


def row_mean(x):
    return jnp.mean(x, axis=-1, keepdims=True)


def normed(y):
    centred = y - row_mean(y)
    scale = lax.rsqrt(row_mean(centred * centred) + 1e-05)
    return centred * scale, scale


def norm_back(g, unit, scale):
    return scale * (g - row_mean(g) - unit * row_mean(g * unit))


def col_sum(x):
    return jnp.sum(x, axis=0, keepdims=True)


class Batch:
    def __init__(self, sem, ruler):
        self.sem, self.ruler, self.size = sem, ruler, 0

    def wait(self):
        span = self.ruler.at[:self.size // UNIT]
        pltpu.make_async_copy(span, span, self.sem).wait()


class Group:
    def __init__(self, post, place, axes, rows, shared, refs, out):
        self.shared = shared
        self.post, self.place, self.axes, self.rows, self.out = post, place, axes, rows, out
        self.g, self.rc, self.s1, self.r1, self.s2, self.r2, self.s3, self.r3, self.s4 = refs
        self.count = rows.stop - rows.start
        self.step = 0
        self.batch = None

    def put(self, i, value):
        half = value.astype(BF16)
        self.g[0, i] = half[:, :H]
        self.g[1, i] = half[:, H:]

    def send(self, src, dst, device):
        self.batch = self.post(src, dst, device, self.batch)

    def landed(self):
        self.batch.wait()
        self.batch = None

    def advance(self):
        getattr(self, "step%d" % self.step)()
        self.step += 1

    def quarter(self):
        return pl.ds(pl.multiple_of(self.place.at(self.axes[0]) * 64, 64), 64)

    def step0(self):
        other = 1 - self.place.core
        src = self.g.at[other, :, self.quarter(), :] if self.shared else self.g.at[other]
        self.send(src, self.rc, self.place.partner())

    def step1(self):
        self.landed()
        core = self.place.core
        if self.shared:
            for i in range(self.count):
                own = self.g[core, i, self.quarter(), :].astype(F32)
                self.s2[i] = (own + self.rc[i].astype(F32)).astype(BF16)
            self.scatter(self.axes[1], 16, self.s2, self.r2)
            self.step = 2
            return
        for i in range(self.count):
            self.s1[i] = (self.g[core, i].astype(F32) + self.rc[i].astype(F32)).astype(BF16)
        self.scatter(self.axes[0], 64, self.s1, self.r1)

    def scatter(self, axis, size, src, landing):
        at = self.place.at(axis)
        for d in (1, 2, 3):
            to = lax.rem(at + d, 4)
            rows = pl.ds(pl.multiple_of(to * size, size), size)
            self.send(src.at[:, rows, :], landing.at[d - 1], self.place.peer(axis, d))

    def gather_sum(self, axis, size, src, landing, out):
        at = self.place.at(axis)
        rows = pl.ds(pl.multiple_of(at * size, size), size)
        for i in range(self.count):
            total = src[i, rows, :].astype(F32)
            for d in range(3):
                total += landing[d, i].astype(F32)
            out[i] = total.astype(BF16)

    def step2(self):
        self.landed()
        self.gather_sum(self.axes[0], 64, self.s1, self.r1, self.s2)
        self.scatter(self.axes[1], 16, self.s2, self.r2)

    def step3(self):
        self.landed()
        self.gather_sum(self.axes[1], 16, self.s2, self.r2, self.s3)
        self.share(self.axes[2], self.s3, self.r3)

    def share(self, axis, src, slots):
        at = self.place.at(axis)
        for d in (1, 2, 3):
            self.send(src, slots.at[at], self.place.peer(axis, d))
        slots[at] = src[...]

    def slot_sum(self, slots, out):
        for i in range(self.count):
            total = slots[0, i].astype(F32)
            for j in (1, 2, 3):
                total += slots[j, i].astype(F32)
            out[i] = total.astype(BF16)

    def step4(self):
        self.landed()
        self.slot_sum(self.r3, self.s4)
        start = self.place.at(self.axes[0]) * 64 + self.place.at(self.axes[1]) * 16
        rows = pl.ds(pl.multiple_of(start, 16), 16)
        spot = self.out.at[self.place.core, self.rows, rows, :]
        for d in (1, 2, 3):
            self.send(self.s4, spot, self.place.peer(self.axes[1], d))
        for i in range(self.count):
            self.out[self.place.core, self.rows.start + i, rows, :] = self.s4[i]

    def step5(self):
        self.landed()
        spot = self.out.at[self.place.core, self.rows, self.quarter(), :]
        for d in (1, 2, 3):
            self.send(spot, spot, self.place.peer(self.axes[0], d))

    def step6(self):
        self.landed()
        spot = self.out.at[self.place.core, self.rows, :, :]
        self.send(spot, spot, self.place.partner())

    def step7(self):
        self.landed()


class Quick(Group):
    def step2(self):
        self.landed()
        self.gather_sum(self.axes[0], 64, self.s1, self.r1, self.s2)
        self.share(self.axes[1], self.s2, self.r2)

    def step3(self):
        self.landed()
        self.slot_sum(self.r2, self.s3)
        self.share(self.axes[2], self.s3, self.r3)

    def step4(self):
        self.landed()
        self.slot_sum(self.r3, self.s4)
        spot = self.out.at[self.place.core, self.rows, self.quarter(), :]
        for d in (1, 2, 3):
            self.send(self.s4, spot, self.place.peer(self.axes[0], d))
        for i in range(self.count):
            self.out[self.place.core, self.rows.start + i, self.quarter(), :] = self.s4[i]
        self.step = 5


class Place:
    def __init__(self):
        self.gx = lax.axis_index("gx")
        self.gy = lax.axis_index("gy")
        self.core = lax.rem(self.gy, 2)
        self.x = lax.rem(self.gy // 2, 4)
        self.z = self.gy // 8

    def at(self, axis):
        return {"x": self.x, "y": self.gx, "z": self.z}[axis]

    def partner(self):
        return (self.gx, self.gy + 1 - 2 * self.core)

    def peer(self, axis, d):
        if axis == "y":
            return (lax.rem(self.gx + d, 4), self.gy)
        if axis == "x":
            return (self.gx, self.z * 8 + lax.rem(self.x + d, 4) * 2 + self.core)
        return (self.gx, lax.rem(self.z + d, 4) * 8 + self.x * 2 + self.core)

    def beside(self, d):
        return (self.gx, lax.rem(self.gy + d + 32, 32))


def deal(source, raw, index, first, end):
    ways = end - first
    raw[:2 * ways, :] = source[...]
    rows = raw[...]
    lane = lax.broadcasted_iota(jnp.int32, rows.shape, 1)
    for k in range(ways):
        place = lane * ways + k
        picked = jnp.take_along_axis(rows, lax.rem(place, H), axis=1, mode="promise_in_bounds")
        line = place[0:1] // H
        for half in (0, 1):
            row = picked[ways * half:ways * half + 1]
            for i in range(1, ways):
                row = jnp.where(line == i, picked[ways * half + i:ways * half + i + 1], row)
            index[first + k:first + k + 1, half * H:half * H + H] = row


def kernel(total_fine, *refs):
    inputs, (fine_out, lifted_cot, grads, gbias) = refs[:9], refs[9:13]
    (send_sems, recv_sems, onehot, samehot, act, slope, unit, scale, dys, nact, nslope, nunit, nscale,
     table, ext, gtab, pres, csend, crecv, hsend, hback, node_in, bias_acc, bias_core, bias_slots, raw, index, load_sems, summed, own_part, ruler,
     fine, coarse, cot, up_raw, down_raw, halo_raw, same_raw, mats, bias) = refs[13:53]
    group_refs = refs[53:]
    place = Place()
    batches = []
    leaving = []

    def next_sends():
        leaving.append(Batch(send_sems.at[len(leaving)], ruler))

    def post(src, dst, device, batch=None):
        if batch is None:
            batch = Batch(recv_sems.at[len(batches)], ruler)
            batches.append(batch)
        pltpu.make_async_remote_copy(
            src_ref=src, dst_ref=dst, send_sem=leaving[-1].sem, recv_sem=batch.sem,
            device_id=device, device_id_type=MESH,
        ).start()
        size = math.prod(dst.shape) * dst.dtype.itemsize
        assert size % UNIT == 0
        batch.size += size
        leaving[-1].size += size
        return batch

    next_sends()
    loads = []
    for i, (src, dst) in enumerate([
        (inputs[3], up_raw), (inputs[0], fine), (inputs[1], coarse), (inputs[8], bias),
        (inputs[7].at[0, 0:3], mats.at[0, 0:3]), (inputs[4], down_raw), (inputs[6], same_raw), (inputs[5], halo_raw),
        (inputs[7].at[0, 3:6], mats.at[0, 3:6]), (inputs[7].at[2], mats.at[2]), (inputs[7].at[1], mats.at[1]),
        (inputs[2], cot),
    ]):
        loads.append(pltpu.make_async_copy(src, dst, load_sems.at[i]))
    for load in loads[:5]:
        load.start()

    barrier = pltpu.get_barrier_semaphore()
    near = [place.peer(a, d) for a in ("x", "y", "z") for d in (1, 2, 3)]
    near += [place.partner(), place.beside(1), place.beside(-1)]
    for device in near:
        pl.semaphore_signal(barrier, inc=1, device_id=device, device_id_type=MESH)
    for load in loads[5:]:
        load.start()

    groups = [
        (Quick if kind == "quick" else Group)(
            post, place, axes, slice(first, end), kind == "same", group_refs[9 * at:9 * at + 9], grads
        )
        for at, (kind, axes, first, end) in enumerate(GROUPS)
    ]
    edge0, (node0, layer1, layer2a, layer2b) = groups[:3], groups[3:]

    bias_acc[...] = jnp.zeros_like(bias_acc)
    loads[0].wait()
    deal(up_raw, raw, index, *UP)

    def step_on(*groups):
        for group in groups:
            if group.step < 8:
                group.advance()

    def add_bias(row, value):
        bias_acc[row:row + 1, :] += value

    def w(layer, i):
        return mats[layer, i]

    def b(layer, i):
        return bias[layer, i:i + 1, :]

    def hot_rows(block, size):
        nodes = lax.broadcasted_iota(jnp.int32, (size, B), 0)
        return jnp.where(nodes == index[block:block + 1, :], 1.0, 0.0).astype(BF16)

    def edge_forward(block, pre, layer):
        active, slope_now = silu_parts(pre)
        half = active.astype(BF16)
        act[block] = half
        slope[block] = slope_now.astype(BF16)
        message, scale_now = normed(dot_plain(half, w(layer, 2)) + b(layer, 1))
        unit[block] = message.astype(BF16)
        scale[block] = scale_now
        return message

    def edge_backward(block, g, layer):
        dy = norm_back(g, unit[block].astype(F32), scale[block])
        half = dy.astype(BF16)
        dys[block] = half
        dp = slope[block].astype(F32) * dot_cols(half, w(layer, 2))
        return dp, col_sum(dy), col_sum(dp)

    def node_forward(layer, state, agg, pre):
        node_in[layer] = agg
        active, slope_now = silu_parts(0.5 * (pre + dot_plain(agg, w(layer, 4))))
        half = active.astype(BF16)
        nact[layer] = half
        nslope[layer] = slope_now.astype(BF16)
        unit_now, scale_now = normed(dot_plain(half, w(layer, 5)) + b(layer, 3))
        nunit[layer] = unit_now.astype(BF16)
        nscale[layer] = scale_now
        return (state.astype(F32) + unit_now).astype(BF16)

    def node_backward(layer, g, share):
        dz = norm_back(g, nunit[layer].astype(F32), nscale[layer])
        dz16 = dz.astype(BF16)
        dq = nslope[layer].astype(F32) * dot_cols(dz16, w(layer, 5))
        dq16 = dq.astype(BF16)
        add_bias(4 * layer + 3, share * col_sum(dz))
        add_bias(4 * layer + 2, share * col_sum(dq))
        return dz16, dq16

    def piece(i):
        return pl.ds(i * (H // PIECES), H // PIECES)

    def sum_start(first, value):
        half = value.astype(BF16)
        csend[first, 0] = half[:H]
        csend[first, 1] = half[H:]
        odd = lax.rem(place.gx, 2)
        one = (place.gx + 1 - 2 * odd, place.gy)
        two = (lax.rem(place.gx + 2 * odd + 3, 4), place.gy)
        waits = []
        for i in range(PIECES):
            batch = None
            for side, device in ((0, one), (1, two)):
                batch = post(csend.at[first, side, piece(i)], crecv.at[first, side, piece(i)], device, batch)
            waits.append(batch)
        return waits, one, two

    def add_piece(at, i, side):
        both = csend[at, side, piece(i)].astype(F32) + crecv[at, side, piece(i)].astype(F32)
        return both.astype(BF16)

    def sum_middle(first, state):
        waits, one, two = state
        later = []
        for i in range(PIECES):
            waits[i].wait()
            batch = None
            for side, device in ((0, two), (1, one)):
                csend[first + 1, side, piece(i)] = add_piece(first, i, side)
                batch = post(csend.at[first + 1, side, piece(i)], crecv.at[first + 1, side, piece(i)], device, batch)
            later.append(batch)
        return later

    def sum_end(first, waits):
        for i in range(PIECES):
            waits[i].wait()
            for side in (0, 1):
                summed[side, piece(i)] = add_piece(first + 1, i, side)
        return summed[...].reshape(B, B)

    for block in range(*UP):
        onehot[block] = hot_rows(block, B)
    for load in loads[1:5]:
        load.wait()
    sent = 0.5 * (dot_plain(fine[...], w(0, 0)) + b(0, 0))
    table[...] = (0.5 * dot_plain(coarse[...], w(0, 1))).astype(BF16)
    up_sum = None
    for block in range(*UP):
        message = edge_forward(block, sent + dot_rows(onehot[block], table[...]), 0)
        part = dot_plain(onehot[block], message.astype(BF16))
        up_sum = part if up_sum is None else up_sum + part

    pl.semaphore_wait(barrier, len(near))
    state = sum_start(0, up_sum)
    for load in loads[5:]:
        load.wait()
    pres[0] = dot_plain(coarse[...], w(0, 3)) + b(0, 2)
    deal(down_raw, raw, index, *DOWN)
    deal(same_raw, raw, index, *SAME)
    place_in = index[SAME[0]:SAME[1], :]
    moved = jnp.where(place_in < H, place_in + B, place_in - H)
    index[SAME[0]:SAME[1], :] = jnp.where(place_in < H + B, moved, place_in)
    index[11:12, :H] = halo_raw[0:1, :]
    index[11:12, H:] = halo_raw[1:2, :]
    for block in range(*DOWN):
        onehot[block] = hot_rows(block, B)
    onehot[5] = hot_rows(11, B)
    state = sum_middle(0, state)
    for block in range(*SAME):
        samehot[block - 5] = hot_rows(block, 2 * B)
    pres[1] = dot_plain(fine[...], w(2, 3)) + b(2, 2)
    pres[2] = 0.5 * (dot_plain(fine[...], w(2, 1)) + b(2, 0))
    agg = sum_end(0, state)
    lifted = node_forward(0, coarse[...], agg, pres[0])
    ext[:B] = lifted
    payload = dot_rows(onehot[5], lifted).astype(BF16)
    hsend[0] = payload[:H]
    hsend[1] = payload[H:]
    halo = post(hsend.at[0], ext.at[B + H:], place.beside(-1))
    post(hsend.at[1], ext.at[B:B + H], place.beside(1), halo)

    pres[3] = 0.5 * (dot_plain(lifted, w(1, 1)) + b(1, 0))
    gtab[:B] = (0.5 * dot_plain(lifted, w(1, 0))).astype(BF16)
    for block in range(*SAME):
        own_part[block - 5] = pres[3] + dot_rows(samehot[block - 5, :B], gtab[:B])
    pres[4] = dot_plain(lifted, w(1, 3)) + b(1, 2)
    halo.wait()
    gtab[B:] = (0.5 * dot_plain(ext[B:], w(1, 0))).astype(BF16)
    same_sum = None
    for block in range(*SAME):
        message = edge_forward(
            block, own_part[block - 5] + dot_rows(samehot[block - 5, B:], gtab[B:]), 1
        )
        same_sum = message if same_sum is None else same_sum + message
    mixed = node_forward(1, ext[:B], same_sum.astype(BF16), pres[4])
    nact[3] = mixed

    table[...] = (0.5 * dot_plain(mixed, w(2, 0))).astype(BF16)
    down_sum = None
    for block in range(*DOWN):
        message = edge_forward(block, pres[2] + dot_rows(onehot[block], table[...]), 2)
        down_sum = message if down_sum is None else down_sum + message
    fine_out[...] = node_forward(2, fine[...], down_sum.astype(BF16), pres[1])
    dz2, dq2 = node_backward(2, cot[...].astype(F32) * (1.0 / math.sqrt(total_fine)), 1.0)
    g = dot_cols(dq2, w(2, 4))
    taken = back = None
    for block in range(*DOWN):
        dp, db2, db1 = edge_backward(block, g, 2)
        add_bias(8, db1)
        add_bias(9, db2)
        part = dot_plain(onehot[block], dp.astype(BF16))
        taken = dp if taken is None else taken + dp
        back = part if back is None else back + part
    state = sum_start(2, back)
    layer2a.put(1, dot_rows(fine[...], taken.astype(BF16)))
    layer2a.put(2, dot_rows(act[2:5].reshape(3 * B, B), dys[2:5].reshape(3 * B, B)))
    state = sum_middle(2, state)
    layer2b.put(0, dot_rows(fine[...], dq2))
    layer2b.put(1, dot_rows(node_in[2], dq2))
    layer2b.put(2, dot_rows(nact[2], dz2))
    sent_half = sum_end(2, state)
    grad_mixed = dot_cols(sent_half, w(2, 0))
    layer2a.put(0, 0.25 * dot_rows(nact[3], sent_half))
    step_on(layer2a, layer2b)

    dz1, dq1 = node_backward(1, grad_mixed, 0.25)
    pres[0] = grad_mixed + dot_cols(dq1, w(1, 3))
    g = dot_cols(dq1, w(1, 4))
    taken = back = None
    for block in range(*SAME):
        dp, db2, db1 = edge_backward(block, g, 1)
        add_bias(4, 0.25 * db1)
        add_bias(5, 0.25 * db2)
        part = dot_plain(samehot[block - 5], dp.astype(BF16))
        taken = dp if taken is None else taken + dp
        back = part if back is None else back + part
    hsend[2] = back[B:B + H].astype(BF16)
    hsend[3] = back[B + H:].astype(BF16)
    returns = post(hsend.at[2], hback.at[1], place.beside(-1))
    post(hsend.at[3], hback.at[0], place.beside(1), returns)
    own = back[:B]
    step_on(layer2a, layer2b)
    lifted = ext[:B]
    taken_half = taken.astype(BF16)
    layer1.put(1, 1.0 * dot_rows(lifted, taken_half))
    layer1.put(2, dot_rows(act[5:11].reshape(6 * B, B), dys[5:11].reshape(6 * B, B)))
    layer1.put(3, dot_rows(lifted, dq1))
    layer1.put(4, dot_rows(node_in[1], dq1))
    layer1.put(5, dot_rows(nact[1], dz1))
    grad_lifted = pres[0] + dot_cols(taken_half, w(1, 1))
    returns.wait()
    next_sends()
    own += dot_plain(onehot[5], hback[...].reshape(B, B))
    own_half = own.astype(BF16)
    grad_lifted += dot_cols(own_half, w(1, 0))
    lifted_cot[...] = grad_lifted * math.sqrt(total_fine)
    layer1.put(0, dot_rows(lifted, own_half))
    step_on(layer1)

    dz0, dq0 = node_backward(0, grad_lifted, 0.25)
    table[...] = dot_cols(dq0, w(0, 4)).astype(BF16)
    taken = back = None
    for block in range(*UP):
        if block == UP[1] - 1:
            step_on(layer2a, layer2b, layer1)
        dp, db2, db1 = edge_backward(block, dot_rows(onehot[block], table[...]), 0)
        add_bias(0, db1)
        add_bias(1, db2)
        part = dot_plain(onehot[block], dp.astype(BF16))
        taken = dp if taken is None else taken + dp
        back = part if back is None else back + part
    edge0[0].put(0, dot_rows(fine[...], taken.astype(BF16)))
    edge0[1].put(0, dot_rows(coarse[...], back.astype(BF16)))
    edge0[2].put(0, dot_rows(act[0:2].reshape(2 * B, B), dys[0:2].reshape(2 * B, B)))
    step_on(*edge0)
    bias_batch = [post(bias_acc, bias_core, place.partner())]
    node0.put(0, dot_rows(coarse[...], dq0))
    node0.put(1, dot_rows(node_in[0], dq0))
    node0.put(2, dot_rows(nact[0], dz0))
    step_on(node0)

    def bias_step(step):
        bias_batch.pop().wait()
        batch = None
        if step == 0:
            total = bias_acc[...] + bias_core[...]
        else:
            total = bias_slots[step - 1, 0] + bias_slots[step - 1, 1]
            total = total + bias_slots[step - 1, 2] + bias_slots[step - 1, 3]
        if step == 3:
            gbias[...] = total
            return
        axis = "yxz"[step]
        at = place.at(axis)
        bias_slots[step, at] = total
        for d in (1, 2, 3):
            spot = bias_slots.at[step, at]
            batch = post(spot, spot, place.peer(axis, d), batch)
        bias_batch.append(batch)

    for step in range(6):
        step_on(*edge0, node0, layer1, layer2a, layer2b)
        if step < 4:
            bias_step(step)
        if step == 2:
            leaving[0].wait()
            next_sends()
        if step == 3:
            leaving[1].wait()
    assert all(group.step == 8 for group in groups)
    leaving[2].wait()
    assert len(batches) == BATCHES and len(leaving) == SENDS
    assert max(batch.size for batch in batches + leaving) <= RULER * UNIT


def finish(fine_in, lifted_in, grads, gbias, fine_out, lifted_out, matrices_out, biases_out, wide, sems):
    copies = [
        pltpu.make_async_copy(fine_in, fine_out, sems.at[3]),
        pltpu.make_async_copy(lifted_in, lifted_out, sems.at[4]),
    ]
    for copy in copies:
        copy.start()
    for i in range(18):
        layer = i // 6
        wide[i, :, :H] = grads[0, i].astype(F32)
        wide[i, :, H:] = grads[1, i].astype(F32)
        pltpu.make_async_copy(wide.at[i], matrices_out.at[layer, i % 6], sems.at[layer]).start()
    for layer in range(3):
        biases_out[layer] = gbias[4 * layer:4 * layer + 4, :]
        copies.append(pltpu.make_async_copy(wide.at[6 * layer:6 * layer + 6], matrices_out.at[layer], sems.at[layer]))
    for copy in copies:
        copy.wait()


def group_scratch(kind, count):
    whole = 64 if kind == "same" else B
    spare = 16 if kind == "same" else B
    small = 64 if kind == "quick" else 16
    slots = 4 if kind == "quick" else 3
    return [
        pltpu.VMEM((2, count, B, H), BF16),
        pltpu.VMEM((count, whole, H), BF16),
        pltpu.VMEM((count, spare, H), BF16),
        pltpu.VMEM((3, count, spare // 4, H), BF16),
        pltpu.VMEM((count, 64, H), BF16),
        pltpu.VMEM((slots, count, small, H), BF16),
        pltpu.VMEM((count, small, H), BF16),
        pltpu.VMEM((4, count, small, H), BF16),
        pltpu.VMEM((count, small, H), BF16),
    ]


def local(fine_state, coarse_state, up_target, down_source, halo_lists, same_source, matrices, biases, fine_cotangent):
    total_fine = fine_state.shape[0] * lax.axis_size("gx") * lax.axis_size("gy")
    scratch = [
        pltpu.SemaphoreType.DMA((SENDS,)),
        pltpu.SemaphoreType.DMA((BATCHES,)),
        pltpu.VMEM((6, B, B), BF16),
        pltpu.VMEM((6, 2 * B, B), BF16),
        pltpu.VMEM((11, B, B), BF16),
        pltpu.VMEM((11, B, B), BF16),
        pltpu.VMEM((11, B, B), BF16),
        pltpu.VMEM((11, B, 1), F32),
        pltpu.VMEM((11, B, B), BF16),
        pltpu.VMEM((4, B, B), BF16),
        pltpu.VMEM((3, B, B), BF16),
        pltpu.VMEM((3, B, B), BF16),
        pltpu.VMEM((3, B, 1), F32),
        pltpu.VMEM((B, B), BF16),
        pltpu.VMEM((2 * B, B), BF16),
        pltpu.VMEM((2 * B, B), BF16),
        pltpu.VMEM((5, B, B), F32),
        pltpu.VMEM((4, 2, H, B), BF16),
        pltpu.VMEM((4, 2, H, B), BF16),
        pltpu.VMEM((4, H, B), BF16),
        pltpu.VMEM((2, H, B), BF16),
        pltpu.VMEM((3, B, B), BF16),
        pltpu.VMEM((16, B), F32),
        pltpu.VMEM((16, B), F32),
        pltpu.VMEM((3, 4, 16, B), F32),
        pltpu.VMEM((16, H), jnp.int32),
        pltpu.VMEM((16, B), jnp.int32),
        pltpu.SemaphoreType.DMA((12,)),
        pltpu.VMEM((2, H, B), BF16),
        pltpu.VMEM((6, B, B), F32),
        pltpu.VMEM((RULER, 16, H), BF16),
        pltpu.VMEM((B, B), BF16),
        pltpu.VMEM((B, B), BF16),
        pltpu.VMEM((B, B), BF16),
        pltpu.VMEM((4, H), jnp.int32),
        pltpu.VMEM((6, H), jnp.int32),
        pltpu.VMEM((2, H), jnp.int32),
        pltpu.VMEM((12, H), jnp.int32),
        pltpu.VMEM((3, 6, B, B), BF16),
        pltpu.VMEM((3, 4, B), F32),
    ]
    for kind, _, first, end in GROUPS:
        scratch += group_scratch(kind, end - first)
    vmem = pl.BlockSpec(memory_space=pltpu.VMEM)

    def body(*refs):
        kernel(total_fine, *refs)

    fine_out, lifted, grads, gbias = pl.pallas_call(
        body,
        out_shape=(
            jax.ShapeDtypeStruct((B, B), BF16),
            jax.ShapeDtypeStruct((B, B), F32),
            jax.ShapeDtypeStruct((2, 18, B, H), BF16),
            jax.ShapeDtypeStruct((16, B), F32),
        ),
        in_specs=[pl.BlockSpec(memory_space=pltpu.HBM)] * 9,
        out_specs=(vmem,) * 4,
        scratch_shapes=scratch,
        compiler_params=pltpu.CompilerParams(
            collective_id=0, has_side_effects=True, vmem_limit_bytes=32 << 20
        ),
        name="sweep",
    )(*[
        pltpu.with_memory_space_constraint(value, pltpu.HBM)
        for value in (
            fine_state, coarse_state, fine_cotangent, up_target.reshape(4, H), down_source.reshape(6, H), halo_lists,
            same_source.reshape(12, H), matrices, biases,
        )
    ])
    hbm = pl.BlockSpec(memory_space=pl.ANY)
    return pl.pallas_call(
        finish,
        out_shape=(
            jax.ShapeDtypeStruct((B, B), BF16),
            jax.ShapeDtypeStruct((B, B), F32),
            jax.ShapeDtypeStruct((3, 6, B, B), F32),
            jax.ShapeDtypeStruct((3, 4, B), F32),
        ),
        in_specs=[vmem] * 4,
        out_specs=(hbm, hbm, hbm, vmem),
        scratch_shapes=[pltpu.VMEM((18, B, B), F32), pltpu.SemaphoreType.DMA((5,))],
        compiler_params=pltpu.CompilerParams(vmem_limit_bytes=16 << 20),
        name="finish",
    )(fine_out, lifted, grads, gbias)


def solution(mesh):
    in_specs = (
        P(("gx", "gy"), None),
        P("gy", None),
        P(("gx", "gy")),
        P(("gx", "gy")),
        P("gy", None),
        P("gy"),
        P(),
        P(),
        P(("gx", "gy"), None),
    )
    out_specs = (P(("gx", "gy"), None), P("gy", None), P(), P())
    return jax.shard_map(local, mesh=mesh, in_specs=in_specs, out_specs=out_specs, check_vma=False)
```

```python
import math

import jax
import jax.numpy as jnp
from jax import lax
from jax.experimental import pallas as pl
from jax.experimental.pallas import tpu as pltpu
from jax.sharding import PartitionSpec as P

MESH = pl.DeviceIdType.MESH
F32 = jnp.float32
BF16 = jnp.bfloat16
B = 256
H = 128
UP, DOWN, SAME = (0, 2), (2, 5), (5, 11)
BATCHES = 82
SENDS = 3
UNIT = 4096
RULER = 512
PIECES = 8
GROUPS = (
    ("quick", ("x", "y", "z"), 0, 1),
    ("quick", ("z", "x", "y"), 1, 2),
    ("quick", ("x", "z", "y"), 2, 3),
    ("same", ("y", "x", "z"), 3, 6),
    ("same", ("y", "z", "x"), 6, 12),
    ("fine", ("x", "z", "y"), 12, 15),
    ("fine", ("z", "x", "y"), 15, 18),
)


def dot_plain(a, b):
    return jnp.dot(a, b, preferred_element_type=F32)


def dot_rows(a, b):
    return lax.dot_general(a, b, (((0,), (0,)), ((), ())), preferred_element_type=F32)


def dot_cols(a, b):
    return lax.dot_general(a, b, (((1,), (1,)), ((), ())), preferred_element_type=F32)


def silu_parts(u):
    twice = 1.0 + jnp.tanh(u)
    active = u * twice
    return active, 0.5 * (twice + active * (2.0 - twice))


def row_mean(x):
    return jnp.mean(x, axis=-1, keepdims=True)


def normed(y):
    centred = y - row_mean(y)
    scale = lax.rsqrt(row_mean(centred * centred) + 1e-05)
    return centred * scale, scale


def norm_back(g, unit, scale):
    return scale * (g - row_mean(g) - unit * row_mean(g * unit))


def col_sum(x):
    return jnp.sum(x, axis=0, keepdims=True)


class Batch:
    def __init__(self, sem, ruler):
        self.sem, self.ruler, self.size = sem, ruler, 0

    def wait(self):
        span = self.ruler.at[:self.size // UNIT]
        pltpu.make_async_copy(span, span, self.sem).wait()


class Group:
    def __init__(self, post, place, axes, rows, shared, refs, out):
        self.shared = shared
        self.post, self.place, self.axes, self.rows, self.out = post, place, axes, rows, out
        self.g, self.rc, self.s1, self.r1, self.s2, self.r2, self.s3, self.r3, self.s4 = refs
        self.count = rows.stop - rows.start
        self.step = 0
        self.batch = None

    def put(self, i, value):
        half = value.astype(BF16)
        self.g[0, i] = half[:, :H]
        self.g[1, i] = half[:, H:]

    def send(self, src, dst, device):
        self.batch = self.post(src, dst, device, self.batch)

    def landed(self):
        self.batch.wait()
        self.batch = None

    def advance(self):
        getattr(self, "step%d" % self.step)()
        self.step += 1

    def quarter(self):
        return pl.ds(pl.multiple_of(self.place.at(self.axes[0]) * 64, 64), 64)

    def step0(self):
        other = 1 - self.place.core
        src = self.g.at[other, :, self.quarter(), :] if self.shared else self.g.at[other]
        self.send(src, self.rc, self.place.partner())

    def step1(self):
        self.landed()
        core = self.place.core
        if self.shared:
            for i in range(self.count):
                own = self.g[core, i, self.quarter(), :].astype(F32)
                self.s2[i] = (own + self.rc[i].astype(F32)).astype(BF16)
            self.scatter(self.axes[1], 16, self.s2, self.r2)
            self.step = 2
            return
        for i in range(self.count):
            self.s1[i] = (self.g[core, i].astype(F32) + self.rc[i].astype(F32)).astype(BF16)
        self.scatter(self.axes[0], 64, self.s1, self.r1)

    def scatter(self, axis, size, src, landing):
        at = self.place.at(axis)
        for d in (1, 2, 3):
            to = lax.rem(at + d, 4)
            rows = pl.ds(pl.multiple_of(to * size, size), size)
            self.send(src.at[:, rows, :], landing.at[d - 1], self.place.peer(axis, d))

    def gather_sum(self, axis, size, src, landing, out):
        at = self.place.at(axis)
        rows = pl.ds(pl.multiple_of(at * size, size), size)
        for i in range(self.count):
            total = src[i, rows, :].astype(F32)
            for d in range(3):
                total += landing[d, i].astype(F32)
            out[i] = total.astype(BF16)

    def step2(self):
        self.landed()
        self.gather_sum(self.axes[0], 64, self.s1, self.r1, self.s2)
        self.scatter(self.axes[1], 16, self.s2, self.r2)

    def step3(self):
        self.landed()
        self.gather_sum(self.axes[1], 16, self.s2, self.r2, self.s3)
        self.share(self.axes[2], self.s3, self.r3)

    def share(self, axis, src, slots):
        at = self.place.at(axis)
        for d in (1, 2, 3):
            self.send(src, slots.at[at], self.place.peer(axis, d))
        slots[at] = src[...]

    def slot_sum(self, slots, out):
        for i in range(self.count):
            total = slots[0, i].astype(F32)
            for j in (1, 2, 3):
                total += slots[j, i].astype(F32)
            out[i] = total.astype(BF16)

    def step4(self):
        self.landed()
        self.slot_sum(self.r3, self.s4)
        start = self.place.at(self.axes[0]) * 64 + self.place.at(self.axes[1]) * 16
        rows = pl.ds(pl.multiple_of(start, 16), 16)
        spot = self.out.at[self.place.core, self.rows, rows, :]
        for d in (1, 2, 3):
            self.send(self.s4, spot, self.place.peer(self.axes[1], d))
        for i in range(self.count):
            self.out[self.place.core, self.rows.start + i, rows, :] = self.s4[i]

    def step5(self):
        self.landed()
        spot = self.out.at[self.place.core, self.rows, self.quarter(), :]
        for d in (1, 2, 3):
            self.send(spot, spot, self.place.peer(self.axes[0], d))

    def step6(self):
        self.landed()
        spot = self.out.at[self.place.core, self.rows, :, :]
        self.send(spot, spot, self.place.partner())

    def step7(self):
        self.landed()


class Quick(Group):
    def step2(self):
        self.landed()
        self.gather_sum(self.axes[0], 64, self.s1, self.r1, self.s2)
        self.share(self.axes[1], self.s2, self.r2)

    def step3(self):
        self.landed()
        self.slot_sum(self.r2, self.s3)
        self.share(self.axes[2], self.s3, self.r3)

    def step4(self):
        self.landed()
        self.slot_sum(self.r3, self.s4)
        spot = self.out.at[self.place.core, self.rows, self.quarter(), :]
        for d in (1, 2, 3):
            self.send(self.s4, spot, self.place.peer(self.axes[0], d))
        for i in range(self.count):
            self.out[self.place.core, self.rows.start + i, self.quarter(), :] = self.s4[i]
        self.step = 5


class Place:
    def __init__(self):
        self.gx = lax.axis_index("gx")
        self.gy = lax.axis_index("gy")
        self.core = lax.rem(self.gy, 2)
        self.x = lax.rem(self.gy // 2, 4)
        self.z = self.gy // 8

    def at(self, axis):
        return {"x": self.x, "y": self.gx, "z": self.z}[axis]

    def partner(self):
        return (self.gx, self.gy + 1 - 2 * self.core)

    def peer(self, axis, d):
        if axis == "y":
            return (lax.rem(self.gx + d, 4), self.gy)
        if axis == "x":
            return (self.gx, self.z * 8 + lax.rem(self.x + d, 4) * 2 + self.core)
        return (self.gx, lax.rem(self.z + d, 4) * 8 + self.x * 2 + self.core)

    def beside(self, d):
        return (self.gx, lax.rem(self.gy + d + 32, 32))


def deal(source, raw, index, first, end):
    ways = end - first
    raw[:2 * ways, :] = source[...]
    rows = raw[...]
    lane = lax.broadcasted_iota(jnp.int32, rows.shape, 1)
    for k in range(ways):
        place = lane * ways + k
        picked = jnp.take_along_axis(rows, lax.rem(place, H), axis=1, mode="promise_in_bounds")
        line = place[0:1] // H
        for half in (0, 1):
            row = picked[ways * half:ways * half + 1]
            for i in range(1, ways):
                row = jnp.where(line == i, picked[ways * half + i:ways * half + i + 1], row)
            index[first + k:first + k + 1, half * H:half * H + H] = row


def kernel(total_fine, *refs):
    inputs, (fine_out, lifted_cot, grads, gbias) = refs[:9], refs[9:13]
    (send_sems, recv_sems, onehot, samehot, act, slope, unit, scale, dys, nact, nslope, nunit, nscale,
     table, ext, gtab, pres, csend, crecv, hsend, hback, node_in, bias_acc, bias_core, bias_slots, raw, index, load_sems, summed, own_part, ruler,
     fine, coarse, cot, up_raw, down_raw, halo_raw, same_raw, mats, bias) = refs[13:53]
    group_refs = refs[53:]
    place = Place()
    batches = []
    leaving = []

    def next_sends():
        leaving.append(Batch(send_sems.at[len(leaving)], ruler))

    def post(src, dst, device, batch=None):
        if batch is None:
            batch = Batch(recv_sems.at[len(batches)], ruler)
            batches.append(batch)
        pltpu.make_async_remote_copy(
            src_ref=src, dst_ref=dst, send_sem=leaving[-1].sem, recv_sem=batch.sem,
            device_id=device, device_id_type=MESH,
        ).start()
        size = math.prod(dst.shape) * dst.dtype.itemsize
        assert size % UNIT == 0
        batch.size += size
        leaving[-1].size += size
        return batch

    next_sends()
    loads = []
    for i, (src, dst) in enumerate([
        (inputs[3], up_raw), (inputs[0], fine), (inputs[1], coarse), (inputs[8], bias),
        (inputs[7].at[0, 0:3], mats.at[0, 0:3]), (inputs[4], down_raw), (inputs[6], same_raw), (inputs[5], halo_raw),
        (inputs[7].at[0, 3:6], mats.at[0, 3:6]), (inputs[7].at[2], mats.at[2]), (inputs[7].at[1], mats.at[1]),
        (inputs[2], cot),
    ]):
        loads.append(pltpu.make_async_copy(src, dst, load_sems.at[i]))
    for load in loads[:5]:
        load.start()

    barrier = pltpu.get_barrier_semaphore()
    near = [place.peer(a, d) for a in ("x", "y", "z") for d in (1, 2, 3)]
    near += [place.partner(), place.beside(1), place.beside(-1)]
    for device in near:
        pl.semaphore_signal(barrier, inc=1, device_id=device, device_id_type=MESH)
    for load in loads[5:]:
        load.start()

    groups = [
        (Quick if kind == "quick" else Group)(
            post, place, axes, slice(first, end), kind == "same", group_refs[9 * at:9 * at + 9], grads
        )
        for at, (kind, axes, first, end) in enumerate(GROUPS)
    ]
    edge0, (node0, layer1, layer2a, layer2b) = groups[:3], groups[3:]

    bias_acc[...] = jnp.zeros_like(bias_acc)
    loads[0].wait()
    deal(up_raw, raw, index, *UP)

    def step_on(*groups):
        for group in groups:
            if group.step < 8:
                group.advance()

    def add_bias(row, value):
        bias_acc[row:row + 1, :] += value

    def w(layer, i):
        return mats[layer, i]

    def b(layer, i):
        return bias[layer, i:i + 1, :]

    def hot_rows(block, size):
        nodes = lax.broadcasted_iota(jnp.int32, (size, B), 0)
        return jnp.where(nodes == index[block:block + 1, :], 1.0, 0.0).astype(BF16)

    def edge_forward(block, pre, layer):
        active, slope_now = silu_parts(pre)
        half = active.astype(BF16)
        act[block] = half
        slope[block] = slope_now.astype(BF16)
        message, scale_now = normed(dot_plain(half, w(layer, 2)) + b(layer, 1))
        unit[block] = message.astype(BF16)
        scale[block] = scale_now
        return message

    def edge_backward(block, g, layer):
        dy = norm_back(g, unit[block].astype(F32), scale[block])
        half = dy.astype(BF16)
        dys[block] = half
        dp = slope[block].astype(F32) * dot_cols(half, w(layer, 2))
        return dp, col_sum(dy), col_sum(dp)

    def node_forward(layer, state, agg, pre):
        node_in[layer] = agg
        active, slope_now = silu_parts(0.5 * (pre + dot_plain(agg, w(layer, 4))))
        half = active.astype(BF16)
        nact[layer] = half
        nslope[layer] = slope_now.astype(BF16)
        unit_now, scale_now = normed(dot_plain(half, w(layer, 5)) + b(layer, 3))
        nunit[layer] = unit_now.astype(BF16)
        nscale[layer] = scale_now
        return (state.astype(F32) + unit_now).astype(BF16)

    def node_backward(layer, g, share):
        dz = norm_back(g, nunit[layer].astype(F32), nscale[layer])
        dz16 = dz.astype(BF16)
        dq = nslope[layer].astype(F32) * dot_cols(dz16, w(layer, 5))
        dq16 = dq.astype(BF16)
        add_bias(4 * layer + 3, share * col_sum(dz))
        add_bias(4 * layer + 2, share * col_sum(dq))
        return dz16, dq16

    def piece(i):
        return pl.ds(i * (H // PIECES), H // PIECES)

    def sum_start(first, value):
        half = value.astype(BF16)
        csend[first, 0] = half[:H]
        csend[first, 1] = half[H:]
        odd = lax.rem(place.gx, 2)
        one = (place.gx + 1 - 2 * odd, place.gy)
        two = (lax.rem(place.gx + 2 * odd + 3, 4), place.gy)
        waits = []
        for i in range(PIECES):
            batch = None
            for side, device in ((0, one), (1, two)):
                batch = post(csend.at[first, side, piece(i)], crecv.at[first, side, piece(i)], device, batch)
            waits.append(batch)
        return waits, one, two

    def add_piece(at, i, side):
        both = csend[at, side, piece(i)].astype(F32) + crecv[at, side, piece(i)].astype(F32)
        return both.astype(BF16)

    def sum_middle(first, state):
        waits, one, two = state
        later = []
        for i in range(PIECES):
            waits[i].wait()
            batch = None
            for side, device in ((0, two), (1, one)):
                csend[first + 1, side, piece(i)] = add_piece(first, i, side)
                batch = post(csend.at[first + 1, side, piece(i)], crecv.at[first + 1, side, piece(i)], device, batch)
            later.append(batch)
        return later

    def sum_end(first, waits):
        for i in range(PIECES):
            waits[i].wait()
            for side in (0, 1):
                summed[side, piece(i)] = add_piece(first + 1, i, side)
        return summed[...].reshape(B, B)

    for block in range(*UP):
        onehot[block] = hot_rows(block, B)
    for load in loads[1:5]:
        load.wait()
    sent = 0.5 * (dot_plain(fine[...], w(0, 0)) + b(0, 0))
    table[...] = (0.5 * dot_plain(coarse[...], w(0, 1))).astype(BF16)
    up_sum = None
    for block in range(*UP):
        message = edge_forward(block, sent + dot_rows(onehot[block], table[...]), 0)
        part = dot_plain(onehot[block], message.astype(BF16))
        up_sum = part if up_sum is None else up_sum + part

    pl.semaphore_wait(barrier, len(near))
    state = sum_start(0, up_sum)
    for load in loads[5:]:
        load.wait()
    pres[0] = dot_plain(coarse[...], w(0, 3)) + b(0, 2)
    deal(down_raw, raw, index, *DOWN)
    deal(same_raw, raw, index, *SAME)
    place_in = index[SAME[0]:SAME[1], :]
    moved = jnp.where(place_in < H, place_in + B, place_in - H)
    index[SAME[0]:SAME[1], :] = jnp.where(place_in < H + B, moved, place_in)
    index[11:12, :H] = halo_raw[0:1, :]
    index[11:12, H:] = halo_raw[1:2, :]
    for block in range(*DOWN):
        onehot[block] = hot_rows(block, B)
    onehot[5] = hot_rows(11, B)
    state = sum_middle(0, state)
    for block in range(*SAME):
        samehot[block - 5] = hot_rows(block, 2 * B)
    pres[1] = dot_plain(fine[...], w(2, 3)) + b(2, 2)
    pres[2] = 0.5 * (dot_plain(fine[...], w(2, 1)) + b(2, 0))
    agg = sum_end(0, state)
    lifted = node_forward(0, coarse[...], agg, pres[0])
    ext[:B] = lifted
    payload = dot_rows(onehot[5], lifted).astype(BF16)
    hsend[0] = payload[:H]
    hsend[1] = payload[H:]
    halo = post(hsend.at[0], ext.at[B + H:], place.beside(-1))
    post(hsend.at[1], ext.at[B:B + H], place.beside(1), halo)

    pres[3] = 0.5 * (dot_plain(lifted, w(1, 1)) + b(1, 0))
    gtab[:B] = (0.5 * dot_plain(lifted, w(1, 0))).astype(BF16)
    for block in range(*SAME):
        own_part[block - 5] = pres[3] + dot_rows(samehot[block - 5, :B], gtab[:B])
    pres[4] = dot_plain(lifted, w(1, 3)) + b(1, 2)
    halo.wait()
    gtab[B:] = (0.5 * dot_plain(ext[B:], w(1, 0))).astype(BF16)
    same_sum = None
    for block in range(*SAME):
        message = edge_forward(
            block, own_part[block - 5] + dot_rows(samehot[block - 5, B:], gtab[B:]), 1
        )
        same_sum = message if same_sum is None else same_sum + message
    mixed = node_forward(1, ext[:B], same_sum.astype(BF16), pres[4])
    nact[3] = mixed

    table[...] = (0.5 * dot_plain(mixed, w(2, 0))).astype(BF16)
    down_sum = None
    for block in range(*DOWN):
        message = edge_forward(block, pres[2] + dot_rows(onehot[block], table[...]), 2)
        down_sum = message if down_sum is None else down_sum + message
    fine_out[...] = node_forward(2, fine[...], down_sum.astype(BF16), pres[1])
    dz2, dq2 = node_backward(2, cot[...].astype(F32) * (1.0 / math.sqrt(total_fine)), 1.0)
    g = dot_cols(dq2, w(2, 4))
    taken = back = None
    for block in range(*DOWN):
        dp, db2, db1 = edge_backward(block, g, 2)
        add_bias(8, db1)
        add_bias(9, db2)
        part = dot_plain(onehot[block], dp.astype(BF16))
        taken = dp if taken is None else taken + dp
        back = part if back is None else back + part
    state = sum_start(2, back)
    layer2a.put(1, dot_rows(fine[...], taken.astype(BF16)))
    layer2a.put(2, dot_rows(act[2:5].reshape(3 * B, B), dys[2:5].reshape(3 * B, B)))
    state = sum_middle(2, state)
    layer2b.put(0, dot_rows(fine[...], dq2))
    layer2b.put(1, dot_rows(node_in[2], dq2))
    layer2b.put(2, dot_rows(nact[2], dz2))
    sent_half = sum_end(2, state)
    grad_mixed = dot_cols(sent_half, w(2, 0))
    layer2a.put(0, 0.25 * dot_rows(nact[3], sent_half))
    step_on(layer2a, layer2b)

    dz1, dq1 = node_backward(1, grad_mixed, 0.25)
    pres[0] = grad_mixed + dot_cols(dq1, w(1, 3))
    g = dot_cols(dq1, w(1, 4))
    taken = back = None
    for block in range(*SAME):
        dp, db2, db1 = edge_backward(block, g, 1)
        add_bias(4, 0.25 * db1)
        add_bias(5, 0.25 * db2)
        part = dot_plain(samehot[block - 5], dp.astype(BF16))
        taken = dp if taken is None else taken + dp
        back = part if back is None else back + part
    hsend[2] = back[B:B + H].astype(BF16)
    hsend[3] = back[B + H:].astype(BF16)
    returns = post(hsend.at[2], hback.at[1], place.beside(-1))
    post(hsend.at[3], hback.at[0], place.beside(1), returns)
    own = back[:B]
    step_on(layer2a, layer2b)
    lifted = ext[:B]
    taken_half = taken.astype(BF16)
    layer1.put(1, 1.0 * dot_rows(lifted, taken_half))
    layer1.put(2, dot_rows(act[5:11].reshape(6 * B, B), dys[5:11].reshape(6 * B, B)))
    layer1.put(3, dot_rows(lifted, dq1))
    layer1.put(4, dot_rows(node_in[1], dq1))
    layer1.put(5, dot_rows(nact[1], dz1))
    grad_lifted = pres[0] + dot_cols(taken_half, w(1, 1))
    returns.wait()
    next_sends()
    own += dot_plain(onehot[5], hback[...].reshape(B, B))
    own_half = own.astype(BF16)
    grad_lifted += dot_cols(own_half, w(1, 0))
    lifted_cot[...] = grad_lifted * math.sqrt(total_fine)
    layer1.put(0, dot_rows(lifted, own_half))
    step_on(layer1)

    dz0, dq0 = node_backward(0, grad_lifted, 0.25)
    table[...] = dot_cols(dq0, w(0, 4)).astype(BF16)
    taken = back = None
    for block in range(*UP):
        if block == UP[1] - 1:
            step_on(layer2a, layer2b, layer1)
        dp, db2, db1 = edge_backward(block, dot_rows(onehot[block], table[...]), 0)
        add_bias(0, db1)
        add_bias(1, db2)
        part = dot_plain(onehot[block], dp.astype(BF16))
        taken = dp if taken is None else taken + dp
        back = part if back is None else back + part
    edge0[0].put(0, dot_rows(fine[...], taken.astype(BF16)))
    edge0[1].put(0, dot_rows(coarse[...], back.astype(BF16)))
    edge0[2].put(0, dot_rows(act[0:2].reshape(2 * B, B), dys[0:2].reshape(2 * B, B)))
    step_on(*edge0)
    bias_batch = [post(bias_acc, bias_core, place.partner())]
    node0.put(0, dot_rows(coarse[...], dq0))
    node0.put(1, dot_rows(node_in[0], dq0))
    node0.put(2, dot_rows(nact[0], dz0))
    step_on(node0)

    def bias_step(step):
        bias_batch.pop().wait()
        batch = None
        if step == 0:
            total = bias_acc[...] + bias_core[...]
        else:
            total = bias_slots[step - 1, 0] + bias_slots[step - 1, 1]
            total = total + bias_slots[step - 1, 2] + bias_slots[step - 1, 3]
        if step == 3:
            gbias[...] = total
            return
        axis = "yxz"[step]
        at = place.at(axis)
        bias_slots[step, at] = total
        for d in (1, 2, 3):
            spot = bias_slots.at[step, at]
            batch = post(spot, spot, place.peer(axis, d), batch)
        bias_batch.append(batch)

    for step in range(6):
        step_on(*edge0, node0, layer1, layer2a, layer2b)
        if step < 4:
            bias_step(step)
        if step == 2:
            leaving[0].wait()
            next_sends()
        if step == 3:
            leaving[1].wait()
    assert all(group.step == 8 for group in groups)
    leaving[2].wait()
    assert len(batches) == BATCHES and len(leaving) == SENDS
    assert max(batch.size for batch in batches + leaving) <= RULER * UNIT


def finish(fine_in, lifted_in, grads, gbias, fine_out, lifted_out, matrices_out, biases_out, wide, sems):
    copies = [
        pltpu.make_async_copy(fine_in, fine_out, sems.at[3]),
        pltpu.make_async_copy(lifted_in, lifted_out, sems.at[4]),
    ]
    for copy in copies:
        copy.start()
    for i in range(18):
        layer = i // 6
        wide[i, :, :H] = grads[0, i].astype(F32)
        wide[i, :, H:] = grads[1, i].astype(F32)
        pltpu.make_async_copy(wide.at[i], matrices_out.at[layer, i % 6], sems.at[layer]).start()
    for layer in range(3):
        biases_out[layer] = gbias[4 * layer:4 * layer + 4, :]
        copies.append(pltpu.make_async_copy(wide.at[6 * layer:6 * layer + 6], matrices_out.at[layer], sems.at[layer]))
    for copy in copies:
        copy.wait()


def group_scratch(kind, count):
    whole = 64 if kind == "same" else B
    spare = 16 if kind == "same" else B
    small = 64 if kind == "quick" else 16
    slots = 4 if kind == "quick" else 3
    return [
        pltpu.VMEM((2, count, B, H), BF16),
        pltpu.VMEM((count, whole, H), BF16),
        pltpu.VMEM((count, spare, H), BF16),
        pltpu.VMEM((3, count, spare // 4, H), BF16),
        pltpu.VMEM((count, 64, H), BF16),
        pltpu.VMEM((slots, count, small, H), BF16),
        pltpu.VMEM((count, small, H), BF16),
        pltpu.VMEM((4, count, small, H), BF16),
        pltpu.VMEM((count, small, H), BF16),
    ]


def local(fine_state, coarse_state, up_target, down_source, halo_lists, same_source, matrices, biases, fine_cotangent):
    total_fine = fine_state.shape[0] * lax.axis_size("gx") * lax.axis_size("gy")
    scratch = [
        pltpu.SemaphoreType.DMA((SENDS,)),
        pltpu.SemaphoreType.DMA((BATCHES,)),
        pltpu.VMEM((6, B, B), BF16),
        pltpu.VMEM((6, 2 * B, B), BF16),
        pltpu.VMEM((11, B, B), BF16),
        pltpu.VMEM((11, B, B), BF16),
        pltpu.VMEM((11, B, B), BF16),
        pltpu.VMEM((11, B, 1), F32),
        pltpu.VMEM((11, B, B), BF16),
        pltpu.VMEM((4, B, B), BF16),
        pltpu.VMEM((3, B, B), BF16),
        pltpu.VMEM((3, B, B), BF16),
        pltpu.VMEM((3, B, 1), F32),
        pltpu.VMEM((B, B), BF16),
        pltpu.VMEM((2 * B, B), BF16),
        pltpu.VMEM((2 * B, B), BF16),
        pltpu.VMEM((5, B, B), F32),
        pltpu.VMEM((4, 2, H, B), BF16),
        pltpu.VMEM((4, 2, H, B), BF16),
        pltpu.VMEM((4, H, B), BF16),
        pltpu.VMEM((2, H, B), BF16),
        pltpu.VMEM((3, B, B), BF16),
        pltpu.VMEM((16, B), F32),
        pltpu.VMEM((16, B), F32),
        pltpu.VMEM((3, 4, 16, B), F32),
        pltpu.VMEM((16, H), jnp.int32),
        pltpu.VMEM((16, B), jnp.int32),
        pltpu.SemaphoreType.DMA((12,)),
        pltpu.VMEM((2, H, B), BF16),
        pltpu.VMEM((6, B, B), F32),
        pltpu.VMEM((RULER, 16, H), BF16),
        pltpu.VMEM((B, B), BF16),
        pltpu.VMEM((B, B), BF16),
        pltpu.VMEM((B, B), BF16),
        pltpu.VMEM((4, H), jnp.int32),
        pltpu.VMEM((6, H), jnp.int32),
        pltpu.VMEM((2, H), jnp.int32),
        pltpu.VMEM((12, H), jnp.int32),
        pltpu.VMEM((3, 6, B, B), BF16),
        pltpu.VMEM((3, 4, B), F32),
    ]
    for kind, _, first, end in GROUPS:
        scratch += group_scratch(kind, end - first)
    vmem = pl.BlockSpec(memory_space=pltpu.VMEM)

    def body(*refs):
        kernel(total_fine, *refs)

    fine_out, lifted, grads, gbias = pl.pallas_call(
        body,
        out_shape=(
            jax.ShapeDtypeStruct((B, B), BF16),
            jax.ShapeDtypeStruct((B, B), F32),
            jax.ShapeDtypeStruct((2, 18, B, H), BF16),
            jax.ShapeDtypeStruct((16, B), F32),
        ),
        in_specs=[pl.BlockSpec(memory_space=pltpu.HBM)] * 9,
        out_specs=(vmem,) * 4,
        scratch_shapes=scratch,
        compiler_params=pltpu.CompilerParams(
            collective_id=0, has_side_effects=True, vmem_limit_bytes=32 << 20
        ),
        name="sweep",
    )(*[
        pltpu.with_memory_space_constraint(value, pltpu.HBM)
        for value in (
            fine_state, coarse_state, fine_cotangent, up_target.reshape(4, H), down_source.reshape(6, H), halo_lists,
            same_source.reshape(12, H), matrices, biases,
        )
    ])
    hbm = pl.BlockSpec(memory_space=pl.ANY)
    return pl.pallas_call(
        finish,
        out_shape=(
            jax.ShapeDtypeStruct((B, B), BF16),
            jax.ShapeDtypeStruct((B, B), F32),
            jax.ShapeDtypeStruct((3, 6, B, B), F32),
            jax.ShapeDtypeStruct((3, 4, B), F32),
        ),
        in_specs=[vmem] * 4,
        out_specs=(hbm, hbm, hbm, vmem),
        scratch_shapes=[pltpu.VMEM((18, B, B), F32), pltpu.SemaphoreType.DMA((5,))],
        compiler_params=pltpu.CompilerParams(vmem_limit_bytes=16 << 20),
        name="finish",
    )(fine_out, lifted, grads, gbias)


def solution(mesh):
    in_specs = (
        P(("gx", "gy"), None),
        P("gy", None),
        P(("gx", "gy")),
        P(("gx", "gy")),
        P("gy", None),
        P("gy"),
        P(),
        P(),
        P(("gx", "gy"), None),
    )
    out_specs = (P(("gx", "gy"), None), P("gy", None), P(), P())
    return jax.shard_map(local, mesh=mesh, in_specs=in_specs, out_specs=out_specs, check_vma=False)
```

```python
import math

import jax
import jax.numpy as jnp
from jax import lax
from jax.experimental import pallas as pl
from jax.experimental.pallas import tpu as pltpu
from jax.sharding import PartitionSpec as P

MESH = pl.DeviceIdType.MESH
F32 = jnp.float32
BF16 = jnp.bfloat16
B = 256
H = 128
UP, DOWN, SAME = (0, 2), (2, 5), (5, 11)
BATCHES = 82
SENDS = 3
UNIT = 4096
RULER = 512
PIECES = 8
GROUPS = (
    ("quick", ("x", "y", "z"), 0, 1),
    ("quick", ("z", "x", "y"), 1, 2),
    ("quick", ("x", "z", "y"), 2, 3),
    ("same", ("y", "x", "z"), 3, 6),
    ("same", ("y", "z", "x"), 6, 12),
    ("fine", ("x", "z", "y"), 12, 15),
    ("fine", ("z", "x", "y"), 15, 18),
)


def dot_plain(a, b):
    return jnp.dot(a, b, preferred_element_type=F32)


def dot_rows(a, b):
    return lax.dot_general(a, b, (((0,), (0,)), ((), ())), preferred_element_type=F32)


def dot_cols(a, b):
    return lax.dot_general(a, b, (((1,), (1,)), ((), ())), preferred_element_type=F32)


def silu_parts(x):
    gate = 0.5 * jnp.tanh(0.5 * x) + 0.5
    active = x * gate
    return active, gate + active * (1.0 - gate)


def row_mean(x):
    return jnp.mean(x, axis=-1, keepdims=True)


def normed(y):
    centred = y - row_mean(y)
    scale = lax.rsqrt(row_mean(centred * centred) + 1e-05)
    return centred * scale, scale


def norm_back(g, unit, scale):
    return scale * (g - row_mean(g) - unit * row_mean(g * unit))


def col_sum(x):
    return jnp.sum(x, axis=0, keepdims=True)


class Batch:
    def __init__(self, sem, ruler):
        self.sem, self.ruler, self.size = sem, ruler, 0

    def wait(self):
        span = self.ruler.at[:self.size // UNIT]
        pltpu.make_async_copy(span, span, self.sem).wait()


class Group:
    def __init__(self, post, place, axes, rows, shared, refs, out):
        self.shared = shared
        self.post, self.place, self.axes, self.rows, self.out = post, place, axes, rows, out
        self.g, self.rc, self.s1, self.r1, self.s2, self.r2, self.s3, self.r3, self.s4 = refs
        self.count = rows.stop - rows.start
        self.step = 0
        self.batch = None

    def put(self, i, value):
        half = value.astype(BF16)
        self.g[0, i] = half[:, :H]
        self.g[1, i] = half[:, H:]

    def send(self, src, dst, device):
        self.batch = self.post(src, dst, device, self.batch)

    def landed(self):
        self.batch.wait()
        self.batch = None

    def advance(self):
        getattr(self, "step%d" % self.step)()
        self.step += 1

    def quarter(self):
        return pl.ds(pl.multiple_of(self.place.at(self.axes[0]) * 64, 64), 64)

    def step0(self):
        other = 1 - self.place.core
        src = self.g.at[other, :, self.quarter(), :] if self.shared else self.g.at[other]
        self.send(src, self.rc, self.place.partner())

    def step1(self):
        self.landed()
        core = self.place.core
        if self.shared:
            for i in range(self.count):
                own = self.g[core, i, self.quarter(), :].astype(F32)
                self.s2[i] = (own + self.rc[i].astype(F32)).astype(BF16)
            self.scatter(self.axes[1], 16, self.s2, self.r2)
            self.step = 2
            return
        for i in range(self.count):
            self.s1[i] = (self.g[core, i].astype(F32) + self.rc[i].astype(F32)).astype(BF16)
        self.scatter(self.axes[0], 64, self.s1, self.r1)

    def scatter(self, axis, size, src, landing):
        at = self.place.at(axis)
        for d in (1, 2, 3):
            to = lax.rem(at + d, 4)
            rows = pl.ds(pl.multiple_of(to * size, size), size)
            self.send(src.at[:, rows, :], landing.at[d - 1], self.place.peer(axis, d))

    def gather_sum(self, axis, size, src, landing, out):
        at = self.place.at(axis)
        rows = pl.ds(pl.multiple_of(at * size, size), size)
        for i in range(self.count):
            total = src[i, rows, :].astype(F32)
            for d in range(3):
                total += landing[d, i].astype(F32)
            out[i] = total.astype(BF16)

    def step2(self):
        self.landed()
        self.gather_sum(self.axes[0], 64, self.s1, self.r1, self.s2)
        self.scatter(self.axes[1], 16, self.s2, self.r2)

    def step3(self):
        self.landed()
        self.gather_sum(self.axes[1], 16, self.s2, self.r2, self.s3)
        self.share(self.axes[2], self.s3, self.r3)

    def share(self, axis, src, slots):
        at = self.place.at(axis)
        for d in (1, 2, 3):
            self.send(src, slots.at[at], self.place.peer(axis, d))
        slots[at] = src[...]

    def slot_sum(self, slots, out):
        for i in range(self.count):
            total = slots[0, i].astype(F32)
            for j in (1, 2, 3):
                total += slots[j, i].astype(F32)
            out[i] = total.astype(BF16)

    def step4(self):
        self.landed()
        self.slot_sum(self.r3, self.s4)
        start = self.place.at(self.axes[0]) * 64 + self.place.at(self.axes[1]) * 16
        rows = pl.ds(pl.multiple_of(start, 16), 16)
        spot = self.out.at[self.place.core, self.rows, rows, :]
        for d in (1, 2, 3):
            self.send(self.s4, spot, self.place.peer(self.axes[1], d))
        for i in range(self.count):
            self.out[self.place.core, self.rows.start + i, rows, :] = self.s4[i]

    def step5(self):
        self.landed()
        spot = self.out.at[self.place.core, self.rows, self.quarter(), :]
        for d in (1, 2, 3):
            self.send(spot, spot, self.place.peer(self.axes[0], d))

    def step6(self):
        self.landed()
        spot = self.out.at[self.place.core, self.rows, :, :]
        self.send(spot, spot, self.place.partner())

    def step7(self):
        self.landed()


class Quick(Group):
    def step2(self):
        self.landed()
        self.gather_sum(self.axes[0], 64, self.s1, self.r1, self.s2)
        self.share(self.axes[1], self.s2, self.r2)

    def step3(self):
        self.landed()
        self.slot_sum(self.r2, self.s3)
        self.share(self.axes[2], self.s3, self.r3)

    def step4(self):
        self.landed()
        self.slot_sum(self.r3, self.s4)
        spot = self.out.at[self.place.core, self.rows, self.quarter(), :]
        for d in (1, 2, 3):
            self.send(self.s4, spot, self.place.peer(self.axes[0], d))
        for i in range(self.count):
            self.out[self.place.core, self.rows.start + i, self.quarter(), :] = self.s4[i]
        self.step = 5


class Place:
    def __init__(self):
        self.gx = lax.axis_index("gx")
        self.gy = lax.axis_index("gy")
        self.core = lax.rem(self.gy, 2)
        self.x = lax.rem(self.gy // 2, 4)
        self.z = self.gy // 8

    def at(self, axis):
        return {"x": self.x, "y": self.gx, "z": self.z}[axis]

    def partner(self):
        return (self.gx, self.gy + 1 - 2 * self.core)

    def peer(self, axis, d):
        if axis == "y":
            return (lax.rem(self.gx + d, 4), self.gy)
        if axis == "x":
            return (self.gx, self.z * 8 + lax.rem(self.x + d, 4) * 2 + self.core)
        return (self.gx, lax.rem(self.z + d, 4) * 8 + self.x * 2 + self.core)

    def beside(self, d):
        return (self.gx, lax.rem(self.gy + d + 32, 32))


def deal(source, raw, index, first, end):
    ways = end - first
    raw[:2 * ways, :] = source[...]
    rows = raw[...]
    lane = lax.broadcasted_iota(jnp.int32, rows.shape, 1)
    for k in range(ways):
        place = lane * ways + k
        picked = jnp.take_along_axis(rows, lax.rem(place, H), axis=1, mode="promise_in_bounds")
        line = place[0:1] // H
        for half in (0, 1):
            row = picked[ways * half:ways * half + 1]
            for i in range(1, ways):
                row = jnp.where(line == i, picked[ways * half + i:ways * half + i + 1], row)
            index[first + k:first + k + 1, half * H:half * H + H] = row


def kernel(total_fine, *refs):
    inputs, (fine_out, lifted_cot, grads, gbias) = refs[:9], refs[9:13]
    (send_sems, recv_sems, onehot, samehot, act, slope, unit, scale, dys, nact, nslope, nunit, nscale,
     table, ext, gtab, pres, csend, crecv, hsend, hback, node_in, bias_acc, bias_core, bias_slots, raw, index, load_sems, summed, own_part, ruler,
     fine, coarse, cot, up_raw, down_raw, halo_raw, same_raw, mats, bias) = refs[13:53]
    group_refs = refs[53:]
    place = Place()
    batches = []
    leaving = []

    def next_sends():
        leaving.append(Batch(send_sems.at[len(leaving)], ruler))

    def post(src, dst, device, batch=None):
        if batch is None:
            batch = Batch(recv_sems.at[len(batches)], ruler)
            batches.append(batch)
        pltpu.make_async_remote_copy(
            src_ref=src, dst_ref=dst, send_sem=leaving[-1].sem, recv_sem=batch.sem,
            device_id=device, device_id_type=MESH,
        ).start()
        size = math.prod(dst.shape) * dst.dtype.itemsize
        assert size % UNIT == 0
        batch.size += size
        leaving[-1].size += size
        return batch

    next_sends()
    loads = []
    for i, (src, dst) in enumerate([
        (inputs[3], up_raw), (inputs[0], fine), (inputs[1], coarse), (inputs[8], bias),
        (inputs[7].at[0, 0:3], mats.at[0, 0:3]), (inputs[4], down_raw), (inputs[6], same_raw), (inputs[5], halo_raw),
        (inputs[7].at[0, 3:6], mats.at[0, 3:6]), (inputs[7].at[2], mats.at[2]), (inputs[7].at[1], mats.at[1]),
        (inputs[2], cot),
    ]):
        loads.append(pltpu.make_async_copy(src, dst, load_sems.at[i]))
    for load in loads[:5]:
        load.start()

    barrier = pltpu.get_barrier_semaphore()
    near = [place.peer(a, d) for a in ("x", "y", "z") for d in (1, 2, 3)]
    near += [place.partner(), place.beside(1), place.beside(-1)]
    for device in near:
        pl.semaphore_signal(barrier, inc=1, device_id=device, device_id_type=MESH)
    for load in loads[5:]:
        load.start()

    groups = [
        (Quick if kind == "quick" else Group)(
            post, place, axes, slice(first, end), kind == "same", group_refs[9 * at:9 * at + 9], grads
        )
        for at, (kind, axes, first, end) in enumerate(GROUPS)
    ]
    edge0, (node0, layer1, layer2a, layer2b) = groups[:3], groups[3:]

    bias_acc[...] = jnp.zeros_like(bias_acc)
    loads[0].wait()
    deal(up_raw, raw, index, *UP)

    def step_on(*groups):
        for group in groups:
            if group.step < 8:
                group.advance()

    def add_bias(row, value):
        bias_acc[row:row + 1, :] += value

    def w(layer, i):
        return mats[layer, i]

    def b(layer, i):
        return bias[layer, i:i + 1, :]

    def hot_rows(block, size):
        nodes = lax.broadcasted_iota(jnp.int32, (size, B), 0)
        return jnp.where(nodes == index[block:block + 1, :], 1.0, 0.0).astype(BF16)

    def edge_forward(block, pre, layer):
        active, slope_now = silu_parts(pre)
        half = active.astype(BF16)
        act[block] = half
        slope[block] = slope_now.astype(BF16)
        message, scale_now = normed(dot_plain(half, w(layer, 2)) + b(layer, 1))
        unit[block] = message.astype(BF16)
        scale[block] = scale_now
        return message

    def edge_backward(block, g, layer):
        dy = norm_back(g, unit[block].astype(F32), scale[block])
        half = dy.astype(BF16)
        dys[block] = half
        dp = slope[block].astype(F32) * dot_cols(half, w(layer, 2))
        return dp, col_sum(dy), col_sum(dp)

    def node_forward(layer, state, agg, pre):
        node_in[layer] = agg
        active, slope_now = silu_parts(pre + dot_plain(agg, w(layer, 4)))
        half = active.astype(BF16)
        nact[layer] = half
        nslope[layer] = slope_now.astype(BF16)
        unit_now, scale_now = normed(dot_plain(half, w(layer, 5)) + b(layer, 3))
        nunit[layer] = unit_now.astype(BF16)
        nscale[layer] = scale_now
        return (state.astype(F32) + unit_now).astype(BF16)

    def node_backward(layer, g, share):
        dz = norm_back(g, nunit[layer].astype(F32), nscale[layer])
        dz16 = dz.astype(BF16)
        dq = nslope[layer].astype(F32) * dot_cols(dz16, w(layer, 5))
        dq16 = dq.astype(BF16)
        add_bias(4 * layer + 3, share * col_sum(dz))
        add_bias(4 * layer + 2, share * col_sum(dq))
        return dz16, dq16

    def piece(i):
        return pl.ds(i * (H // PIECES), H // PIECES)

    def sum_start(first, value):
        half = value.astype(BF16)
        csend[first, 0] = half[:H]
        csend[first, 1] = half[H:]
        odd = lax.rem(place.gx, 2)
        one = (place.gx + 1 - 2 * odd, place.gy)
        two = (lax.rem(place.gx + 2 * odd + 3, 4), place.gy)
        waits = []
        for i in range(PIECES):
            batch = None
            for side, device in ((0, one), (1, two)):
                batch = post(csend.at[first, side, piece(i)], crecv.at[first, side, piece(i)], device, batch)
            waits.append(batch)
        return waits, one, two

    def add_piece(at, i, side):
        both = csend[at, side, piece(i)].astype(F32) + crecv[at, side, piece(i)].astype(F32)
        return both.astype(BF16)

    def sum_middle(first, state):
        waits, one, two = state
        later = []
        for i in range(PIECES):
            waits[i].wait()
            batch = None
            for side, device in ((0, two), (1, one)):
                csend[first + 1, side, piece(i)] = add_piece(first, i, side)
                batch = post(csend.at[first + 1, side, piece(i)], crecv.at[first + 1, side, piece(i)], device, batch)
            later.append(batch)
        return later

    def sum_end(first, waits):
        for i in range(PIECES):
            waits[i].wait()
            for side in (0, 1):
                summed[side, piece(i)] = add_piece(first + 1, i, side)
        return summed[...].reshape(B, B)

    for block in range(*UP):
        onehot[block] = hot_rows(block, B)
    for load in loads[1:5]:
        load.wait()
    sent = dot_plain(fine[...], w(0, 0)) + b(0, 0)
    table[...] = dot_plain(coarse[...], w(0, 1)).astype(BF16)
    up_sum = None
    for block in range(*UP):
        message = edge_forward(block, sent + dot_rows(onehot[block], table[...]), 0)
        part = dot_plain(onehot[block], message.astype(BF16))
        up_sum = part if up_sum is None else up_sum + part

    pl.semaphore_wait(barrier, len(near))
    state = sum_start(0, up_sum)
    for load in loads[5:]:
        load.wait()
    pres[0] = dot_plain(coarse[...], w(0, 3)) + b(0, 2)
    deal(down_raw, raw, index, *DOWN)
    deal(same_raw, raw, index, *SAME)
    place_in = index[SAME[0]:SAME[1], :]
    moved = jnp.where(place_in < H, place_in + B, place_in - H)
    index[SAME[0]:SAME[1], :] = jnp.where(place_in < H + B, moved, place_in)
    index[11:12, :H] = halo_raw[0:1, :]
    index[11:12, H:] = halo_raw[1:2, :]
    for block in range(*DOWN):
        onehot[block] = hot_rows(block, B)
    onehot[5] = hot_rows(11, B)
    state = sum_middle(0, state)
    for block in range(*SAME):
        samehot[block - 5] = hot_rows(block, 2 * B)
    pres[1] = dot_plain(fine[...], w(2, 3)) + b(2, 2)
    pres[2] = dot_plain(fine[...], w(2, 1)) + b(2, 0)
    agg = sum_end(0, state)
    lifted = node_forward(0, coarse[...], agg, pres[0])
    ext[:B] = lifted
    payload = dot_rows(onehot[5], lifted).astype(BF16)
    hsend[0] = payload[:H]
    hsend[1] = payload[H:]
    halo = post(hsend.at[0], ext.at[B + H:], place.beside(-1))
    post(hsend.at[1], ext.at[B:B + H], place.beside(1), halo)

    pres[3] = dot_plain(lifted, w(1, 1)) + b(1, 0)
    gtab[:B] = dot_plain(lifted, w(1, 0)).astype(BF16)
    for block in range(*SAME):
        own_part[block - 5] = pres[3] + dot_rows(samehot[block - 5, :B], gtab[:B])
    pres[4] = dot_plain(lifted, w(1, 3)) + b(1, 2)
    halo.wait()
    gtab[B:] = dot_plain(ext[B:], w(1, 0)).astype(BF16)
    same_sum = None
    for block in range(*SAME):
        message = edge_forward(
            block, own_part[block - 5] + dot_rows(samehot[block - 5, B:], gtab[B:]), 1
        )
        same_sum = message if same_sum is None else same_sum + message
    mixed = node_forward(1, ext[:B], same_sum.astype(BF16), pres[4])
    nact[3] = mixed

    table[...] = dot_plain(mixed, w(2, 0)).astype(BF16)
    down_sum = None
    for block in range(*DOWN):
        message = edge_forward(block, pres[2] + dot_rows(onehot[block], table[...]), 2)
        down_sum = message if down_sum is None else down_sum + message
    fine_out[...] = node_forward(2, fine[...], down_sum.astype(BF16), pres[1])
    dz2, dq2 = node_backward(2, cot[...].astype(F32) * (1.0 / math.sqrt(total_fine)), 1.0)
    g = dot_cols(dq2, w(2, 4))
    taken = back = None
    for block in range(*DOWN):
        dp, db2, db1 = edge_backward(block, g, 2)
        add_bias(8, db1)
        add_bias(9, db2)
        part = dot_plain(onehot[block], dp.astype(BF16))
        taken = dp if taken is None else taken + dp
        back = part if back is None else back + part
    state = sum_start(2, back)
    layer2a.put(1, dot_rows(fine[...], taken.astype(BF16)))
    layer2a.put(2, dot_rows(act[2:5].reshape(3 * B, B), dys[2:5].reshape(3 * B, B)))
    state = sum_middle(2, state)
    layer2b.put(0, dot_rows(fine[...], dq2))
    layer2b.put(1, dot_rows(node_in[2], dq2))
    layer2b.put(2, dot_rows(nact[2], dz2))
    sent_half = sum_end(2, state)
    grad_mixed = dot_cols(sent_half, w(2, 0))
    layer2a.put(0, 0.25 * dot_rows(nact[3], sent_half))
    step_on(layer2a, layer2b)

    dz1, dq1 = node_backward(1, grad_mixed, 0.25)
    pres[0] = grad_mixed + dot_cols(dq1, w(1, 3))
    g = dot_cols(dq1, w(1, 4))
    taken = back = None
    for block in range(*SAME):
        dp, db2, db1 = edge_backward(block, g, 1)
        add_bias(4, 0.25 * db1)
        add_bias(5, 0.25 * db2)
        part = dot_plain(samehot[block - 5], dp.astype(BF16))
        taken = dp if taken is None else taken + dp
        back = part if back is None else back + part
    hsend[2] = back[B:B + H].astype(BF16)
    hsend[3] = back[B + H:].astype(BF16)
    returns = post(hsend.at[2], hback.at[1], place.beside(-1))
    post(hsend.at[3], hback.at[0], place.beside(1), returns)
    own = back[:B]
    step_on(layer2a, layer2b)
    lifted = ext[:B]
    taken_half = taken.astype(BF16)
    layer1.put(1, 1.0 * dot_rows(lifted, taken_half))
    layer1.put(2, dot_rows(act[5:11].reshape(6 * B, B), dys[5:11].reshape(6 * B, B)))
    layer1.put(3, dot_rows(lifted, dq1))
    layer1.put(4, dot_rows(node_in[1], dq1))
    layer1.put(5, dot_rows(nact[1], dz1))
    grad_lifted = pres[0] + dot_cols(taken_half, w(1, 1))
    returns.wait()
    next_sends()
    own += dot_plain(onehot[5], hback[...].reshape(B, B))
    own_half = own.astype(BF16)
    grad_lifted += dot_cols(own_half, w(1, 0))
    lifted_cot[...] = grad_lifted * math.sqrt(total_fine)
    layer1.put(0, dot_rows(lifted, own_half))
    step_on(layer1)

    dz0, dq0 = node_backward(0, grad_lifted, 0.25)
    table[...] = dot_cols(dq0, w(0, 4)).astype(BF16)
    taken = back = None
    for block in range(*UP):
        if block == UP[1] - 1:
            step_on(layer2a, layer2b, layer1)
        dp, db2, db1 = edge_backward(block, dot_rows(onehot[block], table[...]), 0)
        add_bias(0, db1)
        add_bias(1, db2)
        part = dot_plain(onehot[block], dp.astype(BF16))
        taken = dp if taken is None else taken + dp
        back = part if back is None else back + part
    edge0[0].put(0, dot_rows(fine[...], taken.astype(BF16)))
    edge0[1].put(0, dot_rows(coarse[...], back.astype(BF16)))
    edge0[2].put(0, dot_rows(act[0:2].reshape(2 * B, B), dys[0:2].reshape(2 * B, B)))
    step_on(*edge0)
    bias_batch = [post(bias_acc, bias_core, place.partner())]
    node0.put(0, dot_rows(coarse[...], dq0))
    node0.put(1, dot_rows(node_in[0], dq0))
    node0.put(2, dot_rows(nact[0], dz0))
    step_on(node0)

    def bias_step(step):
        bias_batch.pop().wait()
        batch = None
        if step == 0:
            total = bias_acc[...] + bias_core[...]
        else:
            total = bias_slots[step - 1, 0] + bias_slots[step - 1, 1]
            total = total + bias_slots[step - 1, 2] + bias_slots[step - 1, 3]
        if step == 3:
            gbias[...] = total
            return
        axis = "yxz"[step]
        at = place.at(axis)
        bias_slots[step, at] = total
        for d in (1, 2, 3):
            spot = bias_slots.at[step, at]
            batch = post(spot, spot, place.peer(axis, d), batch)
        bias_batch.append(batch)

    for step in range(6):
        step_on(*edge0, node0, layer1, layer2a, layer2b)
        if step < 4:
            bias_step(step)
        if step == 2:
            leaving[0].wait()
            next_sends()
        if step == 3:
            leaving[1].wait()
    assert all(group.step == 8 for group in groups)
    leaving[2].wait()
    assert len(batches) == BATCHES and len(leaving) == SENDS
    assert max(batch.size for batch in batches + leaving) <= RULER * UNIT


def finish(fine_in, lifted_in, grads, gbias, fine_out, lifted_out, matrices_out, biases_out, wide, sems):
    copies = [
        pltpu.make_async_copy(fine_in, fine_out, sems.at[3]),
        pltpu.make_async_copy(lifted_in, lifted_out, sems.at[4]),
    ]
    for copy in copies:
        copy.start()
    for i in range(18):
        layer = i // 6
        wide[i, :, :H] = grads[0, i].astype(F32)
        wide[i, :, H:] = grads[1, i].astype(F32)
        pltpu.make_async_copy(wide.at[i], matrices_out.at[layer, i % 6], sems.at[layer]).start()
    for layer in range(3):
        biases_out[layer] = gbias[4 * layer:4 * layer + 4, :]
        copies.append(pltpu.make_async_copy(wide.at[6 * layer:6 * layer + 6], matrices_out.at[layer], sems.at[layer]))
    for copy in copies:
        copy.wait()


def group_scratch(kind, count):
    whole = 64 if kind == "same" else B
    spare = 16 if kind == "same" else B
    small = 64 if kind == "quick" else 16
    slots = 4 if kind == "quick" else 3
    return [
        pltpu.VMEM((2, count, B, H), BF16),
        pltpu.VMEM((count, whole, H), BF16),
        pltpu.VMEM((count, spare, H), BF16),
        pltpu.VMEM((3, count, spare // 4, H), BF16),
        pltpu.VMEM((count, 64, H), BF16),
        pltpu.VMEM((slots, count, small, H), BF16),
        pltpu.VMEM((count, small, H), BF16),
        pltpu.VMEM((4, count, small, H), BF16),
        pltpu.VMEM((count, small, H), BF16),
    ]


def local(fine_state, coarse_state, up_target, down_source, halo_lists, same_source, matrices, biases, fine_cotangent):
    total_fine = fine_state.shape[0] * lax.axis_size("gx") * lax.axis_size("gy")
    scratch = [
        pltpu.SemaphoreType.DMA((SENDS,)),
        pltpu.SemaphoreType.DMA((BATCHES,)),
        pltpu.VMEM((6, B, B), BF16),
        pltpu.VMEM((6, 2 * B, B), BF16),
        pltpu.VMEM((11, B, B), BF16),
        pltpu.VMEM((11, B, B), BF16),
        pltpu.VMEM((11, B, B), BF16),
        pltpu.VMEM((11, B, 1), F32),
        pltpu.VMEM((11, B, B), BF16),
        pltpu.VMEM((4, B, B), BF16),
        pltpu.VMEM((3, B, B), BF16),
        pltpu.VMEM((3, B, B), BF16),
        pltpu.VMEM((3, B, 1), F32),
        pltpu.VMEM((B, B), BF16),
        pltpu.VMEM((2 * B, B), BF16),
        pltpu.VMEM((2 * B, B), BF16),
        pltpu.VMEM((5, B, B), F32),
        pltpu.VMEM((4, 2, H, B), BF16),
        pltpu.VMEM((4, 2, H, B), BF16),
        pltpu.VMEM((4, H, B), BF16),
        pltpu.VMEM((2, H, B), BF16),
        pltpu.VMEM((3, B, B), BF16),
        pltpu.VMEM((16, B), F32),
        pltpu.VMEM((16, B), F32),
        pltpu.VMEM((3, 4, 16, B), F32),
        pltpu.VMEM((16, H), jnp.int32),
        pltpu.VMEM((16, B), jnp.int32),
        pltpu.SemaphoreType.DMA((12,)),
        pltpu.VMEM((2, H, B), BF16),
        pltpu.VMEM((6, B, B), F32),
        pltpu.VMEM((RULER, 16, H), BF16),
        pltpu.VMEM((B, B), BF16),
        pltpu.VMEM((B, B), BF16),
        pltpu.VMEM((B, B), BF16),
        pltpu.VMEM((4, H), jnp.int32),
        pltpu.VMEM((6, H), jnp.int32),
        pltpu.VMEM((2, H), jnp.int32),
        pltpu.VMEM((12, H), jnp.int32),
        pltpu.VMEM((3, 6, B, B), BF16),
        pltpu.VMEM((3, 4, B), F32),
    ]
    for kind, _, first, end in GROUPS:
        scratch += group_scratch(kind, end - first)
    vmem = pl.BlockSpec(memory_space=pltpu.VMEM)

    def body(*refs):
        kernel(total_fine, *refs)

    fine_out, lifted, grads, gbias = pl.pallas_call(
        body,
        out_shape=(
            jax.ShapeDtypeStruct((B, B), BF16),
            jax.ShapeDtypeStruct((B, B), F32),
            jax.ShapeDtypeStruct((2, 18, B, H), BF16),
            jax.ShapeDtypeStruct((16, B), F32),
        ),
        in_specs=[pl.BlockSpec(memory_space=pltpu.HBM)] * 9,
        out_specs=(vmem,) * 4,
        scratch_shapes=scratch,
        compiler_params=pltpu.CompilerParams(
            collective_id=0, has_side_effects=True, vmem_limit_bytes=32 << 20
        ),
        name="sweep",
    )(*[
        pltpu.with_memory_space_constraint(value, pltpu.HBM)
        for value in (
            fine_state, coarse_state, fine_cotangent, up_target.reshape(4, H), down_source.reshape(6, H), halo_lists,
            same_source.reshape(12, H), matrices, biases,
        )
    ])
    hbm = pl.BlockSpec(memory_space=pl.ANY)
    return pl.pallas_call(
        finish,
        out_shape=(
            jax.ShapeDtypeStruct((B, B), BF16),
            jax.ShapeDtypeStruct((B, B), F32),
            jax.ShapeDtypeStruct((3, 6, B, B), F32),
            jax.ShapeDtypeStruct((3, 4, B), F32),
        ),
        in_specs=[vmem] * 4,
        out_specs=(hbm, hbm, hbm, vmem),
        scratch_shapes=[pltpu.VMEM((18, B, B), F32), pltpu.SemaphoreType.DMA((5,))],
        compiler_params=pltpu.CompilerParams(vmem_limit_bytes=16 << 20),
        name="finish",
    )(fine_out, lifted, grads, gbias)


def solution(mesh):
    in_specs = (
        P(("gx", "gy"), None),
        P("gy", None),
        P(("gx", "gy")),
        P(("gx", "gy")),
        P("gy", None),
        P("gy"),
        P(),
        P(),
        P(("gx", "gy"), None),
    )
    out_specs = (P(("gx", "gy"), None), P("gy", None), P(), P())
    return jax.shard_map(local, mesh=mesh, in_specs=in_specs, out_specs=out_specs, check_vma=False)
```
